512 devices in a mesh: pipe: 8 (over x, core), dp: 64 (over y, z).
Axes of the slice: x: 4, y: 4, z: 16, core: 2. Of those that a mesh axis runs over, the one named last changes fastest.
Arguments:
- saved_inputs: bfloat16 [8, 8192, 8192], P('pipe', 'dp'), may hold values from -1000 to 1000
- cotangent: bfloat16 [8192, 8192], P('dp', 'pipe'), may hold values from -500 to 500
- weights_bf16: bfloat16 [8, 2, 64, 8192], P('pipe', None, None, 'dp'), may hold values from -6 to 6
- master: float32 [8, 2, 64, 8192], P('pipe', None, None, 'dp'), may hold values from -6 to 6
- moment1: float32 [8, 2, 64, 8192], P('pipe', None, None, 'dp'), may hold values from -6 to 6
- moment2: float32 [8, 2, 64, 8192], P('pipe', None, None, 'dp'), may hold values from 0.5 to 8
- valid_rows: int32 [64], P('dp'), may hold values from 1 to 128, 6144 in all
Outputs:
- new_master: float32 [8, 2, 64, 8192], P('pipe', None, None, 'dp')
- new_moment1: float32 [8, 2, 64, 8192], P('pipe', None, None, 'dp')
- new_moment2: float32 [8, 2, 64, 8192], P('pipe', None, None, 'dp')
- new_weights: bfloat16 [8, 2, 64, 8192], P('pipe', None, None, 'dp')
The draws below stay inside these ranges and needn't reach their ends.
Inputs may be any that keep to these rules, and one draw needn't show every extreme that they name: `valid_rows`: the counts sum to 6144.
All inputs are finite; a program needn't handle non-finite values. No bound on the sum of `valid_rows` on one device may be relied on, other than what follows from the above.
Results may differ from the reference program's by a relative error of at most 0.02.
Values may be sent and summed in bfloat16 or wider, within the bound.
No kernel may reach another device: no remote copies, remote signals or barrier semaphores. Data moves between devices by JAX's collectives and lax.ppermute only.
A program may use at most 64 MiB of HBM per device.

```python
import math
import jax
import jax.numpy as jnp
import numpy as np
from jax import lax

D = 8192
R = 64
ROWS = 128
SECTIONS = 8
TOKENS = 8192
N_PIPE = 8
N_DP = 64


def draw_saved_inputs(key, part):
    keys = jax.random.split(key, 3)
    shape = (SECTIONS, TOKENS, D)
    rise_end = 3.0
    base = jnp.clip(jax.random.normal(keys[0], shape, jnp.float32), -4.0, 4.0)
    column_pos = jnp.arange(D, dtype=jnp.float32) / D
    columns = jnp.exp(math.log(rise_end) * column_pos)[None, None, :] * jnp.exp(jax.random.uniform(keys[1], (SECTIONS, 1, D), jnp.float32, 0.0, math.log(3.3)))
    row_scale = jnp.exp(jax.random.uniform(keys[2], (SECTIONS, TOKENS, 1), jnp.float32, 0.0, math.log(10.0)))
    section_pos = jnp.arange(SECTIONS, dtype=jnp.float32) / max(SECTIONS - 1, 1)
    section_scale = jnp.exp(math.log(3.0) * section_pos)[:, None, None]
    values = base * columns * row_scale * section_scale * 0.25
    return values.astype(jnp.bfloat16)


def draw_cotangent(key, part):
    keys = jax.random.split(key, 3)
    shape = (TOKENS, D)
    rise_end = 3.0
    base = jnp.clip(jax.random.normal(keys[0], shape, jnp.float32), -4.0, 4.0)
    column_pos = jnp.arange(D, dtype=jnp.float32) / D
    columns = jnp.exp(math.log(rise_end) * column_pos)[None, :] * jnp.exp(jax.random.uniform(keys[1], (1, D), jnp.float32, 0.0, math.log(3.3)))
    row_scale = jnp.exp(jax.random.uniform(keys[2], (TOKENS, 1), jnp.float32, 0.0, math.log(10.0)))
    values = base * columns * row_scale * 0.25
    return values.astype(jnp.bfloat16)


def block_scale(rng, shape, pieces, low, largest):
    loudness = 1.0
    for position, parts in pieces:
        steps = jax.random.uniform(jax.random.fold_in(jax.random.fold_in(rng, 6), position), (parts,), jnp.float32, low / len(pieces), largest / len(pieces))
        loudness = loudness * jnp.repeat(jnp.exp(steps), shape[position] // parts).reshape((-1,) + (1,) * (len(shape) - 1 - position))
    return loudness


def length_profile(number_of, total, bound, lean):
    weights = [(1 << 20) // math.isqrt(rank ** lean) + 1 for rank in range(2, number_of + 1)]
    surplus, holding = total - bound - (number_of - 1), [1] * (number_of - 1)
    while surplus > 0:
        free = [i for i in range(number_of - 1) if holding[i] < bound]
        pool, budget = sum([weights[i] for i in free]), surplus
        for i in free:
            extra = min(bound - holding[i], max(1, budget * weights[i] // pool), surplus)
            holding[i] = holding[i] + extra
            surplus = surplus - extra
    return np.array([bound] + holding)


def ragged(rng, count, total, limit, skew):
    if count == 2:
        one = jax.random.randint(rng, (), max(1, total - limit), min(limit, total - 1) + 1)
        return jnp.stack([one, total - one])
    lengths = jnp.asarray(length_profile(count, total, limit, skew), jnp.int32)
    twos = (count - 1) // 2
    donor, sink = lengths[1:1 + 2 * twos:2], lengths[2:2 + 2 * twos:2]
    margin = jnp.minimum(donor - 1, limit - sink)
    moved = jax.random.randint(jax.random.fold_in(rng, 1), (twos,), 0, 1 << 20) % (margin + 1)
    lengths = lengths.at[1:1 + 2 * twos:2].set(donor - moved).at[2:2 + 2 * twos:2].set(sink + moved)
    return lengths[jax.random.permutation(jax.random.fold_in(rng, 2), count)]


def scatter_about(rng, shape, scale, limit, cuts=(), kind=jnp.bfloat16):
    entries = jax.random.normal(rng, shape, jnp.float32) * scale
    if len(cuts) > 0:
        entries = block_scale(rng, shape, cuts, -0.22, 0.18) * entries
    return jnp.clip(entries, min=-limit, max=limit).astype(kind)


def setup_inputs(seed: int = 0) -> dict:
    streams_of = jax.random.split(jax.random.key(seed), 8)
    return {
        "saved_inputs": draw_saved_inputs(jax.random.fold_in(streams_of[7], 71), 0),
        "cotangent": draw_cotangent(jax.random.fold_in(streams_of[7], 71), 0),
        "weights_bf16": scatter_about(streams_of[2], (SECTIONS, 2, R, D), 1.0, 6.0, ((0, 8), (3, 64))),
        "master": scatter_about(streams_of[3], (SECTIONS, 2, R, D), 1.0, 6.0, ((0, 8), (3, 64)), jnp.float32),
        "moment1": scatter_about(streams_of[4], (SECTIONS, 2, R, D), 1.0, 6.0, ((0, 8), (3, 64)), jnp.float32),
        "moment2": jnp.clip(jnp.exp(math.log(8.0) - 2.7725887 * jax.random.uniform(streams_of[5], (SECTIONS, 2, R, D), jnp.float32) ** block_scale(streams_of[5], (SECTIONS, 2, R, D), ((0, 8), (3, 64)), -0.2, 0.2)), 0.5, 8.0),
        "valid_rows": ragged(streams_of[6], N_DP, 3 * TOKENS // 4, ROWS, 0).astype(jnp.int32),
    }


BETA_ONE = 0.9
BETA_TWO = 0.95
LEARN_RATE = 0.05
DECAY_RATE = 0.1
ADAM_EPS = 1e-08
CLIP_RMS = 2.0
NORM_EPS = 1e-12

def section_backward(inputs_block, incoming, weights):
    down_proj = weights[0]
    up_proj = weights[1]
    model_width = inputs_block.shape[1]
    adapter_rank = weights.shape[1]
    pre_act = lax.dot_general(inputs_block, down_proj, (((1,), (1,)), ((), ())), preferred_element_type=jnp.float32) * (1.0 / math.sqrt(model_width))
    activated = jax.nn.silu(pre_act).astype(jnp.bfloat16)
    logistic = jax.nn.sigmoid(pre_act)
    derivative = logistic * (1.0 + pre_act * (1.0 - logistic))
    along_rank = lax.dot_general(incoming, up_proj, (((1,), (1,)), ((), ())), preferred_element_type=jnp.float32) * (1.0 / math.sqrt(adapter_rank))
    back_grad = (along_rank * derivative).astype(jnp.bfloat16)
    grad_up = lax.dot_general(activated, incoming, (((0,), (0,)), ((), ())), preferred_element_type=jnp.float32) * (1.0 / math.sqrt(adapter_rank))
    grad_down = lax.dot_general(back_grad, inputs_block, (((0,), (0,)), ((), ())), preferred_element_type=jnp.float32) * (1.0 / math.sqrt(model_width))
    outgoing = (incoming.astype(jnp.float32) + jnp.dot(back_grad, down_proj, preferred_element_type=jnp.float32) * (1.0 / math.sqrt(model_width))).astype(jnp.bfloat16)
    return (outgoing, jnp.stack([grad_down, grad_up]))

def reference(saved_inputs, cotangent, weights_bf16, master, moment1, moment2, valid_rows):
    row_index = jnp.arange(TOKENS, dtype=jnp.int32)
    owner = (row_index // ROWS).astype(jnp.int32)
    live_rows = row_index % ROWS < valid_rows[owner]
    incoming = jnp.where(live_rows[:, None], cotangent, jnp.zeros_like(cotangent))
    gradient_list = []
    for section_index in range(N_PIPE - 1, -1, -1):
        incoming, grad_section = section_backward(saved_inputs[section_index], incoming, weights_bf16[section_index])
        gradient_list.append(grad_section)
    gradients = jnp.stack(gradient_list[::-1])
    square_sum = jnp.sum(gradients * gradients)
    norm_limit = CLIP_RMS * math.sqrt(2.0 * N_PIPE * R * D)
    clip_factor = jnp.minimum(1.0, norm_limit / jnp.sqrt(square_sum + NORM_EPS))
    scaled = gradients * clip_factor
    new_moment1 = BETA_ONE * moment1 + (1.0 - BETA_ONE) * scaled
    new_moment2 = BETA_TWO * moment2 + (1.0 - BETA_TWO) * scaled * scaled
    new_master = master - LEARN_RATE * (new_moment1 / (jnp.sqrt(new_moment2) + ADAM_EPS) + DECAY_RATE * master)
    return (new_master, new_moment1, new_moment2, new_master.astype(jnp.bfloat16))
```

```python
import functools
import math

import jax
import jax.numpy as jnp
import numpy as np
from jax import lax
from jax.experimental import pallas as pl
from jax.experimental.pallas import tpu as pltpu
from jax.sharding import PartitionSpec as P

BETA_ONE = 0.9
BETA_TWO = 0.95
LEARN_RATE = 0.05
DECAY_RATE = 0.1
ADAM_EPS = 1e-08
CLIP_RMS = 2.0
NORM_EPS = 1e-12

LANES = 128
Y_SIZE = 4
VMEM_LIMIT = 48 * 1024 * 1024
INTERPRET = False
BF16 = jnp.bfloat16
F32 = jnp.float32


def contract_last(a, b):
    return lax.dot_general(a, b, (((1,), (1,)), ((), ())), preferred_element_type=F32)


def contract_first(a, b):
    return lax.dot_general(a, b, (((0,), (0,)), ((), ())), preferred_element_type=F32)


def vmem_specs(count):
    return [pl.BlockSpec(memory_space=pltpu.VMEM)] * count


def call(kernel, out_shape, operands, scratch=(), flops=0):
    size = sum(math.prod(a.shape) * a.dtype.itemsize for a in (*operands, out_shape))
    return pl.pallas_call(
        kernel,
        out_shape=out_shape,
        in_specs=[pl.BlockSpec(memory_space=pltpu.SMEM)] + vmem_specs(len(operands) - 1),
        out_specs=pl.BlockSpec(memory_space=pltpu.VMEM),
        scratch_shapes=list(scratch),
        compiler_params=pltpu.CompilerParams(vmem_limit_bytes=VMEM_LIMIT),
        cost_estimate=pl.CostEstimate(flops=flops, bytes_accessed=size, transcendentals=0),
        interpret=INTERPRET,
    )(*operands)


class Layout:
    def __init__(self, pipe, dp, rows, width, rank):
        self.pipe, self.dp, self.rows, self.width, self.rank = pipe, dp, rows, width, rank
        self.y = Y_SIZE if dp >= 64 else 2
        self.z = dp // self.y
        self.group = pipe * self.y
        self.span = width // self.y
        self.share = width // self.group
        self.per = self.z // pipe
        self.half = pipe // self.y
        self.piece = rows // pipe
        self.tiles = pipe * rank // LANES
        self.ranks = pipe * rank
        self.gram = max(self.tiles - 1, 2) * LANES
        y, z = self.y, self.z
        self.along_z = [[a * z + b for b in range(z)] for a in range(y)]
        self.along_y = [[a * z + b for a in range(y)] for b in range(z)]
        self.plane = [
            [p * dp + a * z + b for p in range(pipe) for a in range(y)] for b in range(z)
        ]

    def device(self, p, y, z):
        return p * self.dp + y * self.z + z

    def everywhere(self):
        return [(p, a, b) for p in range(self.pipe) for a in range(self.y) for b in range(self.z)]

    def turn_y(self, by):
        return [
            (a * self.z + b, (a + by) % self.y * self.z + b)
            for a in range(self.y)
            for b in range(self.z)
        ]

    def cotangent_turn(self, i):
        return [
            (
                self.device(p, a, b),
                self.device(self.y * (p % self.half) + (i + a) % self.y, p // self.half, b),
            )
            for p, a, b in self.everywhere()
        ]

    def gradient_home(self):
        return [
            (
                self.device(p, a, b),
                self.device(b // self.per, a, p * self.per + b % self.per),
            )
            for p, a, b in self.everywhere()
        ]

    def table(self):
        rows = []
        for p, a, b in self.everywhere():
            row = [(a - k) % self.y for k in range(self.y)]
            row += [(p % self.y - i) % self.y for i in range(self.y)]
            row += [p // 2, p % 2, 1 - p % 2]
            rows.append(row + [0] * (16 - len(row)))
        return np.asarray(rows, np.int32)


def pre_kernel(lay, table, w_ref, *refs):
    x_refs, out_ref = refs[: lay.y], refs[lay.y]
    lower, upper = table[0, 2 * lay.y + 1], table[0, 2 * lay.y + 2]
    maps = jnp.concatenate(
        [jnp.concatenate([w_ref[b, lower], w_ref[b, upper]], axis=0) for b in range(lay.z)],
        axis=1,
    )
    for k in range(lay.y):
        out_ref[table[0, k]] = contract_last(x_refs[k][...], maps).astype(BF16)


def section_maps(lay, w_ref, which):
    return jnp.concatenate(
        [
            jnp.concatenate([w_ref[s, j, which] for j in range(lay.per)], axis=1)
            for s in range(lay.pipe)
        ],
        axis=0,
    )


def pack_kernel(lay, table, w_ref, pre_ref, *refs):
    c_refs, out_ref = refs[: lay.y], refs[lay.y]
    down, up = section_maps(lay, w_ref, 0), section_maps(lay, w_ref, 1)
    gram_at, pre_at = lay.ranks, lay.ranks + lay.gram
    for i in range(lay.y):
        block = table[0, lay.y + i]
        part = contract_last(c_refs[i][...], up).astype(BF16)
        for p in range(lay.pipe):
            rows = slice(p * lay.piece, (p + 1) * lay.piece)
            out_ref[p * lay.y + block, :, 0:gram_at] = part[rows]
    for a in range(lay.y):
        for p in range(lay.pipe):
            rows = slice(p * lay.piece, (p + 1) * lay.piece)
            out_ref[p * lay.y + a, :, pre_at:] = pre_ref[a, rows, :]
    last = lay.tiles - 1
    each = lay.ranks // lay.group
    for t in range(lay.tiles):
        rows = down[t * LANES : (t + 1) * LANES]
        wide = min(t + 1, last if last >= 2 else t + 1) if t < last else last
        cols = [contract_last(rows, up[: wide * LANES]).astype(BF16)]
        if t == 0:
            corner = slice(last * LANES, (last + 1) * LANES)
            cols.append(contract_last(down[corner], up[corner]).astype(BF16))
            wide += 1
        if wide * LANES < lay.gram:
            cols.append(jnp.zeros((LANES, lay.gram - wide * LANES), BF16))
        full = jnp.concatenate(cols, axis=1) if len(cols) > 1 else cols[0]
        for q in range(LANES // each):
            out_ref[t * (LANES // each) + q, :, gram_at:pre_at] = full[q * each : (q + 1) * each]


def sum_kernel(lay, table, r_ref, out_ref):
    gram_end = lay.ranks + lay.gram
    total = r_ref[0, :, 0:gram_end].astype(F32)
    for q in range(1, lay.group):
        total += r_ref[q, :, 0:gram_end].astype(F32)
    lower = lax.broadcasted_iota(jnp.int32, (lay.piece, LANES), 1) < lay.rank
    pres = []
    for s in range(lay.pipe):
        one = r_ref[s * lay.y, :, gram_end:].astype(F32)
        for a in range(1, lay.y):
            one += r_ref[s * lay.y + a, :, gram_end:].astype(F32)
        pres.append(one)
    cols = [total] + [jnp.where(lower, pres[2 * t], pres[2 * t + 1]) for t in range(lay.tiles)]
    message = jnp.concatenate(cols, axis=1).astype(BF16)
    for q in range(lay.group):
        out_ref[q] = message


def chain_kernel(lay, table, q_ref, w_ref, *refs):
    c_refs, x_refs = refs[: lay.y], refs[lay.y : 2 * lay.y]
    out_ref, along, slope, acts, backs, gram, cots, held = refs[2 * lay.y :]
    width_scale, rank_scale = 1.0 / math.sqrt(lay.width), 1.0 / math.sqrt(lay.rank)
    gram_at, pre_at = lay.ranks, lay.ranks + lay.gram
    each = lay.ranks // lay.group
    for q in range(lay.group):
        p, a = q // lay.y, q % lay.y
        rows = slice(a * lay.rows + p * lay.piece, a * lay.rows + (p + 1) * lay.piece)
        along[rows, :] = q_ref[q, :, 0:gram_at].astype(F32)
        gram[q * each : (q + 1) * each, :] = q_ref[q, :, gram_at:pre_at]
        pre = q_ref[q, :, pre_at:].astype(F32) * width_scale
        gate = 1.0 / (1.0 + jnp.exp(-pre))
        acts[rows, :] = (pre * gate).astype(BF16)
        slope[rows, :] = gate * (1.0 + pre * (1.0 - gate)) * rank_scale
    for i in range(lay.y):
        cots[table[0, lay.y + i]] = c_refs[i][...]
    tokens = lay.y * lay.rows
    last = lay.tiles - 1
    lower = lax.broadcasted_iota(jnp.int32, (tokens, LANES), 1) < lay.rank
    for s in range(lay.pipe - 1, -1, -1):
        t, odd = s // 2, s % 2 == 1
        tile = slice(t * LANES, (t + 1) * LANES)
        back = along[:, tile] * slope[:, tile]
        back = jnp.where(lower != odd, back, 0.0).astype(BF16)
        if odd:
            backs[t] = back
        else:
            backs[t] = backs[t] + back
        if s == 0:
            continue
        plain = t if t == last or not odd else t + 1
        if plain > 0:
            cols = slice(0, plain * LANES)
            along[:, cols] += width_scale * jnp.dot(
                back, gram[tile, cols], preferred_element_type=F32
            )
        if t == last and odd:
            along[:, tile] += width_scale * jnp.dot(
                back, gram[0:LANES, LANES : 2 * LANES], preferred_element_type=F32
            )
    acted = acts[...]
    back_all = jnp.concatenate([backs[t] for t in range(lay.tiles)], axis=1)
    cross = contract_first(acted, back_all)
    before = lax.broadcasted_iota(jnp.int32, cross.shape, 0) // lay.rank
    after = lax.broadcasted_iota(jnp.int32, cross.shape, 1) // lay.rank
    cross = jnp.where(before < after, cross * width_scale, 0.0).astype(BF16)
    cot_all = cots[...].reshape(tokens, lay.share)
    grad_up = contract_first(acted, cot_all) + jnp.dot(
        cross, section_maps(lay, w_ref, 0), preferred_element_type=F32
    )
    grad_up = (grad_up * rank_scale).astype(BF16)
    for s in range(lay.pipe):
        for j in range(lay.per):
            out_ref[s * lay.per + j, lay.rank :, :] = grad_up[
                s * lay.rank : (s + 1) * lay.rank, j * LANES : (j + 1) * LANES
            ]
    mine, odd = table[0, 2 * lay.y], table[0, 2 * lay.y + 1]
    total = None
    for k in range(lay.y):
        start = pl.multiple_of(table[0, k] * lay.rows, lay.rows)
        part = contract_first(backs[mine, pl.ds(start, lay.rows), :], x_refs[k][...])
        total = part if total is None else total + part
    held[...] = (total * width_scale).reshape(2, lay.rank, lay.span)
    grad_down = held[odd].astype(BF16)
    for b in range(lay.z):
        out_ref[b, 0 : lay.rank, :] = grad_down[:, b * LANES : (b + 1) * LANES]


def body(saved_inputs, cotangent, weights_bf16, master, moment1, moment2, valid_rows):
    pipe, dp = lax.axis_size("pipe"), lax.axis_size("dp")
    inputs, weights = saved_inputs[0], weights_bf16[0]
    lay = Layout(pipe, dp, inputs.shape[0], inputs.shape[1], weights.shape[1])
    both = ("pipe", "dp")
    p_index, d_index = lax.axis_index("pipe"), lax.axis_index("dp")
    y_index = d_index // lay.z
    table = lax.dynamic_slice(jnp.asarray(lay.table()), (p_index * dp + d_index, 0), (1, 16))

    x_pieces = []
    for k in range(lay.y):
        start = (y_index + k) % lay.y * lay.span
        piece = lax.dynamic_slice(inputs, (0, start), (lay.rows, lay.span))
        x_pieces.append(lax.ppermute(piece, "dp", lay.turn_y(k)) if k else piece)
    live_rows = jnp.arange(lay.rows, dtype=jnp.int32) < valid_rows[0]
    loss_grad = jnp.where(live_rows[:, None], cotangent, jnp.zeros_like(cotangent))
    c_pieces = []
    for i in range(lay.y):
        start = (y_index + i) % lay.y * lay.share
        piece = lax.dynamic_slice(loss_grad, (0, start), (lay.rows, lay.share))
        c_pieces.append(lax.ppermute(piece, both, lay.cotangent_turn(i)))

    maps = lax.all_gather(weights, "dp", axis_index_groups=lay.along_z)
    shared = lax.all_to_all(
        maps.reshape(pipe, lay.per, 2, lay.rank, LANES), "pipe", 0, 0
    )
    pre_part = call(
        functools.partial(pre_kernel, lay),
        jax.ShapeDtypeStruct((lay.y, lay.rows, LANES), BF16),
        (table, maps, *x_pieces),
        flops=2 * lay.y * lay.rows * lay.span * LANES,
    )
    message = lay.ranks + lay.gram + LANES
    parts = call(
        functools.partial(pack_kernel, lay),
        jax.ShapeDtypeStruct((lay.group, lay.piece, message), BF16),
        (table, shared, pre_part, *c_pieces),
        flops=4 * lay.y * lay.rows * lay.share * lay.ranks,
    )
    parts = lax.all_to_all(parts, both, 0, 0, axis_index_groups=lay.plane)
    reply = 2 * lay.ranks + lay.gram
    sums = call(
        functools.partial(sum_kernel, lay),
        jax.ShapeDtypeStruct((lay.group, lay.piece, reply), BF16),
        (table, parts),
    )
    sums = lax.all_to_all(sums, both, 0, 0, axis_index_groups=lay.plane)
    tokens = lay.y * lay.rows
    grads = call(
        functools.partial(chain_kernel, lay),
        jax.ShapeDtypeStruct((lay.z, 2 * lay.rank, LANES), BF16),
        (table, sums, shared, *c_pieces, *x_pieces),
        scratch=(
            pltpu.VMEM((tokens, lay.ranks), F32),
            pltpu.VMEM((tokens, lay.ranks), F32),
            pltpu.VMEM((tokens, lay.ranks), BF16),
            pltpu.VMEM((lay.tiles, tokens, LANES), BF16),
            pltpu.VMEM((lay.ranks, lay.gram), BF16),
            pltpu.VMEM((lay.y, lay.rows, lay.share), BF16),
            pltpu.VMEM((2, lay.rank, lay.span), F32),
        ),
        flops=8 * tokens * lay.ranks * lay.share,
    )
    grads = lax.all_to_all(grads, "dp", 0, 0, axis_index_groups=lay.along_z)
    grads = jnp.sum(grads.astype(F32), axis=0)
    squares = jnp.sum((grads * grads).reshape(-1, 8, LANES), axis=0)
    grad_up = lax.ppermute(grads[lay.rank :], both, lay.gradient_home())
    squares = jnp.broadcast_to(squares, (lay.group, 8, LANES))
    squares = lax.all_to_all(squares, both, 0, 0, axis_index_groups=lay.plane)
    squares = jnp.broadcast_to(jnp.sum(squares, axis=0), (lay.z, 8, LANES))
    squares = lax.all_to_all(squares, "dp", 0, 0, axis_index_groups=lay.along_z)
    square_sum = jnp.sum(squares)
    norm_limit = CLIP_RMS * math.sqrt(2.0 * pipe * lay.rank * lay.width)
    clip_factor = jnp.minimum(1.0, norm_limit / jnp.sqrt(square_sum + NORM_EPS))
    scaled = jnp.stack([grads[: lay.rank], grad_up]) * clip_factor
    new_moment1 = BETA_ONE * moment1[0] + (1.0 - BETA_ONE) * scaled
    new_moment2 = BETA_TWO * moment2[0] + (1.0 - BETA_TWO) * scaled * scaled
    new_master = master[0] - LEARN_RATE * (
        new_moment1 / (jnp.sqrt(new_moment2) + ADAM_EPS) + DECAY_RATE * master[0]
    )
    return (
        new_master[None],
        new_moment1[None],
        new_moment2[None],
        new_master.astype(BF16)[None],
    )


def solution(mesh):
    in_specs = (
        P("pipe", "dp", None),
        P("dp", "pipe"),
        P("pipe", None, None, "dp"),
        P("pipe", None, None, "dp"),
        P("pipe", None, None, "dp"),
        P("pipe", None, None, "dp"),
        P("dp"),
    )
    out_specs = (
        P("pipe", None, None, "dp"),
        P("pipe", None, None, "dp"),
        P("pipe", None, None, "dp"),
        P("pipe", None, None, "dp"),
    )
    return jax.shard_map(body, mesh=mesh, in_specs=in_specs, out_specs=out_specs, check_vma=False)
```

```python
import functools
import math

import jax
import jax.numpy as jnp
from jax import lax
from jax.experimental import pallas as pl
from jax.experimental.pallas import tpu as pltpu
from jax.sharding import PartitionSpec as P

BETA_ONE = 0.9
BETA_TWO = 0.95
LEARN_RATE = 0.05
DECAY_RATE = 0.1
ADAM_EPS = 1e-08
CLIP_RMS = 2.0
NORM_EPS = 1e-12

LANES = 128
Y_SIZE = 4
VMEM_LIMIT = 48 * 1024 * 1024
INTERPRET = False
BF16 = jnp.bfloat16
F32 = jnp.float32


def contract_last(a, b):
    return lax.dot_general(a, b, (((1,), (1,)), ((), ())), preferred_element_type=F32)


def contract_first(a, b):
    return lax.dot_general(a, b, (((0,), (0,)), ((), ())), preferred_element_type=F32)


def vmem_specs(count):
    return [pl.BlockSpec(memory_space=pltpu.VMEM)] * count


def call(kernel, out_shape, operands, scratch=(), flops=0):
    size = sum(math.prod(a.shape) * a.dtype.itemsize for a in (*operands, out_shape))
    return pl.pallas_call(
        kernel,
        out_shape=out_shape,
        in_specs=[pl.BlockSpec(memory_space=pltpu.SMEM)] + vmem_specs(len(operands) - 1),
        out_specs=pl.BlockSpec(memory_space=pltpu.VMEM),
        scratch_shapes=list(scratch),
        compiler_params=pltpu.CompilerParams(vmem_limit_bytes=VMEM_LIMIT),
        cost_estimate=pl.CostEstimate(flops=flops, bytes_accessed=size, transcendentals=0),
        interpret=INTERPRET,
    )(*operands)


class Layout:
    def __init__(self, pipe, dp, rows, width, rank):
        self.pipe, self.dp, self.rows, self.width, self.rank = pipe, dp, rows, width, rank
        self.y = Y_SIZE if dp >= 64 else 2
        self.z = dp // self.y
        self.group = pipe * self.y
        self.span = width // self.y
        self.share = width // self.group
        self.per = self.z // pipe
        self.half = pipe // self.y
        self.piece = rows // pipe
        self.tiles = pipe * rank // LANES
        self.ranks = pipe * rank
        self.gram = max(self.tiles - 1, 2) * LANES
        y, z = self.y, self.z
        self.along_z = [[a * z + b for b in range(z)] for a in range(y)]
        self.along_y = [[a * z + b for a in range(y)] for b in range(z)]
        self.plane = [
            [p * dp + a * z + b for p in range(pipe) for a in range(y)] for b in range(z)
        ]

    def device(self, p, y, z):
        return p * self.dp + y * self.z + z

    def everywhere(self):
        return [(p, a, b) for p in range(self.pipe) for a in range(self.y) for b in range(self.z)]

    def cotangent_turn(self):
        return [
            (
                self.device(p, a, b),
                self.device(self.y * (p % self.half) + a, p // self.half, b),
            )
            for p, a, b in self.everywhere()
        ]

    def gradient_home(self):
        return [
            (
                self.device(p, a, b),
                self.device(b // self.per, a, p * self.per + b % self.per),
            )
            for p, a, b in self.everywhere()
        ]


def sort_kernel(lay, valid, x_ref, c_ref, out_ref):
    out_ref[0, :, 0 : lay.span] = x_ref[...]
    cot = c_ref[...]
    live = lax.broadcasted_iota(jnp.int32, cot.shape, 0) < valid[0]
    out_ref[0, :, lay.span :] = jnp.where(live, cot, jnp.zeros_like(cot))


def sort_columns(lay, valid_rows, inputs, cotangent):
    both = lay.span + lay.share
    return pl.pallas_call(
        functools.partial(sort_kernel, lay),
        grid=(lay.y,),
        out_shape=jax.ShapeDtypeStruct((lay.y, lay.rows, both), BF16),
        in_specs=[
            pl.BlockSpec(memory_space=pltpu.SMEM),
            pl.BlockSpec((lay.rows, lay.span), lambda a: (0, a)),
            pl.BlockSpec((lay.rows, lay.share), lambda a: (0, a)),
        ],
        out_specs=pl.BlockSpec((1, lay.rows, both), lambda a: (a, 0, 0)),
        compiler_params=pltpu.CompilerParams(vmem_limit_bytes=VMEM_LIMIT),
        cost_estimate=pl.CostEstimate(
            flops=0, bytes_accessed=4 * lay.y * lay.rows * both, transcendentals=0
        ),
        interpret=INTERPRET,
    )(valid_rows, inputs, cotangent)


def pre_kernel(lay, index, w_ref, x_ref, out_ref):
    lower = index[0] % 2
    maps = jnp.concatenate(
        [jnp.concatenate([w_ref[b, lower], w_ref[b, 1 - lower]], axis=0) for b in range(lay.z)],
        axis=1,
    )
    for a in range(lay.y):
        out_ref[a] = contract_last(x_ref[a, :, 0 : lay.span], maps).astype(BF16)


def section_maps(lay, w_ref, which):
    return jnp.concatenate(
        [
            jnp.concatenate([w_ref[s, j, which] for j in range(lay.per)], axis=1)
            for s in range(lay.pipe)
        ],
        axis=0,
    )


def pack_kernel(lay, index, w_ref, pre_ref, c_ref, out_ref):
    down, up = section_maps(lay, w_ref, 0), section_maps(lay, w_ref, 1)
    gram_at, pre_at = lay.ranks, lay.ranks + lay.gram
    for a in range(lay.y):
        part = contract_last(c_ref[a], up).astype(BF16)
        for p in range(lay.pipe):
            rows = slice(p * lay.piece, (p + 1) * lay.piece)
            out_ref[p * lay.y + a, :, 0:gram_at] = part[rows]
            out_ref[p * lay.y + a, :, pre_at:] = pre_ref[a, rows, :]
    last = lay.tiles - 1
    each = lay.ranks // lay.group
    for t in range(lay.tiles):
        rows = down[t * LANES : (t + 1) * LANES]
        wide = min(t + 1, last if last >= 2 else t + 1) if t < last else last
        cols = [contract_last(rows, up[: wide * LANES]).astype(BF16)]
        if t == 0:
            corner = slice(last * LANES, (last + 1) * LANES)
            cols.append(contract_last(down[corner], up[corner]).astype(BF16))
            wide += 1
        if wide * LANES < lay.gram:
            cols.append(jnp.zeros((LANES, lay.gram - wide * LANES), BF16))
        full = jnp.concatenate(cols, axis=1) if len(cols) > 1 else cols[0]
        for q in range(LANES // each):
            out_ref[t * (LANES // each) + q, :, gram_at:pre_at] = full[q * each : (q + 1) * each]


def sum_kernel(lay, index, r_ref, out_ref):
    gram_end = lay.ranks + lay.gram
    total = r_ref[0, :, 0:gram_end].astype(F32)
    for q in range(1, lay.group):
        total += r_ref[q, :, 0:gram_end].astype(F32)
    lower = lax.broadcasted_iota(jnp.int32, (lay.piece, LANES), 1) < lay.rank
    pres = []
    for s in range(lay.pipe):
        one = r_ref[s * lay.y, :, gram_end:].astype(F32)
        for a in range(1, lay.y):
            one += r_ref[s * lay.y + a, :, gram_end:].astype(F32)
        pres.append(one)
    cols = [total] + [jnp.where(lower, pres[2 * t], pres[2 * t + 1]) for t in range(lay.tiles)]
    message = jnp.concatenate(cols, axis=1).astype(BF16)
    for q in range(lay.group):
        out_ref[q] = message


def chain_kernel(lay, index, q_ref, w_ref, c_ref, x_ref, out_ref, *scratch):
    along, slope, acts, backs, gram, held = scratch
    width_scale, rank_scale = 1.0 / math.sqrt(lay.width), 1.0 / math.sqrt(lay.rank)
    gram_at, pre_at = lay.ranks, lay.ranks + lay.gram
    each = lay.ranks // lay.group
    for q in range(lay.group):
        p, a = q // lay.y, q % lay.y
        rows = slice(a * lay.rows + p * lay.piece, a * lay.rows + (p + 1) * lay.piece)
        along[rows, :] = q_ref[q, :, 0:gram_at].astype(F32)
        gram[q * each : (q + 1) * each, :] = q_ref[q, :, gram_at:pre_at]
        pre = q_ref[q, :, pre_at:].astype(F32) * width_scale
        gate = 1.0 / (1.0 + jnp.exp(-pre))
        acts[rows, :] = (pre * gate).astype(BF16)
        slope[rows, :] = gate * (1.0 + pre * (1.0 - gate)) * rank_scale
    tokens = lay.y * lay.rows
    last = lay.tiles - 1
    lower = lax.broadcasted_iota(jnp.int32, (tokens, LANES), 1) < lay.rank
    for s in range(lay.pipe - 1, -1, -1):
        t, odd = s // 2, s % 2 == 1
        tile = slice(t * LANES, (t + 1) * LANES)
        back = along[:, tile] * slope[:, tile]
        back = jnp.where(lower != odd, back, 0.0).astype(BF16)
        if odd:
            backs[t] = back
        else:
            backs[t] = backs[t] + back
        if s == 0:
            continue
        plain = t if t == last or not odd else t + 1
        if plain > 0:
            cols = slice(0, plain * LANES)
            along[:, cols] += width_scale * jnp.dot(
                back, gram[tile, cols], preferred_element_type=F32
            )
        if t == last and odd:
            along[:, tile] += width_scale * jnp.dot(
                back, gram[0:LANES, LANES : 2 * LANES], preferred_element_type=F32
            )
    acted = acts[...]
    back_all = jnp.concatenate([backs[t] for t in range(lay.tiles)], axis=1)
    cross = contract_first(acted, back_all)
    before = lax.broadcasted_iota(jnp.int32, cross.shape, 0) // lay.rank
    after = lax.broadcasted_iota(jnp.int32, cross.shape, 1) // lay.rank
    cross = jnp.where(before < after, cross * width_scale, 0.0).astype(BF16)
    cot_all = c_ref[...].reshape(tokens, lay.share)
    grad_up = contract_first(acted, cot_all) + jnp.dot(
        cross, section_maps(lay, w_ref, 0), preferred_element_type=F32
    )
    grad_up = (grad_up * rank_scale).astype(BF16)
    for s in range(lay.pipe):
        for j in range(lay.per):
            out_ref[s * lay.per + j, lay.rank :, :] = grad_up[
                s * lay.rank : (s + 1) * lay.rank, j * LANES : (j + 1) * LANES
            ]
    mine, odd = index[0] // 2, index[0] % 2
    total = None
    for a in range(lay.y):
        rows = slice(a * lay.rows, (a + 1) * lay.rows)
        part = contract_first(backs[mine, rows, :], x_ref[a, :, 0 : lay.span])
        total = part if total is None else total + part
    held[...] = (total * width_scale).reshape(2, lay.rank, lay.span)
    grad_down = held[odd].astype(BF16)
    for b in range(lay.z):
        out_ref[b, 0 : lay.rank, :] = grad_down[:, b * LANES : (b + 1) * LANES]


def body(saved_inputs, cotangent, weights_bf16, master, moment1, moment2, valid_rows):
    pipe, dp = lax.axis_size("pipe"), lax.axis_size("dp")
    inputs, weights = saved_inputs[0], weights_bf16[0]
    lay = Layout(pipe, dp, inputs.shape[0], inputs.shape[1], weights.shape[1])
    both = ("pipe", "dp")
    index = lax.axis_index("pipe").astype(jnp.int32).reshape(1)

    by_column = sort_columns(lay, valid_rows, inputs, cotangent)
    by_column = lax.all_to_all(by_column, "dp", 0, 0, axis_index_groups=lay.along_y)
    cots = lax.ppermute(by_column[:, :, lay.span :], both, lay.cotangent_turn())

    maps = lax.all_gather(weights, "dp", axis_index_groups=lay.along_z)
    shared = lax.all_to_all(
        maps.reshape(pipe, lay.per, 2, lay.rank, LANES), "pipe", 0, 0
    )
    pre_part = call(
        functools.partial(pre_kernel, lay),
        jax.ShapeDtypeStruct((lay.y, lay.rows, LANES), BF16),
        (index, maps, by_column),
        flops=2 * lay.y * lay.rows * lay.span * LANES,
    )
    message = lay.ranks + lay.gram + LANES
    parts = call(
        functools.partial(pack_kernel, lay),
        jax.ShapeDtypeStruct((lay.group, lay.piece, message), BF16),
        (index, shared, pre_part, cots),
        flops=4 * lay.y * lay.rows * lay.share * lay.ranks,
    )
    parts = lax.all_to_all(parts, both, 0, 0, axis_index_groups=lay.plane)
    reply = 2 * lay.ranks + lay.gram
    sums = call(
        functools.partial(sum_kernel, lay),
        jax.ShapeDtypeStruct((lay.group, lay.piece, reply), BF16),
        (index, parts),
    )
    sums = lax.all_to_all(sums, both, 0, 0, axis_index_groups=lay.plane)
    tokens = lay.y * lay.rows
    grads = call(
        functools.partial(chain_kernel, lay),
        jax.ShapeDtypeStruct((lay.z, 2 * lay.rank, LANES), BF16),
        (index, sums, shared, cots, by_column),
        scratch=(
            pltpu.VMEM((tokens, lay.ranks), F32),
            pltpu.VMEM((tokens, lay.ranks), F32),
            pltpu.VMEM((tokens, lay.ranks), BF16),
            pltpu.VMEM((lay.tiles, tokens, LANES), BF16),
            pltpu.VMEM((lay.ranks, lay.gram), BF16),
            pltpu.VMEM((2, lay.rank, lay.span), F32),
        ),
        flops=8 * tokens * lay.ranks * lay.share,
    )
    grads = lax.all_to_all(grads, "dp", 0, 0, axis_index_groups=lay.along_z)
    grads = jnp.sum(grads.astype(F32), axis=0)
    squares = jnp.sum((grads * grads).reshape(-1, 8, LANES), axis=0)
    grad_up = lax.ppermute(grads[lay.rank :], both, lay.gradient_home())
    squares = jnp.broadcast_to(squares, (lay.group, 8, LANES))
    squares = lax.all_to_all(squares, both, 0, 0, axis_index_groups=lay.plane)
    squares = jnp.broadcast_to(jnp.sum(squares, axis=0), (lay.z, 8, LANES))
    squares = lax.all_to_all(squares, "dp", 0, 0, axis_index_groups=lay.along_z)
    square_sum = jnp.sum(squares)
    norm_limit = CLIP_RMS * math.sqrt(2.0 * pipe * lay.rank * lay.width)
    clip_factor = jnp.minimum(1.0, norm_limit / jnp.sqrt(square_sum + NORM_EPS))
    scaled = jnp.stack([grads[: lay.rank], grad_up]) * clip_factor
    new_moment1 = BETA_ONE * moment1[0] + (1.0 - BETA_ONE) * scaled
    new_moment2 = BETA_TWO * moment2[0] + (1.0 - BETA_TWO) * scaled * scaled
    new_master = master[0] - LEARN_RATE * (
        new_moment1 / (jnp.sqrt(new_moment2) + ADAM_EPS) + DECAY_RATE * master[0]
    )
    return (
        new_master[None],
        new_moment1[None],
        new_moment2[None],
        new_master.astype(BF16)[None],
    )


def solution(mesh):
    in_specs = (
        P("pipe", "dp", None),
        P("dp", "pipe"),
        P("pipe", None, None, "dp"),
        P("pipe", None, None, "dp"),
        P("pipe", None, None, "dp"),
        P("pipe", None, None, "dp"),
        P("dp"),
    )
    out_specs = (
        P("pipe", None, None, "dp"),
        P("pipe", None, None, "dp"),
        P("pipe", None, None, "dp"),
        P("pipe", None, None, "dp"),
    )
    return jax.shard_map(body, mesh=mesh, in_specs=in_specs, out_specs=out_specs, check_vma=False)
```

```python
import functools
import math

import jax
import jax.numpy as jnp
import numpy as np
from jax import lax
from jax.experimental import pallas as pl
from jax.experimental.pallas import tpu as pltpu
from jax.sharding import PartitionSpec as P

BETA_ONE = 0.9
BETA_TWO = 0.95
LEARN_RATE = 0.05
DECAY_RATE = 0.1
ADAM_EPS = 1e-08
CLIP_RMS = 2.0
NORM_EPS = 1e-12

LANES = 128
Y_SIZE = 4
VMEM_LIMIT = 48 * 1024 * 1024
INTERPRET = False
BF16 = jnp.bfloat16
F32 = jnp.float32


def contract_last(a, b):
    return lax.dot_general(a, b, (((1,), (1,)), ((), ())), preferred_element_type=F32)


def contract_first(a, b):
    return lax.dot_general(a, b, (((0,), (0,)), ((), ())), preferred_element_type=F32)


def vmem_specs(count):
    return [pl.BlockSpec(memory_space=pltpu.VMEM)] * count


def call(kernel, out_shape, operands, scratch=(), flops=0):
    size = sum(math.prod(a.shape) * a.dtype.itemsize for a in (*operands, out_shape))
    return pl.pallas_call(
        kernel,
        out_shape=out_shape,
        in_specs=[pl.BlockSpec(memory_space=pltpu.SMEM)] + vmem_specs(len(operands) - 1),
        out_specs=pl.BlockSpec(memory_space=pltpu.VMEM),
        scratch_shapes=list(scratch),
        compiler_params=pltpu.CompilerParams(vmem_limit_bytes=VMEM_LIMIT),
        cost_estimate=pl.CostEstimate(flops=flops, bytes_accessed=size, transcendentals=0),
        interpret=INTERPRET,
    )(*operands)


class Layout:
    def __init__(self, pipe, dp, rows, width, rank):
        self.pipe, self.dp, self.rows, self.width, self.rank = pipe, dp, rows, width, rank
        self.y = Y_SIZE if dp >= 64 else 2
        self.z = dp // self.y
        self.group = pipe * self.y
        self.span = width // self.y
        self.share = width // self.group
        self.per = self.z // pipe
        self.half = pipe // self.y
        self.piece = rows // pipe
        self.tiles = pipe * rank // LANES
        self.ranks = pipe * rank
        self.gram = max(self.tiles - 1, 2) * LANES
        y, z = self.y, self.z
        self.along_z = [[a * z + b for b in range(z)] for a in range(y)]
        self.along_y = [[a * z + b for a in range(y)] for b in range(z)]
        self.plane = [
            [p * dp + a * z + b for p in range(pipe) for a in range(y)] for b in range(z)
        ]

    def device(self, p, y, z):
        return p * self.dp + y * self.z + z

    def everywhere(self):
        return [(p, a, b) for p in range(self.pipe) for a in range(self.y) for b in range(self.z)]

    def turn_y(self, by):
        return [
            (a * self.z + b, (a + by) % self.y * self.z + b)
            for a in range(self.y)
            for b in range(self.z)
        ]

    def cotangent_turn(self, i):
        return [
            (
                self.device(p, a, b),
                self.device(self.y * (p % self.half) + (i + a) % self.y, p // self.half, b),
            )
            for p, a, b in self.everywhere()
        ]

    def gradient_home(self):
        return [
            (
                self.device(p, a, b),
                self.device(b // self.per, a, p * self.per + b % self.per),
            )
            for p, a, b in self.everywhere()
        ]

    def table(self):
        rows = []
        for p, a, b in self.everywhere():
            row = [(a - k) % self.y for k in range(self.y)]
            row += [(p % self.y - i) % self.y for i in range(self.y)]
            row += [p // 2, p % 2, 1 - p % 2]
            rows.append(row + [0] * (16 - len(row)))
        return np.asarray(rows, np.int32)


def pre_kernel(lay, table, w_ref, *refs):
    x_refs, out_ref = refs[: lay.y], refs[lay.y]
    lower, upper = table[0, 2 * lay.y + 1], table[0, 2 * lay.y + 2]
    maps = jnp.concatenate(
        [jnp.concatenate([w_ref[b, lower], w_ref[b, upper]], axis=0) for b in range(lay.z)],
        axis=1,
    )
    for k in range(lay.y):
        out_ref[table[0, k]] = contract_last(x_refs[k][...], maps).astype(BF16)


def section_maps(lay, w_ref, which):
    return jnp.concatenate(
        [
            jnp.concatenate([w_ref[s, j, which] for j in range(lay.per)], axis=1)
            for s in range(lay.pipe)
        ],
        axis=0,
    )


def pack_kernel(lay, table, w_ref, pre_ref, *refs):
    c_refs, out_ref = refs[: lay.y], refs[lay.y]
    down, up = section_maps(lay, w_ref, 0), section_maps(lay, w_ref, 1)
    gram_at, pre_at = lay.ranks, lay.ranks + lay.gram
    for i in range(lay.y):
        block = table[0, lay.y + i]
        part = contract_last(c_refs[i][...], up).astype(BF16)
        for p in range(lay.pipe):
            rows = slice(p * lay.piece, (p + 1) * lay.piece)
            out_ref[p * lay.y + block, :, 0:gram_at] = part[rows]
    for a in range(lay.y):
        for p in range(lay.pipe):
            rows = slice(p * lay.piece, (p + 1) * lay.piece)
            out_ref[p * lay.y + a, :, pre_at:] = pre_ref[a, rows, :]
    last = lay.tiles - 1
    each = lay.ranks // lay.group
    for t in range(lay.tiles):
        rows = down[t * LANES : (t + 1) * LANES]
        wide = min(t + 1, last if last >= 2 else t + 1) if t < last else last
        cols = [contract_last(rows, up[: wide * LANES]).astype(BF16)]
        if t == 0:
            corner = slice(last * LANES, (last + 1) * LANES)
            cols.append(contract_last(down[corner], up[corner]).astype(BF16))
            wide += 1
        if wide * LANES < lay.gram:
            cols.append(jnp.zeros((LANES, lay.gram - wide * LANES), BF16))
        full = jnp.concatenate(cols, axis=1) if len(cols) > 1 else cols[0]
        for q in range(LANES // each):
            out_ref[t * (LANES // each) + q, :, gram_at:pre_at] = full[q * each : (q + 1) * each]


def sum_kernel(lay, table, r_ref, out_ref):
    gram_end = lay.ranks + lay.gram
    total = r_ref[0, :, 0:gram_end].astype(F32)
    for q in range(1, lay.group):
        total += r_ref[q, :, 0:gram_end].astype(F32)
    lower = lax.broadcasted_iota(jnp.int32, (lay.piece, LANES), 1) < lay.rank
    pres = []
    for s in range(lay.pipe):
        one = r_ref[s * lay.y, :, gram_end:].astype(F32)
        for a in range(1, lay.y):
            one += r_ref[s * lay.y + a, :, gram_end:].astype(F32)
        pres.append(one)
    cols = [total] + [jnp.where(lower, pres[2 * t], pres[2 * t + 1]) for t in range(lay.tiles)]
    message = jnp.concatenate(cols, axis=1).astype(BF16)
    for q in range(lay.group):
        out_ref[q] = message


def chain_kernel(lay, table, q_ref, w_ref, *refs):
    c_refs, x_refs = refs[: lay.y], refs[lay.y : 2 * lay.y]
    out_ref, along, slope, acts, backs, gram, cots, held = refs[2 * lay.y :]
    width_scale, rank_scale = 1.0 / math.sqrt(lay.width), 1.0 / math.sqrt(lay.rank)
    gram_at, pre_at = lay.ranks, lay.ranks + lay.gram
    each = lay.ranks // lay.group
    for q in range(lay.group):
        p, a = q // lay.y, q % lay.y
        rows = slice(a * lay.rows + p * lay.piece, a * lay.rows + (p + 1) * lay.piece)
        along[rows, :] = q_ref[q, :, 0:gram_at].astype(F32)
        gram[q * each : (q + 1) * each, :] = q_ref[q, :, gram_at:pre_at]
        pre = q_ref[q, :, pre_at:].astype(F32) * width_scale
        gate = 1.0 / (1.0 + jnp.exp(-pre))
        acts[rows, :] = (pre * gate).astype(BF16)
        slope[rows, :] = gate * (1.0 + pre * (1.0 - gate)) * rank_scale
    for i in range(lay.y):
        cots[table[0, lay.y + i]] = c_refs[i][...]
    tokens = lay.y * lay.rows
    last = lay.tiles - 1
    lower = lax.broadcasted_iota(jnp.int32, (tokens, LANES), 1) < lay.rank
    for s in range(lay.pipe - 1, -1, -1):
        t, odd = s // 2, s % 2 == 1
        tile = slice(t * LANES, (t + 1) * LANES)
        back = along[:, tile] * slope[:, tile]
        back = jnp.where(lower != odd, back, 0.0).astype(BF16)
        if odd:
            backs[t] = back
        else:
            backs[t] = backs[t] + back
        if s == 0:
            continue
        plain = t if t == last or not odd else t + 1
        if plain > 0:
            cols = slice(0, plain * LANES)
            along[:, cols] += width_scale * jnp.dot(
                back, gram[tile, cols], preferred_element_type=F32
            )
        if t == last and odd:
            along[:, tile] += width_scale * jnp.dot(
                back, gram[0:LANES, LANES : 2 * LANES], preferred_element_type=F32
            )
    acted = acts[...]
    back_all = jnp.concatenate([backs[t] for t in range(lay.tiles)], axis=1)
    cross = contract_first(acted, back_all)
    before = lax.broadcasted_iota(jnp.int32, cross.shape, 0) // lay.rank
    after = lax.broadcasted_iota(jnp.int32, cross.shape, 1) // lay.rank
    cross = jnp.where(before < after, cross * width_scale, 0.0).astype(BF16)
    cot_all = cots[...].reshape(tokens, lay.share)
    grad_up = contract_first(acted, cot_all) + jnp.dot(
        cross, section_maps(lay, w_ref, 0), preferred_element_type=F32
    )
    grad_up = (grad_up * rank_scale).astype(BF16)
    for s in range(lay.pipe):
        for j in range(lay.per):
            out_ref[s * lay.per + j, lay.rank :, :] = grad_up[
                s * lay.rank : (s + 1) * lay.rank, j * LANES : (j + 1) * LANES
            ]
    mine, odd = table[0, 2 * lay.y], table[0, 2 * lay.y + 1]
    total = None
    for k in range(lay.y):
        start = pl.multiple_of(table[0, k] * lay.rows, lay.rows)
        part = contract_first(backs[mine, pl.ds(start, lay.rows), :], x_refs[k][...])
        total = part if total is None else total + part
    held[...] = (total * width_scale).reshape(2, lay.rank, lay.span)
    grad_down = held[odd].astype(BF16)
    for b in range(lay.z):
        out_ref[b, 0 : lay.rank, :] = grad_down[:, b * LANES : (b + 1) * LANES]


def body(saved_inputs, cotangent, weights_bf16, master, moment1, moment2, valid_rows):
    pipe, dp = lax.axis_size("pipe"), lax.axis_size("dp")
    inputs, weights = saved_inputs[0], weights_bf16[0]
    lay = Layout(pipe, dp, inputs.shape[0], inputs.shape[1], weights.shape[1])
    both = ("pipe", "dp")
    p_index, d_index = lax.axis_index("pipe"), lax.axis_index("dp")
    y_index = lax.div(d_index, lay.z)
    table = lax.dynamic_slice(jnp.asarray(lay.table()), (p_index * dp + d_index, 0), (1, 16))

    x_pieces = []
    for k in range(lay.y):
        start = lax.rem(y_index + k, lay.y) * lay.span
        piece = lax.dynamic_slice(inputs, (0, start), (lay.rows, lay.span))
        x_pieces.append(lax.ppermute(piece, "dp", lay.turn_y(k)) if k else piece)
    live_rows = jnp.arange(lay.rows, dtype=jnp.int32) < valid_rows[0]
    loss_grad = jnp.where(live_rows[:, None], cotangent, jnp.zeros_like(cotangent))
    c_pieces = []
    for i in range(lay.y):
        start = lax.rem(y_index + i, lay.y) * lay.share
        piece = lax.dynamic_slice(loss_grad, (0, start), (lay.rows, lay.share))
        c_pieces.append(lax.ppermute(piece, both, lay.cotangent_turn(i)))

    maps = jnp.broadcast_to(weights, (lay.z, *weights.shape))
    maps = lax.all_to_all(maps, "dp", 0, 0, axis_index_groups=lay.along_z)
    maps, *c_pieces = lax.optimization_barrier((maps, *c_pieces))
    shared = lax.all_to_all(
        maps.reshape(pipe, lay.per, 2, lay.rank, LANES), "pipe", 0, 0
    )
    pre_part = call(
        functools.partial(pre_kernel, lay),
        jax.ShapeDtypeStruct((lay.y, lay.rows, LANES), BF16),
        (table, maps, *x_pieces),
        flops=2 * lay.y * lay.rows * lay.span * LANES,
    )
    message = lay.ranks + lay.gram + LANES
    parts = call(
        functools.partial(pack_kernel, lay),
        jax.ShapeDtypeStruct((lay.group, lay.piece, message), BF16),
        (table, shared, pre_part, *c_pieces),
        flops=4 * lay.y * lay.rows * lay.share * lay.ranks,
    )
    parts = lax.all_to_all(parts, both, 0, 0, axis_index_groups=lay.plane)
    reply = 2 * lay.ranks + lay.gram
    sums = call(
        functools.partial(sum_kernel, lay),
        jax.ShapeDtypeStruct((lay.group, lay.piece, reply), BF16),
        (table, parts),
    )
    sums = lax.all_to_all(sums, both, 0, 0, axis_index_groups=lay.plane)
    tokens = lay.y * lay.rows
    grads = call(
        functools.partial(chain_kernel, lay),
        jax.ShapeDtypeStruct((lay.z, 2 * lay.rank, LANES), BF16),
        (table, sums, shared, *c_pieces, *x_pieces),
        scratch=(
            pltpu.VMEM((tokens, lay.ranks), F32),
            pltpu.VMEM((tokens, lay.ranks), F32),
            pltpu.VMEM((tokens, lay.ranks), BF16),
            pltpu.VMEM((lay.tiles, tokens, LANES), BF16),
            pltpu.VMEM((lay.ranks, lay.gram), BF16),
            pltpu.VMEM((lay.y, lay.rows, lay.share), BF16),
            pltpu.VMEM((2, lay.rank, lay.span), F32),
        ),
        flops=8 * tokens * lay.ranks * lay.share,
    )
    grads = lax.all_to_all(grads, "dp", 0, 0, axis_index_groups=lay.along_z)
    grads = jnp.sum(grads.astype(F32), axis=0)
    squares = jnp.sum((grads * grads).reshape(-1, 8, LANES), axis=0)
    grad_up = lax.ppermute(grads[lay.rank :], both, lay.gradient_home())
    squares = jnp.broadcast_to(squares, (lay.group, 8, LANES))
    squares = lax.all_to_all(squares, both, 0, 0, axis_index_groups=lay.plane)
    squares = jnp.broadcast_to(jnp.sum(squares, axis=0), (lay.z, 8, LANES))
    squares = lax.all_to_all(squares, "dp", 0, 0, axis_index_groups=lay.along_z)
    square_sum = jnp.sum(squares)
    norm_limit = CLIP_RMS * math.sqrt(2.0 * pipe * lay.rank * lay.width)
    clip_factor = jnp.minimum(1.0, norm_limit / jnp.sqrt(square_sum + NORM_EPS))
    scaled = jnp.stack([grads[: lay.rank], grad_up]) * clip_factor
    new_moment1 = BETA_ONE * moment1[0] + (1.0 - BETA_ONE) * scaled
    new_moment2 = BETA_TWO * moment2[0] + (1.0 - BETA_TWO) * scaled * scaled
    new_master = master[0] - LEARN_RATE * (
        new_moment1 / (jnp.sqrt(new_moment2) + ADAM_EPS) + DECAY_RATE * master[0]
    )
    return (
        new_master[None],
        new_moment1[None],
        new_moment2[None],
        new_master.astype(BF16)[None],
    )


def solution(mesh):
    in_specs = (
        P("pipe", "dp", None),
        P("dp", "pipe"),
        P("pipe", None, None, "dp"),
        P("pipe", None, None, "dp"),
        P("pipe", None, None, "dp"),
        P("pipe", None, None, "dp"),
        P("dp"),
    )
    out_specs = (
        P("pipe", None, None, "dp"),
        P("pipe", None, None, "dp"),
        P("pipe", None, None, "dp"),
        P("pipe", None, None, "dp"),
    )
    return jax.shard_map(body, mesh=mesh, in_specs=in_specs, out_specs=out_specs, check_vma=False)
```

```python
import functools
import math

import jax
import jax.numpy as jnp
from jax import lax
from jax.experimental import pallas as pl
from jax.experimental.pallas import tpu as pltpu
from jax.sharding import PartitionSpec as P

BETA_ONE = 0.9
BETA_TWO = 0.95
LEARN_RATE = 0.05
DECAY_RATE = 0.1
ADAM_EPS = 1e-08
CLIP_RMS = 2.0
NORM_EPS = 1e-12

LANES = 128
Y_SIZE = 4
VMEM_LIMIT = 48 * 1024 * 1024
SORT_LIMIT = 63 * 1024 * 1024
PRE_WEIGHT = 12
INTERPRET = False
BF16 = jnp.bfloat16
F32 = jnp.float32


def contract_last(a, b):
    return lax.dot_general(a, b, (((1,), (1,)), ((), ())), preferred_element_type=F32)


def contract_first(a, b):
    return lax.dot_general(a, b, (((0,), (0,)), ((), ())), preferred_element_type=F32)


def vmem_specs(count):
    return [pl.BlockSpec(memory_space=pltpu.VMEM)] * count


def call(kernel, out_shape, operands, scratch=(), flops=0):
    size = sum(math.prod(a.shape) * a.dtype.itemsize for a in (*operands, out_shape))
    return pl.pallas_call(
        kernel,
        out_shape=out_shape,
        in_specs=[pl.BlockSpec(memory_space=pltpu.SMEM)] + vmem_specs(len(operands) - 1),
        out_specs=pl.BlockSpec(memory_space=pltpu.VMEM),
        scratch_shapes=list(scratch),
        compiler_params=pltpu.CompilerParams(vmem_limit_bytes=VMEM_LIMIT),
        cost_estimate=pl.CostEstimate(flops=flops, bytes_accessed=size, transcendentals=0),
        interpret=INTERPRET,
    )(*operands)


class Layout:
    def __init__(self, pipe, dp, rows, width, rank):
        self.pipe, self.dp, self.rows, self.width, self.rank = pipe, dp, rows, width, rank
        self.y = Y_SIZE if dp >= 64 else 2
        self.z = dp // self.y
        self.group = pipe * self.y
        self.span = width // self.y
        self.share = width // self.group
        self.per = self.z // pipe
        self.half = pipe // self.y
        self.piece = rows // pipe
        self.tiles = pipe * rank // LANES
        self.ranks = pipe * rank
        self.gram = 2 * LANES
        self.slots = {(a, b): (a, b) for a in range(1, self.tiles) for b in range(min(a, 2))}
        spare = [(a, 1) for a in range(1, self.tiles) if (a, 1) not in self.slots]
        rest = [(a, b) for a in range(1, self.tiles) for b in range(2, a)]
        self.slots.update(zip(rest, spare))
        y, z = self.y, self.z
        self.along_z = [[a * z + b for b in range(z)] for a in range(y)]
        self.along_y = [[a * z + b for a in range(y)] for b in range(z)]
        self.plane = [
            [p * dp + a * z + b for p in range(pipe) for a in range(y)] for b in range(z)
        ]

    def device(self, p, y, z):
        return p * self.dp + y * self.z + z

    def everywhere(self):
        return [(p, a, b) for p in range(self.pipe) for a in range(self.y) for b in range(self.z)]

    def cotangent_turn(self):
        return [
            (
                self.device(p, a, b),
                self.device(self.y * (p % self.half) + a, p // self.half, b),
            )
            for p, a, b in self.everywhere()
        ]

    def gradient_home(self):
        return [
            (
                self.device(p, a, b),
                self.device(b // self.per, a, p * self.per + b % self.per),
            )
            for p, a, b in self.everywhere()
        ]


def sort_kernel(lay, valid, x_ref, c_ref, out_ref, cots, sems):
    copies = [
        pltpu.make_async_copy(
            x_ref.at[:, pl.ds(a * lay.span, lay.span)],
            out_ref.at[a, :, pl.ds(0, lay.span)],
            sems.at[a],
        )
        for a in range(lay.y)
    ]
    for copy in copies:
        copy.start()
    cot = c_ref[...]
    live = lax.broadcasted_iota(jnp.int32, cot.shape, 0) < valid[0]
    cots[...] = jnp.where(live, cot, jnp.zeros_like(cot))
    copies += [
        pltpu.make_async_copy(
            cots.at[:, pl.ds(a * lay.share, lay.share)],
            out_ref.at[a, :, pl.ds(lay.span, lay.share)],
            sems.at[lay.y + a],
        )
        for a in range(lay.y)
    ]
    for copy in copies[lay.y :]:
        copy.start()
    for copy in copies:
        copy.wait()


def sort_columns(lay, valid_rows, inputs, cotangent):
    both = lay.span + lay.share
    return pl.pallas_call(
        functools.partial(sort_kernel, lay),
        out_shape=jax.ShapeDtypeStruct((lay.y, lay.rows, both), BF16),
        in_specs=[
            pl.BlockSpec(memory_space=pltpu.SMEM),
            pl.BlockSpec(memory_space=pltpu.HBM),
            pl.BlockSpec(memory_space=pltpu.VMEM),
        ],
        out_specs=pl.BlockSpec(memory_space=pltpu.HBM),
        scratch_shapes=[
            pltpu.VMEM(cotangent.shape, BF16),
            pltpu.SemaphoreType.DMA((2 * lay.y,)),
        ],
        compiler_params=pltpu.CompilerParams(vmem_limit_bytes=SORT_LIMIT),
        cost_estimate=pl.CostEstimate(
            flops=0, bytes_accessed=4 * lay.y * lay.rows * both, transcendentals=0
        ),
        interpret=INTERPRET,
    )(valid_rows, inputs, cotangent)


def pre_kernel(lay, index, w_ref, x_ref, out_ref):
    lower = index[0] % 2
    maps = jnp.concatenate(
        [jnp.concatenate([w_ref[b, lower], w_ref[b, 1 - lower]], axis=0) for b in range(lay.z)],
        axis=1,
    )
    for a in range(lay.y):
        out_ref[a] = contract_last(x_ref[a, :, 0 : lay.span], maps).astype(BF16)


def section_maps(lay, w_ref, which):
    return jnp.concatenate(
        [
            jnp.concatenate([w_ref[s, j, which] for j in range(lay.per)], axis=1)
            for s in range(lay.pipe)
        ],
        axis=0,
    )


def gram_tile(down, up, row, col):
    rows, cols = slice(row * LANES, (row + 1) * LANES), slice(col * LANES, (col + 1) * LANES)
    return contract_last(down[rows], up[cols]).astype(BF16)


def diagonal_tile(lay, down, up):
    rank = lay.rank
    lower = lax.broadcasted_iota(jnp.int32, (rank, LANES), 1) < rank
    blocks = []
    for t in range(lay.tiles):
        odd = down[t * LANES + rank : (t + 1) * LANES]
        block = contract_last(odd, up[t * LANES : (t + 1) * LANES])
        blocks.append(block if t % 2 == 0 else pltpu.roll(block, rank, 1))
    halves = [jnp.where(lower, blocks[t], blocks[t + 1]) for t in range(0, lay.tiles, 2)]
    if len(halves) == 1:
        halves.append(halves[0])
    return jnp.concatenate(halves[::-1], axis=0).astype(BF16)


def pack_kernel(lay, index, w_ref, pre_ref, c_ref, out_ref):
    down, up = section_maps(lay, w_ref, 0), section_maps(lay, w_ref, 1)
    gram_at, pre_at = lay.ranks, lay.ranks + lay.gram
    for a in range(lay.y):
        part = contract_last(c_ref[a], up).astype(BF16)
        for p in range(lay.pipe):
            rows = slice(p * lay.piece, (p + 1) * lay.piece)
            out_ref[p * lay.y + a, :, 0:gram_at] = part[rows]
            out_ref[p * lay.y + a, :, pre_at:] = pre_ref[a, rows, :]
    grams = {spot: gram_tile(down, up, *tile) for tile, spot in lay.slots.items()}
    grams[0, 0] = diagonal_tile(lay, down, up)
    each = lay.ranks // lay.group
    count = LANES // each
    for t in range(lay.tiles):
        for side in range(2):
            cols = slice(gram_at + side * LANES, gram_at + (side + 1) * LANES)
            tile = grams.get((t, side), jnp.zeros((LANES, LANES), BF16))
            for q in range(count):
                out_ref[t * count + q, :, cols] = tile[q * each : (q + 1) * each]


def sum_kernel(lay, index, r_ref, out_ref):
    gram_end = lay.ranks + lay.gram
    total = r_ref[0, :, 0:gram_end].astype(F32)
    for q in range(1, lay.group):
        total += r_ref[q, :, 0:gram_end].astype(F32)
    lower = lax.broadcasted_iota(jnp.int32, (lay.piece, LANES), 1) < lay.rank
    pres = []
    for s in range(lay.pipe):
        one = r_ref[s * lay.y, :, gram_end:].astype(F32)
        for a in range(1, lay.y):
            one += r_ref[s * lay.y + a, :, gram_end:].astype(F32)
        pres.append(one)
    cols = [total] + [jnp.where(lower, pres[2 * t], pres[2 * t + 1]) for t in range(lay.tiles)]
    message = jnp.concatenate(cols, axis=1).astype(BF16)
    for q in range(lay.group):
        out_ref[q] = message


def chain_kernel(lay, index, q_ref, w_ref, c_ref, x_ref, out_ref, *scratch):
    along, slope, acts, backs, gram, held = scratch
    width_scale, rank_scale = 1.0 / math.sqrt(lay.width), 1.0 / math.sqrt(lay.rank)
    gram_at, pre_at = lay.ranks, lay.ranks + lay.gram
    each = lay.ranks // lay.group
    for q in range(lay.group):
        p, a = q // lay.y, q % lay.y
        rows = slice(a * lay.rows + p * lay.piece, a * lay.rows + (p + 1) * lay.piece)
        along[rows, :] = q_ref[q, :, 0:gram_at].astype(F32)
        gram[q * each : (q + 1) * each, :] = q_ref[q, :, gram_at:pre_at]
        pre = q_ref[q, :, pre_at:].astype(F32) * width_scale
        gate = 1.0 / (1.0 + jnp.exp(-pre))
        acts[rows, :] = (pre * gate).astype(BF16)
        slope[rows, :] = gate * (1.0 + pre * (1.0 - gate)) * rank_scale
    tokens = lay.y * lay.rows
    lower = lax.broadcasted_iota(jnp.int32, (tokens, LANES), 1) < lay.rank
    for s in range(lay.pipe - 1, -1, -1):
        t, odd = s // 2, s % 2 == 1
        tile = slice(t * LANES, (t + 1) * LANES)
        back = along[:, tile] * slope[:, tile]
        back = jnp.where(lower != odd, back, 0.0).astype(BF16)
        if odd:
            backs[t] = back
        else:
            backs[t] = backs[t] + back
        if s == 0:
            continue
        wide = min(t, 2)
        if wide:
            cols = slice(0, wide * LANES)
            along[:, cols] += width_scale * jnp.dot(
                back, gram[tile, cols], preferred_element_type=F32
            )
        for c in range(2, t):
            cols = slice(c * LANES, (c + 1) * LANES)
            row, side = lay.slots[t, c]
            along[:, cols] += width_scale * jnp.dot(
                back,
                gram[row * LANES : (row + 1) * LANES, side * LANES : (side + 1) * LANES],
                preferred_element_type=F32,
            )
        if odd:
            pair = gram[0:LANES, 0:LANES].astype(F32)
            if t % 2 == 1:
                pair = pltpu.roll(pair, lay.rank, 1)
            if t >= 2:
                pair = jnp.concatenate([pair[lay.rank :], pair[: lay.rank]], axis=0)
            along[:, tile] += width_scale * jnp.dot(
                back, pair.astype(BF16), preferred_element_type=F32
            )
    acted = acts[...]
    back_all = jnp.concatenate([backs[t] for t in range(lay.tiles)], axis=1)
    cross = contract_first(acted, back_all)
    before = lax.broadcasted_iota(jnp.int32, cross.shape, 0) // lay.rank
    after = lax.broadcasted_iota(jnp.int32, cross.shape, 1) // lay.rank
    cross = jnp.where(before < after, cross * width_scale, 0.0).astype(BF16)
    cot_all = c_ref[...].reshape(tokens, lay.share)
    grad_up = contract_first(acted, cot_all) + jnp.dot(
        cross, section_maps(lay, w_ref, 0), preferred_element_type=F32
    )
    grad_up = (grad_up * rank_scale).astype(BF16)
    for s in range(lay.pipe):
        for j in range(lay.per):
            out_ref[s * lay.per + j, lay.rank :, :] = grad_up[
                s * lay.rank : (s + 1) * lay.rank, j * LANES : (j + 1) * LANES
            ]
    mine, odd = index[0] // 2, index[0] % 2
    total = None
    for a in range(lay.y):
        rows = slice(a * lay.rows, (a + 1) * lay.rows)
        part = contract_first(backs[mine, rows, :], x_ref[a, :, 0 : lay.span])
        total = part if total is None else total + part
    held[...] = (total * width_scale).reshape(2, lay.rank, lay.span)
    grad_down = held[odd].astype(BF16)
    for b in range(lay.z):
        out_ref[b, 0 : lay.rank, :] = grad_down[:, b * LANES : (b + 1) * LANES]


def body(saved_inputs, cotangent, weights_bf16, master, moment1, moment2, valid_rows):
    pipe, dp = lax.axis_size("pipe"), lax.axis_size("dp")
    inputs, weights = saved_inputs[0], weights_bf16[0]
    lay = Layout(pipe, dp, inputs.shape[0], inputs.shape[1], weights.shape[1])
    both = ("pipe", "dp")
    index = lax.axis_index("pipe").astype(jnp.int32).reshape(1)

    by_column = sort_columns(lay, valid_rows, inputs, cotangent)
    by_column = lax.all_to_all(by_column, "dp", 0, 0, axis_index_groups=lay.along_y)
    maps = lax.all_gather(weights, "dp", axis_index_groups=lay.along_z)
    cots, maps = lax.optimization_barrier((by_column[:, :, lay.span :], maps))
    cots = lax.ppermute(cots, both, lay.cotangent_turn())
    shared = lax.all_to_all(maps.reshape(pipe, lay.per, 2, lay.rank, LANES), "pipe", 0, 0)
    by_column, cots = lax.optimization_barrier((by_column, cots))
    pre_part = call(
        functools.partial(pre_kernel, lay),
        jax.ShapeDtypeStruct((lay.y, lay.rows, LANES), BF16),
        (index, maps, by_column),
        flops=PRE_WEIGHT * 2 * lay.y * lay.rows * lay.span * LANES,
    )
    message = lay.ranks + lay.gram + LANES
    parts = call(
        functools.partial(pack_kernel, lay),
        jax.ShapeDtypeStruct((lay.group, lay.piece, message), BF16),
        (index, shared, pre_part, cots),
        flops=4 * lay.y * lay.rows * lay.share * lay.ranks,
    )
    parts = lax.all_to_all(parts, both, 0, 0, axis_index_groups=lay.plane)
    reply = 2 * lay.ranks + lay.gram
    sums = call(
        functools.partial(sum_kernel, lay),
        jax.ShapeDtypeStruct((lay.group, lay.piece, reply), BF16),
        (index, parts),
    )
    sums = lax.all_to_all(sums, both, 0, 0, axis_index_groups=lay.plane)
    tokens = lay.y * lay.rows
    grads = call(
        functools.partial(chain_kernel, lay),
        jax.ShapeDtypeStruct((lay.z, 2 * lay.rank, LANES), BF16),
        (index, sums, shared, cots, by_column),
        scratch=(
            pltpu.VMEM((tokens, lay.ranks), F32),
            pltpu.VMEM((tokens, lay.ranks), F32),
            pltpu.VMEM((tokens, lay.ranks), BF16),
            pltpu.VMEM((lay.tiles, tokens, LANES), BF16),
            pltpu.VMEM((lay.ranks, lay.gram), BF16),
            pltpu.VMEM((2, lay.rank, lay.span), F32),
        ),
        flops=8 * tokens * lay.ranks * lay.share,
    )
    grads = lax.all_to_all(grads, "dp", 0, 0, axis_index_groups=lay.along_z)
    grads = jnp.sum(grads.astype(F32), axis=0)
    squares = jnp.sum((grads * grads).reshape(-1, 8, LANES), axis=0)
    grad_up = lax.ppermute(grads[lay.rank :], both, lay.gradient_home())
    squares = jnp.broadcast_to(squares, (lay.group, 8, LANES))
    squares = lax.all_to_all(squares, both, 0, 0, axis_index_groups=lay.plane)
    squares = jnp.broadcast_to(jnp.sum(squares, axis=0), (lay.z, 8, LANES))
    squares = lax.all_to_all(squares, "dp", 0, 0, axis_index_groups=lay.along_z)
    square_sum = jnp.sum(squares)
    norm_limit = CLIP_RMS * math.sqrt(2.0 * pipe * lay.rank * lay.width)
    clip_factor = jnp.minimum(1.0, norm_limit / jnp.sqrt(square_sum + NORM_EPS))
    scaled = jnp.stack([grads[: lay.rank], grad_up]) * clip_factor
    new_moment1 = BETA_ONE * moment1[0] + (1.0 - BETA_ONE) * scaled
    new_moment2 = BETA_TWO * moment2[0] + (1.0 - BETA_TWO) * scaled * scaled
    new_master = master[0] - LEARN_RATE * (
        new_moment1 / (jnp.sqrt(new_moment2) + ADAM_EPS) + DECAY_RATE * master[0]
    )
    return (
        new_master[None],
        new_moment1[None],
        new_moment2[None],
        new_master.astype(BF16)[None],
    )


def solution(mesh):
    in_specs = (
        P("pipe", "dp", None),
        P("dp", "pipe"),
        P("pipe", None, None, "dp"),
        P("pipe", None, None, "dp"),
        P("pipe", None, None, "dp"),
        P("pipe", None, None, "dp"),
        P("dp"),
    )
    out_specs = (
        P("pipe", None, None, "dp"),
        P("pipe", None, None, "dp"),
        P("pipe", None, None, "dp"),
        P("pipe", None, None, "dp"),
    )
    return jax.shard_map(body, mesh=mesh, in_specs=in_specs, out_specs=out_specs, check_vma=False)
```

```python
import functools
import math

import jax
import jax.numpy as jnp
from jax import lax
from jax.experimental import pallas as pl
from jax.experimental.pallas import tpu as pltpu
from jax.sharding import PartitionSpec as P

BETA_ONE = 0.9
BETA_TWO = 0.95
LEARN_RATE = 0.05
DECAY_RATE = 0.1
ADAM_EPS = 1e-08
CLIP_RMS = 2.0
NORM_EPS = 1e-12

LANES = 128
Y_SIZE = 4
VMEM_LIMIT = 48 * 1024 * 1024
SORT_LIMIT = 63 * 1024 * 1024
PRE_WEIGHT = 12
INTERPRET = False
BF16 = jnp.bfloat16
F32 = jnp.float32


def contract_last(a, b):
    return lax.dot_general(a, b, (((1,), (1,)), ((), ())), preferred_element_type=F32)


def contract_first(a, b):
    return lax.dot_general(a, b, (((0,), (0,)), ((), ())), preferred_element_type=F32)


def vmem_specs(count):
    return [pl.BlockSpec(memory_space=pltpu.VMEM)] * count


def call(kernel, out_shape, operands, scratch=(), flops=0):
    size = sum(math.prod(a.shape) * a.dtype.itemsize for a in (*operands, out_shape))
    return pl.pallas_call(
        kernel,
        out_shape=out_shape,
        in_specs=[pl.BlockSpec(memory_space=pltpu.SMEM)] + vmem_specs(len(operands) - 1),
        out_specs=pl.BlockSpec(memory_space=pltpu.VMEM),
        scratch_shapes=list(scratch),
        compiler_params=pltpu.CompilerParams(vmem_limit_bytes=VMEM_LIMIT),
        cost_estimate=pl.CostEstimate(flops=flops, bytes_accessed=size, transcendentals=0),
        interpret=INTERPRET,
    )(*operands)


class Layout:
    def __init__(self, pipe, dp, rows, width, rank):
        self.pipe, self.dp, self.rows, self.width, self.rank = pipe, dp, rows, width, rank
        self.y = Y_SIZE if dp >= 64 else 2
        self.z = dp // self.y
        self.group = pipe * self.y
        self.span = width // self.y
        self.share = width // self.group
        self.per = self.z // pipe
        self.half = pipe // self.y
        self.piece = rows // pipe
        self.tiles = pipe * rank // LANES
        self.ranks = pipe * rank
        self.gram = 2 * LANES
        self.slots = {(a, b): (a, b) for a in range(1, self.tiles) for b in range(min(a, 2))}
        spare = [(a, 1) for a in range(1, self.tiles) if (a, 1) not in self.slots]
        rest = [(a, b) for a in range(1, self.tiles) for b in range(2, a)]
        self.slots.update(zip(rest, spare))
        y, z = self.y, self.z
        self.along_z = [[a * z + b for b in range(z)] for a in range(y)]
        self.along_y = [[a * z + b for a in range(y)] for b in range(z)]
        self.plane = [
            [p * dp + a * z + b for p in range(pipe) for a in range(y)] for b in range(z)
        ]

    def device(self, p, y, z):
        return p * self.dp + y * self.z + z

    def everywhere(self):
        return [(p, a, b) for p in range(self.pipe) for a in range(self.y) for b in range(self.z)]

    def cotangent_turn(self):
        return [
            (
                self.device(p, a, b),
                self.device(self.y * (p % self.half) + a, p // self.half, b),
            )
            for p, a, b in self.everywhere()
        ]

    def gradient_home(self):
        return [
            (
                self.device(p, a, b),
                self.device(b // self.per, a, p * self.per + b % self.per),
            )
            for p, a, b in self.everywhere()
        ]


def sort_kernel(lay, valid, x_ref, c_ref, out_ref, held, cots, sems):
    loads, stores = [], []
    for a in range(lay.y):
        cols = pl.ds(a * lay.span, lay.span)
        loads.append(pltpu.make_async_copy(x_ref.at[:, cols], held.at[a], sems.at[a]))
        stores.append(
            pltpu.make_async_copy(
                held.at[a], out_ref.at[a, :, pl.ds(0, lay.span)], sems.at[lay.y + a]
            )
        )
        loads[a].start()
    cot = c_ref[...]
    live = lax.broadcasted_iota(jnp.int32, cot.shape, 0) < valid[0]
    cots[...] = jnp.where(live, cot, jnp.zeros_like(cot))
    for a in range(lay.y):
        stores.append(
            pltpu.make_async_copy(
                cots.at[:, pl.ds(a * lay.share, lay.share)],
                out_ref.at[a, :, pl.ds(lay.span, lay.share)],
                sems.at[2 * lay.y + a],
            )
        )
        stores[lay.y + a].start()
    for a in range(lay.y):
        loads[a].wait()
        stores[a].start()
    for store in stores:
        store.wait()


def sort_columns(lay, valid_rows, inputs, cotangent):
    both = lay.span + lay.share
    return pl.pallas_call(
        functools.partial(sort_kernel, lay),
        out_shape=jax.ShapeDtypeStruct((lay.y, lay.rows, both), BF16),
        in_specs=[
            pl.BlockSpec(memory_space=pltpu.SMEM),
            pl.BlockSpec(memory_space=pltpu.HBM),
            pl.BlockSpec(memory_space=pltpu.VMEM),
        ],
        out_specs=pl.BlockSpec(memory_space=pltpu.HBM),
        scratch_shapes=[
            pltpu.VMEM((lay.y, lay.rows, lay.span), BF16),
            pltpu.VMEM(cotangent.shape, BF16),
            pltpu.SemaphoreType.DMA((3 * lay.y,)),
        ],
        compiler_params=pltpu.CompilerParams(vmem_limit_bytes=SORT_LIMIT),
        cost_estimate=pl.CostEstimate(
            flops=0, bytes_accessed=4 * lay.y * lay.rows * both, transcendentals=0
        ),
        interpret=INTERPRET,
    )(valid_rows, inputs, cotangent)


def pre_kernel(lay, index, w_ref, x_ref, out_ref):
    lower = index[0] % 2
    maps = jnp.concatenate(
        [jnp.concatenate([w_ref[b, lower], w_ref[b, 1 - lower]], axis=0) for b in range(lay.z)],
        axis=1,
    )
    for a in range(lay.y):
        out_ref[a] = contract_last(x_ref[a, :, 0 : lay.span], maps).astype(BF16)


def section_maps(lay, w_ref, which):
    return jnp.concatenate(
        [
            jnp.concatenate([w_ref[s, j, which] for j in range(lay.per)], axis=1)
            for s in range(lay.pipe)
        ],
        axis=0,
    )


def gram_tile(down, up, row, col):
    rows, cols = slice(row * LANES, (row + 1) * LANES), slice(col * LANES, (col + 1) * LANES)
    return contract_last(down[rows], up[cols]).astype(BF16)


def diagonal_tile(lay, down, up):
    rank = lay.rank
    lower = lax.broadcasted_iota(jnp.int32, (rank, LANES), 1) < rank
    blocks = []
    for t in range(lay.tiles):
        odd = down[t * LANES + rank : (t + 1) * LANES]
        block = contract_last(odd, up[t * LANES : (t + 1) * LANES])
        blocks.append(block if t % 2 == 0 else pltpu.roll(block, rank, 1))
    halves = [jnp.where(lower, blocks[t], blocks[t + 1]) for t in range(0, lay.tiles, 2)]
    if len(halves) == 1:
        halves.append(halves[0])
    return jnp.concatenate(halves[::-1], axis=0).astype(BF16)


def pack_kernel(lay, index, w_ref, pre_ref, c_ref, out_ref):
    down, up = section_maps(lay, w_ref, 0), section_maps(lay, w_ref, 1)
    gram_at, pre_at = lay.ranks, lay.ranks + lay.gram
    for a in range(lay.y):
        part = contract_last(c_ref[a], up).astype(BF16)
        for p in range(lay.pipe):
            rows = slice(p * lay.piece, (p + 1) * lay.piece)
            out_ref[p * lay.y + a, :, 0:gram_at] = part[rows]
            out_ref[p * lay.y + a, :, pre_at:] = pre_ref[a, rows, :]
    grams = {spot: gram_tile(down, up, *tile) for tile, spot in lay.slots.items()}
    grams[0, 0] = diagonal_tile(lay, down, up)
    each = lay.ranks // lay.group
    count = LANES // each
    for t in range(lay.tiles):
        for side in range(2):
            cols = slice(gram_at + side * LANES, gram_at + (side + 1) * LANES)
            tile = grams.get((t, side), jnp.zeros((LANES, LANES), BF16))
            for q in range(count):
                out_ref[t * count + q, :, cols] = tile[q * each : (q + 1) * each]


def sum_kernel(lay, index, r_ref, out_ref):
    gram_end = lay.ranks + lay.gram
    total = r_ref[0, :, 0:gram_end].astype(F32)
    for q in range(1, lay.group):
        total += r_ref[q, :, 0:gram_end].astype(F32)
    lower = lax.broadcasted_iota(jnp.int32, (lay.piece, LANES), 1) < lay.rank
    pres = []
    for s in range(lay.pipe):
        one = r_ref[s * lay.y, :, gram_end:].astype(F32)
        for a in range(1, lay.y):
            one += r_ref[s * lay.y + a, :, gram_end:].astype(F32)
        pres.append(one)
    cols = [total] + [jnp.where(lower, pres[2 * t], pres[2 * t + 1]) for t in range(lay.tiles)]
    message = jnp.concatenate(cols, axis=1).astype(BF16)
    for q in range(lay.group):
        out_ref[q] = message


def chain_kernel(lay, index, q_ref, w_ref, c_ref, x_ref, out_ref, *scratch):
    along, slope, acts, backs, gram, held = scratch
    width_scale, rank_scale = 1.0 / math.sqrt(lay.width), 1.0 / math.sqrt(lay.rank)
    gram_at, pre_at = lay.ranks, lay.ranks + lay.gram
    each = lay.ranks // lay.group
    for q in range(lay.group):
        p, a = q // lay.y, q % lay.y
        rows = slice(a * lay.rows + p * lay.piece, a * lay.rows + (p + 1) * lay.piece)
        along[rows, :] = q_ref[q, :, 0:gram_at].astype(F32)
        gram[q * each : (q + 1) * each, :] = q_ref[q, :, gram_at:pre_at]
        pre = q_ref[q, :, pre_at:].astype(F32) * width_scale
        gate = 1.0 / (1.0 + jnp.exp(-pre))
        acts[rows, :] = (pre * gate).astype(BF16)
        slope[rows, :] = gate * (1.0 + pre * (1.0 - gate)) * rank_scale
    tokens = lay.y * lay.rows
    lower = lax.broadcasted_iota(jnp.int32, (tokens, LANES), 1) < lay.rank
    for s in range(lay.pipe - 1, -1, -1):
        t, odd = s // 2, s % 2 == 1
        tile = slice(t * LANES, (t + 1) * LANES)
        back = along[:, tile] * slope[:, tile]
        back = jnp.where(lower != odd, back, 0.0).astype(BF16)
        if odd:
            backs[t] = back
        else:
            backs[t] = backs[t] + back
        if s == 0:
            continue
        wide = min(t, 2)
        if wide:
            cols = slice(0, wide * LANES)
            along[:, cols] += width_scale * jnp.dot(
                back, gram[tile, cols], preferred_element_type=F32
            )
        for c in range(2, t):
            cols = slice(c * LANES, (c + 1) * LANES)
            row, side = lay.slots[t, c]
            along[:, cols] += width_scale * jnp.dot(
                back,
                gram[row * LANES : (row + 1) * LANES, side * LANES : (side + 1) * LANES],
                preferred_element_type=F32,
            )
        if odd:
            pair = gram[0:LANES, 0:LANES].astype(F32)
            if t % 2 == 1:
                pair = pltpu.roll(pair, lay.rank, 1)
            if t >= 2:
                pair = jnp.concatenate([pair[lay.rank :], pair[: lay.rank]], axis=0)
            along[:, tile] += width_scale * jnp.dot(
                back, pair.astype(BF16), preferred_element_type=F32
            )
    acted = acts[...]
    back_all = jnp.concatenate([backs[t] for t in range(lay.tiles)], axis=1)
    cross = contract_first(acted, back_all)
    before = lax.broadcasted_iota(jnp.int32, cross.shape, 0) // lay.rank
    after = lax.broadcasted_iota(jnp.int32, cross.shape, 1) // lay.rank
    cross = jnp.where(before < after, cross * width_scale, 0.0).astype(BF16)
    cot_all = c_ref[...].reshape(tokens, lay.share)
    grad_up = contract_first(acted, cot_all) + jnp.dot(
        cross, section_maps(lay, w_ref, 0), preferred_element_type=F32
    )
    grad_up = (grad_up * rank_scale).astype(BF16)
    for s in range(lay.pipe):
        for j in range(lay.per):
            out_ref[s * lay.per + j, lay.rank :, :] = grad_up[
                s * lay.rank : (s + 1) * lay.rank, j * LANES : (j + 1) * LANES
            ]
    mine, odd = index[0] // 2, index[0] % 2
    total = None
    for a in range(lay.y):
        rows = slice(a * lay.rows, (a + 1) * lay.rows)
        part = contract_first(backs[mine, rows, :], x_ref[a, :, 0 : lay.span])
        total = part if total is None else total + part
    held[...] = (total * width_scale).reshape(2, lay.rank, lay.span)
    grad_down = held[odd].astype(BF16)
    for b in range(lay.z):
        out_ref[b, 0 : lay.rank, :] = grad_down[:, b * LANES : (b + 1) * LANES]


def body(saved_inputs, cotangent, weights_bf16, master, moment1, moment2, valid_rows):
    pipe, dp = lax.axis_size("pipe"), lax.axis_size("dp")
    inputs, weights = saved_inputs[0], weights_bf16[0]
    lay = Layout(pipe, dp, inputs.shape[0], inputs.shape[1], weights.shape[1])
    both = ("pipe", "dp")
    index = lax.axis_index("pipe").astype(jnp.int32).reshape(1)

    by_column = sort_columns(lay, valid_rows, inputs, cotangent)
    by_column = lax.all_to_all(by_column, "dp", 0, 0, axis_index_groups=lay.along_y)
    maps = lax.all_gather(weights, "dp", axis_index_groups=lay.along_z)
    cots, maps = lax.optimization_barrier((by_column[:, :, lay.span :], maps))
    cots = lax.ppermute(cots, both, lay.cotangent_turn())
    shared = lax.all_to_all(maps.reshape(pipe, lay.per, 2, lay.rank, LANES), "pipe", 0, 0)
    by_column, cots = lax.optimization_barrier((by_column, cots))
    pre_part = call(
        functools.partial(pre_kernel, lay),
        jax.ShapeDtypeStruct((lay.y, lay.rows, LANES), BF16),
        (index, maps, by_column),
        flops=PRE_WEIGHT * 2 * lay.y * lay.rows * lay.span * LANES,
    )
    message = lay.ranks + lay.gram + LANES
    parts = call(
        functools.partial(pack_kernel, lay),
        jax.ShapeDtypeStruct((lay.group, lay.piece, message), BF16),
        (index, shared, pre_part, cots),
        flops=4 * lay.y * lay.rows * lay.share * lay.ranks,
    )
    parts = lax.all_to_all(parts, both, 0, 0, axis_index_groups=lay.plane)
    reply = 2 * lay.ranks + lay.gram
    sums = call(
        functools.partial(sum_kernel, lay),
        jax.ShapeDtypeStruct((lay.group, lay.piece, reply), BF16),
        (index, parts),
    )
    sums = lax.all_to_all(sums, both, 0, 0, axis_index_groups=lay.plane)
    tokens = lay.y * lay.rows
    grads = call(
        functools.partial(chain_kernel, lay),
        jax.ShapeDtypeStruct((lay.z, 2 * lay.rank, LANES), BF16),
        (index, sums, shared, cots, by_column),
        scratch=(
            pltpu.VMEM((tokens, lay.ranks), F32),
            pltpu.VMEM((tokens, lay.ranks), F32),
            pltpu.VMEM((tokens, lay.ranks), BF16),
            pltpu.VMEM((lay.tiles, tokens, LANES), BF16),
            pltpu.VMEM((lay.ranks, lay.gram), BF16),
            pltpu.VMEM((2, lay.rank, lay.span), F32),
        ),
        flops=8 * tokens * lay.ranks * lay.share,
    )
    grads = lax.all_to_all(grads, "dp", 0, 0, axis_index_groups=lay.along_z)
    grads = jnp.sum(grads.astype(F32), axis=0)
    squares = jnp.sum((grads * grads).reshape(-1, 8, LANES), axis=0)
    grad_up = lax.ppermute(grads[lay.rank :], both, lay.gradient_home())
    squares = jnp.broadcast_to(squares, (lay.group, 8, LANES))
    squares = lax.all_to_all(squares, both, 0, 0, axis_index_groups=lay.plane)
    squares = jnp.broadcast_to(jnp.sum(squares, axis=0), (lay.z, 8, LANES))
    squares = lax.all_to_all(squares, "dp", 0, 0, axis_index_groups=lay.along_z)
    square_sum = jnp.sum(squares)
    norm_limit = CLIP_RMS * math.sqrt(2.0 * pipe * lay.rank * lay.width)
    clip_factor = jnp.minimum(1.0, norm_limit / jnp.sqrt(square_sum + NORM_EPS))
    scaled = jnp.stack([grads[: lay.rank], grad_up]) * clip_factor
    new_moment1 = BETA_ONE * moment1[0] + (1.0 - BETA_ONE) * scaled
    new_moment2 = BETA_TWO * moment2[0] + (1.0 - BETA_TWO) * scaled * scaled
    new_master = master[0] - LEARN_RATE * (
        new_moment1 / (jnp.sqrt(new_moment2) + ADAM_EPS) + DECAY_RATE * master[0]
    )
    return (
        new_master[None],
        new_moment1[None],
        new_moment2[None],
        new_master.astype(BF16)[None],
    )


def solution(mesh):
    in_specs = (
        P("pipe", "dp", None),
        P("dp", "pipe"),
        P("pipe", None, None, "dp"),
        P("pipe", None, None, "dp"),
        P("pipe", None, None, "dp"),
        P("pipe", None, None, "dp"),
        P("dp"),
    )
    out_specs = (
        P("pipe", None, None, "dp"),
        P("pipe", None, None, "dp"),
        P("pipe", None, None, "dp"),
        P("pipe", None, None, "dp"),
    )
    return jax.shard_map(body, mesh=mesh, in_specs=in_specs, out_specs=out_specs, check_vma=False)
```

```python
import functools
import math

import jax
import jax.numpy as jnp
from jax import lax
from jax.experimental import pallas as pl
from jax.experimental.pallas import tpu as pltpu
from jax.sharding import PartitionSpec as P

BETA_ONE = 0.9
BETA_TWO = 0.95
LEARN_RATE = 0.05
DECAY_RATE = 0.1
ADAM_EPS = 1e-08
CLIP_RMS = 2.0
NORM_EPS = 1e-12

LANES = 128
Y_SIZE = 4
VMEM_LIMIT = 48 * 1024 * 1024
SORT_LIMIT = 63 * 1024 * 1024
INTERPRET = False
BF16 = jnp.bfloat16
F32 = jnp.float32


def contract_last(a, b):
    return lax.dot_general(a, b, (((1,), (1,)), ((), ())), preferred_element_type=F32)


def contract_first(a, b):
    return lax.dot_general(a, b, (((0,), (0,)), ((), ())), preferred_element_type=F32)


def vmem_specs(count):
    return [pl.BlockSpec(memory_space=pltpu.VMEM)] * count


def call(kernel, out_shape, operands, scratch=(), flops=0):
    size = sum(math.prod(a.shape) * a.dtype.itemsize for a in (*operands, out_shape))
    return pl.pallas_call(
        kernel,
        out_shape=out_shape,
        in_specs=[pl.BlockSpec(memory_space=pltpu.SMEM)] + vmem_specs(len(operands) - 1),
        out_specs=pl.BlockSpec(memory_space=pltpu.VMEM),
        scratch_shapes=list(scratch),
        compiler_params=pltpu.CompilerParams(vmem_limit_bytes=VMEM_LIMIT),
        cost_estimate=pl.CostEstimate(flops=flops, bytes_accessed=size, transcendentals=0),
        interpret=INTERPRET,
    )(*operands)


class Layout:
    def __init__(self, pipe, dp, rows, width, rank):
        self.pipe, self.dp, self.rows, self.width, self.rank = pipe, dp, rows, width, rank
        self.y = Y_SIZE if dp >= 64 else 2
        self.z = dp // self.y
        self.group = pipe * self.y
        self.span = width // self.y
        self.share = width // self.group
        self.per = self.z // pipe
        self.half = pipe // self.y
        self.piece = rows // pipe
        self.tiles = pipe * rank // LANES
        self.ranks = pipe * rank
        self.gram = 2 * LANES
        self.slots = {(a, b): (a, b) for a in range(1, self.tiles) for b in range(min(a, 2))}
        spare = [(a, 1) for a in range(1, self.tiles) if (a, 1) not in self.slots]
        rest = [(a, b) for a in range(1, self.tiles) for b in range(2, a)]
        self.slots.update(zip(rest, spare))
        y, z = self.y, self.z
        half = self.half
        self.order = [half * m + h for h in range(half) for m in range(y)]
        self.across = [[half * m + h for m in range(y)] for h in range(half)]
        self.along_z = [[a * z + b for b in range(z)] for a in range(y)]
        self.along_y = [[a * z + b for a in range(y)] for b in range(z)]
        self.plane = [
            [p * dp + a * z + b for p in range(pipe) for a in range(y)] for b in range(z)
        ]

    def device(self, p, y, z):
        return p * self.dp + y * self.z + z

    def everywhere(self):
        return [(p, a, b) for p in range(self.pipe) for a in range(self.y) for b in range(self.z)]

    def gradient_home(self):
        return [
            (
                self.device(p, a, b),
                self.device(b // self.per, a, self.order.index(p) * self.per + b % self.per),
            )
            for p, a, b in self.everywhere()
        ]


def split_kernel(lay, valid, c_ref, out_ref):
    cot = c_ref[...]
    live = lax.broadcasted_iota(jnp.int32, cot.shape, 0) < valid[0]
    cot = jnp.where(live, cot, jnp.zeros_like(cot))
    for m in range(lay.y):
        out_ref[m] = cot[:, m * lay.share : (m + 1) * lay.share]


def sort_kernel(lay, x_ref, out_ref, held, sems):
    loads, stores = [], []
    for a in range(lay.y):
        cols = pl.ds(a * lay.span, lay.span)
        loads.append(pltpu.make_async_copy(x_ref.at[:, cols], held.at[a], sems.at[a]))
        stores.append(
            pltpu.make_async_copy(
                held.at[a], out_ref.at[a, :, pl.ds(0, lay.span)], sems.at[lay.y + a]
            )
        )
        loads[a].start()
    for a in range(lay.y):
        loads[a].wait()
        stores[a].start()
    for store in stores:
        store.wait()


def sort_columns(lay, inputs):
    both = lay.span + lay.share
    return pl.pallas_call(
        functools.partial(sort_kernel, lay),
        out_shape=jax.ShapeDtypeStruct((lay.y, lay.rows, both), BF16),
        in_specs=[pl.BlockSpec(memory_space=pltpu.HBM)],
        out_specs=pl.BlockSpec(memory_space=pltpu.HBM),
        scratch_shapes=[
            pltpu.VMEM((lay.y, lay.rows, lay.span), BF16),
            pltpu.SemaphoreType.DMA((2 * lay.y,)),
        ],
        compiler_params=pltpu.CompilerParams(vmem_limit_bytes=SORT_LIMIT),
        cost_estimate=pl.CostEstimate(
            flops=0, bytes_accessed=4 * lay.y * lay.rows * both, transcendentals=0
        ),
        interpret=INTERPRET,
    )(inputs)


def join_kernel(lay, by_column, c_ref, out_ref, sem):
    copy = pltpu.make_async_copy(c_ref, out_ref.at[:, :, pl.ds(lay.span, lay.share)], sem)
    copy.start()
    copy.wait()


def join_columns(lay, by_column, cots):
    return pl.pallas_call(
        functools.partial(join_kernel, lay),
        out_shape=jax.ShapeDtypeStruct(by_column.shape, BF16),
        in_specs=[
            pl.BlockSpec(memory_space=pltpu.HBM),
            pl.BlockSpec(memory_space=pltpu.VMEM),
        ],
        out_specs=pl.BlockSpec(memory_space=pltpu.HBM),
        input_output_aliases={0: 0},
        scratch_shapes=[pltpu.SemaphoreType.DMA],
        compiler_params=pltpu.CompilerParams(vmem_limit_bytes=SORT_LIMIT),
        cost_estimate=pl.CostEstimate(
            flops=0, bytes_accessed=4 * math.prod(cots.shape), transcendentals=0
        ),
        interpret=INTERPRET,
    )(by_column, cots)


def pre_kernel(lay, index, w_ref, x_ref, out_ref):
    lower = index[0] % 2
    maps = jnp.concatenate(
        [jnp.concatenate([w_ref[b, lower], w_ref[b, 1 - lower]], axis=0) for b in range(lay.z)],
        axis=1,
    )
    for a in range(lay.y):
        out_ref[a] = contract_last(x_ref[a, :, 0 : lay.span], maps).astype(BF16)


def section_maps(lay, w_ref, which):
    return jnp.concatenate(
        [
            jnp.concatenate([w_ref[lay.order.index(s), j, which] for j in range(lay.per)], axis=1)
            for s in range(lay.pipe)
        ],
        axis=0,
    )


def gram_tile(down, up, row, col):
    rows, cols = slice(row * LANES, (row + 1) * LANES), slice(col * LANES, (col + 1) * LANES)
    return contract_last(down[rows], up[cols]).astype(BF16)


def diagonal_tile(lay, down, up):
    rank = lay.rank
    lower = lax.broadcasted_iota(jnp.int32, (rank, LANES), 1) < rank
    blocks = []
    for t in range(lay.tiles):
        odd = down[t * LANES + rank : (t + 1) * LANES]
        block = contract_last(odd, up[t * LANES : (t + 1) * LANES])
        blocks.append(block if t % 2 == 0 else pltpu.roll(block, rank, 1))
    halves = [jnp.where(lower, blocks[t], blocks[t + 1]) for t in range(0, lay.tiles, 2)]
    if len(halves) == 1:
        halves.append(halves[0])
    return jnp.concatenate(halves[::-1], axis=0).astype(BF16)


def pack_kernel(lay, index, w_ref, pre_ref, c_ref, out_ref):
    down, up = section_maps(lay, w_ref, 0), section_maps(lay, w_ref, 1)
    gram_at, pre_at = lay.ranks, lay.ranks + lay.gram
    for a in range(lay.y):
        part = contract_last(c_ref[a, :, lay.span :], up).astype(BF16)
        for p in range(lay.pipe):
            rows = slice(p * lay.piece, (p + 1) * lay.piece)
            out_ref[p * lay.y + a, :, 0:gram_at] = part[rows]
            out_ref[p * lay.y + a, :, pre_at:] = pre_ref[a, rows, :]
    grams = {spot: gram_tile(down, up, *tile) for tile, spot in lay.slots.items()}
    grams[0, 0] = diagonal_tile(lay, down, up)
    each = lay.ranks // lay.group
    count = LANES // each
    for t in range(lay.tiles):
        for side in range(2):
            cols = slice(gram_at + side * LANES, gram_at + (side + 1) * LANES)
            tile = grams.get((t, side), jnp.zeros((LANES, LANES), BF16))
            for q in range(count):
                out_ref[t * count + q, :, cols] = tile[q * each : (q + 1) * each]


def sum_kernel(lay, index, r_ref, out_ref):
    gram_end = lay.ranks + lay.gram
    total = r_ref[0, :, 0:gram_end].astype(F32)
    for q in range(1, lay.group):
        total += r_ref[q, :, 0:gram_end].astype(F32)
    lower = lax.broadcasted_iota(jnp.int32, (lay.piece, LANES), 1) < lay.rank
    pres = []
    for s in range(lay.pipe):
        one = r_ref[s * lay.y, :, gram_end:].astype(F32)
        for a in range(1, lay.y):
            one += r_ref[s * lay.y + a, :, gram_end:].astype(F32)
        pres.append(one)
    cols = [total] + [jnp.where(lower, pres[2 * t], pres[2 * t + 1]) for t in range(lay.tiles)]
    message = jnp.concatenate(cols, axis=1).astype(BF16)
    for q in range(lay.group):
        out_ref[q] = message


def chain_kernel(lay, index, q_ref, w_ref, x_ref, out_ref, *scratch):
    along, slope, acts, backs, gram, held = scratch
    width_scale, rank_scale = 1.0 / math.sqrt(lay.width), 1.0 / math.sqrt(lay.rank)
    gram_at, pre_at = lay.ranks, lay.ranks + lay.gram
    each = lay.ranks // lay.group
    for q in range(lay.group):
        p, a = q // lay.y, q % lay.y
        rows = slice(a * lay.rows + p * lay.piece, a * lay.rows + (p + 1) * lay.piece)
        along[rows, :] = q_ref[q, :, 0:gram_at].astype(F32)
        gram[q * each : (q + 1) * each, :] = q_ref[q, :, gram_at:pre_at]
        pre = q_ref[q, :, pre_at:].astype(F32) * width_scale
        gate = 1.0 / (1.0 + jnp.exp(-pre))
        acts[rows, :] = (pre * gate).astype(BF16)
        slope[rows, :] = gate * (1.0 + pre * (1.0 - gate)) * rank_scale
    tokens = lay.y * lay.rows
    lower = lax.broadcasted_iota(jnp.int32, (tokens, LANES), 1) < lay.rank
    for s in range(lay.pipe - 1, -1, -1):
        t, odd = s // 2, s % 2 == 1
        tile = slice(t * LANES, (t + 1) * LANES)
        back = along[:, tile] * slope[:, tile]
        back = jnp.where(lower != odd, back, 0.0).astype(BF16)
        if odd:
            backs[t] = back
        else:
            backs[t] = backs[t] + back
        if s == 0:
            continue
        wide = min(t, 2)
        if wide:
            cols = slice(0, wide * LANES)
            along[:, cols] += width_scale * jnp.dot(
                back, gram[tile, cols], preferred_element_type=F32
            )
        for c in range(2, t):
            cols = slice(c * LANES, (c + 1) * LANES)
            row, side = lay.slots[t, c]
            along[:, cols] += width_scale * jnp.dot(
                back,
                gram[row * LANES : (row + 1) * LANES, side * LANES : (side + 1) * LANES],
                preferred_element_type=F32,
            )
        if odd:
            pair = gram[0:LANES, 0:LANES].astype(F32)
            if t % 2 == 1:
                pair = pltpu.roll(pair, lay.rank, 1)
            if t >= 2:
                pair = jnp.concatenate([pair[lay.rank :], pair[: lay.rank]], axis=0)
            along[:, tile] += width_scale * jnp.dot(
                back, pair.astype(BF16), preferred_element_type=F32
            )
    acted = acts[...]
    back_all = jnp.concatenate([backs[t] for t in range(lay.tiles)], axis=1)
    cross = contract_first(acted, back_all)
    before = lax.broadcasted_iota(jnp.int32, cross.shape, 0) // lay.rank
    after = lax.broadcasted_iota(jnp.int32, cross.shape, 1) // lay.rank
    cross = jnp.where(before < after, cross * width_scale, 0.0).astype(BF16)
    cot_all = x_ref[:, :, lay.span :].reshape(tokens, lay.share)
    grad_up = contract_first(acted, cot_all) + jnp.dot(
        cross, section_maps(lay, w_ref, 0), preferred_element_type=F32
    )
    grad_up = (grad_up * rank_scale).astype(BF16)
    for s in range(lay.pipe):
        for j in range(lay.per):
            out_ref[s * lay.per + j, lay.rank :, :] = grad_up[
                s * lay.rank : (s + 1) * lay.rank, j * LANES : (j + 1) * LANES
            ]
    mine, odd = index[0] // 2, index[0] % 2
    total = None
    for a in range(lay.y):
        rows = slice(a * lay.rows, (a + 1) * lay.rows)
        part = contract_first(backs[mine, rows, :], x_ref[a, :, 0 : lay.span])
        total = part if total is None else total + part
    held[...] = (total * width_scale).reshape(2, lay.rank, lay.span)
    grad_down = held[odd].astype(BF16)
    for b in range(lay.z):
        out_ref[b, 0 : lay.rank, :] = grad_down[:, b * LANES : (b + 1) * LANES]


def body(saved_inputs, cotangent, weights_bf16, master, moment1, moment2, valid_rows):
    pipe, dp = lax.axis_size("pipe"), lax.axis_size("dp")
    inputs, weights = saved_inputs[0], weights_bf16[0]
    lay = Layout(pipe, dp, inputs.shape[0], inputs.shape[1], weights.shape[1])
    both = ("pipe", "dp")
    index = lax.axis_index("pipe").astype(jnp.int32).reshape(1)

    cots = call(
        functools.partial(split_kernel, lay),
        jax.ShapeDtypeStruct((lay.y, lay.rows, lay.share), BF16),
        (valid_rows, cotangent),
    )
    cots = lax.all_to_all(cots, "pipe", 0, 0, axis_index_groups=lay.across)
    by_column = join_columns(lay, sort_columns(lay, inputs), cots)
    by_column = lax.all_to_all(by_column, "dp", 0, 0, axis_index_groups=lay.along_y)
    maps = lax.all_gather(weights, "dp", axis_index_groups=lay.along_z)
    shared = lax.all_to_all(
        maps.reshape(pipe, lay.per, 2, lay.rank, LANES),
        "pipe",
        0,
        0,
        axis_index_groups=[lay.order],
    )
    pre_part = call(
        functools.partial(pre_kernel, lay),
        jax.ShapeDtypeStruct((lay.y, lay.rows, LANES), BF16),
        (index, maps, by_column),
        flops=2 * lay.y * lay.rows * lay.span * LANES,
    )
    message = lay.ranks + lay.gram + LANES
    parts = call(
        functools.partial(pack_kernel, lay),
        jax.ShapeDtypeStruct((lay.group, lay.piece, message), BF16),
        (index, shared, pre_part, by_column),
        flops=4 * lay.y * lay.rows * lay.share * lay.ranks,
    )
    parts = lax.all_to_all(parts, both, 0, 0, axis_index_groups=lay.plane)
    reply = 2 * lay.ranks + lay.gram
    sums = call(
        functools.partial(sum_kernel, lay),
        jax.ShapeDtypeStruct((lay.group, lay.piece, reply), BF16),
        (index, parts),
    )
    sums = lax.all_to_all(sums, both, 0, 0, axis_index_groups=lay.plane)
    tokens = lay.y * lay.rows
    grads = call(
        functools.partial(chain_kernel, lay),
        jax.ShapeDtypeStruct((lay.z, 2 * lay.rank, LANES), BF16),
        (index, sums, shared, by_column),
        scratch=(
            pltpu.VMEM((tokens, lay.ranks), F32),
            pltpu.VMEM((tokens, lay.ranks), F32),
            pltpu.VMEM((tokens, lay.ranks), BF16),
            pltpu.VMEM((lay.tiles, tokens, LANES), BF16),
            pltpu.VMEM((lay.ranks, lay.gram), BF16),
            pltpu.VMEM((2, lay.rank, lay.span), F32),
        ),
        flops=8 * tokens * lay.ranks * lay.share,
    )
    grads = lax.all_to_all(grads, "dp", 0, 0, axis_index_groups=lay.along_z)
    grads = jnp.sum(grads.astype(F32), axis=0)
    squares = jnp.sum((grads * grads).reshape(-1, 8, LANES), axis=0)
    grad_up = lax.ppermute(grads[lay.rank :], both, lay.gradient_home())
    squares = jnp.broadcast_to(squares, (lay.group, 8, LANES))
    squares = lax.all_to_all(squares, both, 0, 0, axis_index_groups=lay.plane)
    squares = jnp.broadcast_to(jnp.sum(squares, axis=0), (lay.z, 8, LANES))
    squares = lax.all_to_all(squares, "dp", 0, 0, axis_index_groups=lay.along_z)
    square_sum = jnp.sum(squares)
    norm_limit = CLIP_RMS * math.sqrt(2.0 * pipe * lay.rank * lay.width)
    clip_factor = jnp.minimum(1.0, norm_limit / jnp.sqrt(square_sum + NORM_EPS))
    scaled = jnp.stack([grads[: lay.rank], grad_up]) * clip_factor
    new_moment1 = BETA_ONE * moment1[0] + (1.0 - BETA_ONE) * scaled
    new_moment2 = BETA_TWO * moment2[0] + (1.0 - BETA_TWO) * scaled * scaled
    new_master = master[0] - LEARN_RATE * (
        new_moment1 / (jnp.sqrt(new_moment2) + ADAM_EPS) + DECAY_RATE * master[0]
    )
    return (
        new_master[None],
        new_moment1[None],
        new_moment2[None],
        new_master.astype(BF16)[None],
    )


def solution(mesh):
    in_specs = (
        P("pipe", "dp", None),
        P("dp", "pipe"),
        P("pipe", None, None, "dp"),
        P("pipe", None, None, "dp"),
        P("pipe", None, None, "dp"),
        P("pipe", None, None, "dp"),
        P("dp"),
    )
    out_specs = (
        P("pipe", None, None, "dp"),
        P("pipe", None, None, "dp"),
        P("pipe", None, None, "dp"),
        P("pipe", None, None, "dp"),
    )
    return jax.shard_map(body, mesh=mesh, in_specs=in_specs, out_specs=out_specs, check_vma=False)
```

```python
import functools
import math

import jax
import jax.numpy as jnp
from jax import lax
from jax.experimental import pallas as pl
from jax.experimental.pallas import tpu as pltpu
from jax.sharding import PartitionSpec as P

BETA_ONE = 0.9
BETA_TWO = 0.95
LEARN_RATE = 0.05
DECAY_RATE = 0.1
ADAM_EPS = 1e-08
CLIP_RMS = 2.0
NORM_EPS = 1e-12

LANES = 128
Y_SIZE = 4
VMEM_LIMIT = 48 * 1024 * 1024
SORT_LIMIT = 63 * 1024 * 1024
PRE_WEIGHT = 12
INTERPRET = False
BF16 = jnp.bfloat16
F32 = jnp.float32


def contract_last(a, b):
    return lax.dot_general(a, b, (((1,), (1,)), ((), ())), preferred_element_type=F32)


def contract_first(a, b):
    return lax.dot_general(a, b, (((0,), (0,)), ((), ())), preferred_element_type=F32)


def vmem_specs(count):
    return [pl.BlockSpec(memory_space=pltpu.VMEM)] * count


def call(kernel, out_shape, operands, scratch=(), flops=0):
    size = sum(math.prod(a.shape) * a.dtype.itemsize for a in (*operands, out_shape))
    return pl.pallas_call(
        kernel,
        out_shape=out_shape,
        in_specs=[pl.BlockSpec(memory_space=pltpu.SMEM)] + vmem_specs(len(operands) - 1),
        out_specs=pl.BlockSpec(memory_space=pltpu.VMEM),
        scratch_shapes=list(scratch),
        compiler_params=pltpu.CompilerParams(vmem_limit_bytes=VMEM_LIMIT),
        cost_estimate=pl.CostEstimate(flops=flops, bytes_accessed=size, transcendentals=0),
        interpret=INTERPRET,
    )(*operands)


class Layout:
    def __init__(self, pipe, dp, rows, width, rank):
        self.pipe, self.dp, self.rows, self.width, self.rank = pipe, dp, rows, width, rank
        self.y = Y_SIZE if dp >= 64 else 2
        self.z = dp // self.y
        self.group = pipe * self.y
        self.span = width // self.y
        self.share = width // self.group
        self.per = self.z // pipe
        self.half = pipe // self.y
        self.piece = rows // pipe
        self.tiles = pipe * rank // LANES
        self.ranks = pipe * rank
        self.gram = 2 * LANES
        self.slots = {(a, b): (a, b) for a in range(1, self.tiles) for b in range(min(a, 2))}
        spare = [(a, 1) for a in range(1, self.tiles) if (a, 1) not in self.slots]
        rest = [(a, b) for a in range(1, self.tiles) for b in range(2, a)]
        self.slots.update(zip(rest, spare))
        y, z = self.y, self.z
        self.along_z = [[a * z + b for b in range(z)] for a in range(y)]
        self.along_y = [[a * z + b for a in range(y)] for b in range(z)]
        self.plane = [
            [p * dp + a * z + b for p in range(pipe) for a in range(y)] for b in range(z)
        ]

    def device(self, p, y, z):
        return p * self.dp + y * self.z + z

    def everywhere(self):
        return [(p, a, b) for p in range(self.pipe) for a in range(self.y) for b in range(self.z)]

    def cotangent_turn(self):
        return [
            (
                self.device(p, a, b),
                self.device(self.y * (p % self.half) + a, p // self.half, b),
            )
            for p, a, b in self.everywhere()
        ]

    def gradient_home(self):
        return [
            (
                self.device(p, a, b),
                self.device(b // self.per, a, p * self.per + b % self.per),
            )
            for p, a, b in self.everywhere()
        ]


def sort_kernel(lay, valid, x_ref, c_ref, out_ref, held, cots, sems):
    loads, stores = [], []
    fetch = pltpu.make_async_copy(c_ref, cots, sems.at[3 * lay.y])
    fetch.start()
    for a in range(lay.y):
        cols = pl.ds(a * lay.span, lay.span)
        loads.append(pltpu.make_async_copy(x_ref.at[:, cols], held.at[a], sems.at[a]))
        stores.append(
            pltpu.make_async_copy(
                held.at[a], out_ref.at[a, :, pl.ds(0, lay.span)], sems.at[lay.y + a]
            )
        )
        loads[a].start()
    fetch.wait()
    cot = cots[...]
    live = lax.broadcasted_iota(jnp.int32, cot.shape, 0) < valid[0]
    cots[...] = jnp.where(live, cot, jnp.zeros_like(cot))
    for a in range(lay.y):
        stores.append(
            pltpu.make_async_copy(
                cots.at[:, pl.ds(a * lay.share, lay.share)],
                out_ref.at[a, :, pl.ds(lay.span, lay.share)],
                sems.at[2 * lay.y + a],
            )
        )
        stores[lay.y + a].start()
    for a in range(lay.y):
        loads[a].wait()
        stores[a].start()
    for store in stores:
        store.wait()


def sort_columns(lay, valid_rows, inputs, cotangent):
    both = lay.span + lay.share
    return pl.pallas_call(
        functools.partial(sort_kernel, lay),
        out_shape=jax.ShapeDtypeStruct((lay.y, lay.rows, both), BF16),
        in_specs=[
            pl.BlockSpec(memory_space=pltpu.SMEM),
            pl.BlockSpec(memory_space=pltpu.HBM),
            pl.BlockSpec(memory_space=pltpu.HBM),
        ],
        out_specs=pl.BlockSpec(memory_space=pltpu.HBM),
        scratch_shapes=[
            pltpu.VMEM((lay.y, lay.rows, lay.span), BF16),
            pltpu.VMEM(cotangent.shape, BF16),
            pltpu.SemaphoreType.DMA((3 * lay.y + 1,)),
        ],
        compiler_params=pltpu.CompilerParams(vmem_limit_bytes=SORT_LIMIT),
        cost_estimate=pl.CostEstimate(
            flops=0, bytes_accessed=4 * lay.y * lay.rows * both, transcendentals=0
        ),
        interpret=INTERPRET,
    )(valid_rows, inputs, cotangent)


def pre_kernel(lay, index, w_ref, x_ref, out_ref):
    lower = index[0] % 2
    maps = jnp.concatenate(
        [jnp.concatenate([w_ref[b, lower], w_ref[b, 1 - lower]], axis=0) for b in range(lay.z)],
        axis=1,
    )
    for a in range(lay.y):
        out_ref[a] = contract_last(x_ref[a, :, 0 : lay.span], maps).astype(BF16)


def section_maps(lay, w_ref, which):
    return jnp.concatenate(
        [
            jnp.concatenate([w_ref[s, j, which] for j in range(lay.per)], axis=1)
            for s in range(lay.pipe)
        ],
        axis=0,
    )


def gram_tile(down, up, row, col):
    rows, cols = slice(row * LANES, (row + 1) * LANES), slice(col * LANES, (col + 1) * LANES)
    return contract_last(down[rows], up[cols]).astype(BF16)


def diagonal_tile(lay, down, up):
    rank = lay.rank
    lower = lax.broadcasted_iota(jnp.int32, (rank, LANES), 1) < rank
    blocks = []
    for t in range(lay.tiles):
        odd = down[t * LANES + rank : (t + 1) * LANES]
        block = contract_last(odd, up[t * LANES : (t + 1) * LANES])
        blocks.append(block if t % 2 == 0 else pltpu.roll(block, rank, 1))
    halves = [jnp.where(lower, blocks[t], blocks[t + 1]) for t in range(0, lay.tiles, 2)]
    if len(halves) == 1:
        halves.append(halves[0])
    return jnp.concatenate(halves[::-1], axis=0).astype(BF16)


def pack_kernel(lay, index, w_ref, pre_ref, c_ref, out_ref):
    down, up = section_maps(lay, w_ref, 0), section_maps(lay, w_ref, 1)
    gram_at, pre_at = lay.ranks, lay.ranks + lay.gram
    for a in range(lay.y):
        part = contract_last(c_ref[a], up).astype(BF16)
        for p in range(lay.pipe):
            rows = slice(p * lay.piece, (p + 1) * lay.piece)
            out_ref[p * lay.y + a, :, 0:gram_at] = part[rows]
            out_ref[p * lay.y + a, :, pre_at:] = pre_ref[a, rows, :]
    grams = {spot: gram_tile(down, up, *tile) for tile, spot in lay.slots.items()}
    grams[0, 0] = diagonal_tile(lay, down, up)
    each = lay.ranks // lay.group
    count = LANES // each
    for t in range(lay.tiles):
        for side in range(2):
            cols = slice(gram_at + side * LANES, gram_at + (side + 1) * LANES)
            tile = grams.get((t, side), jnp.zeros((LANES, LANES), BF16))
            for q in range(count):
                out_ref[t * count + q, :, cols] = tile[q * each : (q + 1) * each]


def sum_kernel(lay, index, r_ref, out_ref):
    gram_end = lay.ranks + lay.gram
    total = r_ref[0, :, 0:gram_end].astype(F32)
    for q in range(1, lay.group):
        total += r_ref[q, :, 0:gram_end].astype(F32)
    lower = lax.broadcasted_iota(jnp.int32, (lay.piece, LANES), 1) < lay.rank
    pres = []
    for s in range(lay.pipe):
        one = r_ref[s * lay.y, :, gram_end:].astype(F32)
        for a in range(1, lay.y):
            one += r_ref[s * lay.y + a, :, gram_end:].astype(F32)
        pres.append(one)
    cols = [total] + [jnp.where(lower, pres[2 * t], pres[2 * t + 1]) for t in range(lay.tiles)]
    message = jnp.concatenate(cols, axis=1).astype(BF16)
    for q in range(lay.group):
        out_ref[q] = message


def chain_kernel(lay, index, q_ref, w_ref, c_ref, x_ref, out_ref, *scratch):
    along, slope, acts, backs, gram, held = scratch
    width_scale, rank_scale = 1.0 / math.sqrt(lay.width), 1.0 / math.sqrt(lay.rank)
    gram_at, pre_at = lay.ranks, lay.ranks + lay.gram
    each = lay.ranks // lay.group
    for q in range(lay.group):
        p, a = q // lay.y, q % lay.y
        rows = slice(a * lay.rows + p * lay.piece, a * lay.rows + (p + 1) * lay.piece)
        along[rows, :] = q_ref[q, :, 0:gram_at].astype(F32)
        gram[q * each : (q + 1) * each, :] = q_ref[q, :, gram_at:pre_at]
        pre = q_ref[q, :, pre_at:].astype(F32) * width_scale
        gate = 1.0 / (1.0 + jnp.exp(-pre))
        acts[rows, :] = (pre * gate).astype(BF16)
        slope[rows, :] = gate * (1.0 + pre * (1.0 - gate)) * rank_scale
    tokens = lay.y * lay.rows
    lower = lax.broadcasted_iota(jnp.int32, (tokens, LANES), 1) < lay.rank
    for s in range(lay.pipe - 1, -1, -1):
        t, odd = s // 2, s % 2 == 1
        tile = slice(t * LANES, (t + 1) * LANES)
        back = along[:, tile] * slope[:, tile]
        back = jnp.where(lower != odd, back, 0.0).astype(BF16)
        if odd:
            backs[t] = back
        else:
            backs[t] = backs[t] + back
        if s == 0:
            continue
        wide = min(t, 2)
        if wide:
            cols = slice(0, wide * LANES)
            along[:, cols] += width_scale * jnp.dot(
                back, gram[tile, cols], preferred_element_type=F32
            )
        for c in range(2, t):
            cols = slice(c * LANES, (c + 1) * LANES)
            row, side = lay.slots[t, c]
            along[:, cols] += width_scale * jnp.dot(
                back,
                gram[row * LANES : (row + 1) * LANES, side * LANES : (side + 1) * LANES],
                preferred_element_type=F32,
            )
        if odd:
            pair = gram[0:LANES, 0:LANES].astype(F32)
            if t % 2 == 1:
                pair = pltpu.roll(pair, lay.rank, 1)
            if t >= 2:
                pair = jnp.concatenate([pair[lay.rank :], pair[: lay.rank]], axis=0)
            along[:, tile] += width_scale * jnp.dot(
                back, pair.astype(BF16), preferred_element_type=F32
            )
    acted = acts[...]
    back_all = jnp.concatenate([backs[t] for t in range(lay.tiles)], axis=1)
    cross = contract_first(acted, back_all)
    before = lax.broadcasted_iota(jnp.int32, cross.shape, 0) // lay.rank
    after = lax.broadcasted_iota(jnp.int32, cross.shape, 1) // lay.rank
    cross = jnp.where(before < after, cross * width_scale, 0.0).astype(BF16)
    cot_all = c_ref[...].reshape(tokens, lay.share)
    grad_up = contract_first(acted, cot_all) + jnp.dot(
        cross, section_maps(lay, w_ref, 0), preferred_element_type=F32
    )
    grad_up = (grad_up * rank_scale).astype(BF16)
    for s in range(lay.pipe):
        for j in range(lay.per):
            out_ref[s * lay.per + j, lay.rank :, :] = grad_up[
                s * lay.rank : (s + 1) * lay.rank, j * LANES : (j + 1) * LANES
            ]
    mine, odd = index[0] // 2, index[0] % 2
    total = None
    for a in range(lay.y):
        rows = slice(a * lay.rows, (a + 1) * lay.rows)
        part = contract_first(backs[mine, rows, :], x_ref[a, :, 0 : lay.span])
        total = part if total is None else total + part
    held[...] = (total * width_scale).reshape(2, lay.rank, lay.span)
    grad_down = held[odd].astype(BF16)
    for b in range(lay.z):
        out_ref[b, 0 : lay.rank, :] = grad_down[:, b * LANES : (b + 1) * LANES]


def update_kernel(norm_limit, squares, grads, grad_up, master, moment1, moment2, *outs):
    new_master, new_moment1, new_moment2, new_weights = outs
    rank = grad_up.shape[0]
    square_sum = jnp.sum(jnp.sum(squares[...], axis=0), keepdims=True)
    clip_factor = jnp.minimum(1.0, norm_limit / jnp.sqrt(square_sum + NORM_EPS))
    for side, grad in enumerate((grads[0:rank, :], grad_up[...])):
        scaled = grad * clip_factor
        first = BETA_ONE * moment1[0, side] + (1.0 - BETA_ONE) * scaled
        second = BETA_TWO * moment2[0, side] + (1.0 - BETA_TWO) * scaled * scaled
        old = master[0, side]
        new = old - LEARN_RATE * (first / (jnp.sqrt(second) + ADAM_EPS) + DECAY_RATE * old)
        new_moment1[0, side] = first
        new_moment2[0, side] = second
        new_master[0, side] = new
        new_weights[0, side] = new.astype(BF16)


def body(saved_inputs, cotangent, weights_bf16, master, moment1, moment2, valid_rows):
    pipe, dp = lax.axis_size("pipe"), lax.axis_size("dp")
    inputs, weights = saved_inputs[0], weights_bf16[0]
    lay = Layout(pipe, dp, inputs.shape[0], inputs.shape[1], weights.shape[1])
    both = ("pipe", "dp")
    index = lax.axis_index("pipe").astype(jnp.int32).reshape(1)

    by_column = sort_columns(lay, valid_rows, inputs, cotangent)
    by_column = lax.all_to_all(by_column, "dp", 0, 0, axis_index_groups=lay.along_y)
    maps = lax.all_gather(weights, "dp", axis_index_groups=lay.along_z)
    cots, maps = lax.optimization_barrier((by_column[:, :, lay.span :], maps))
    cots = lax.ppermute(cots, both, lay.cotangent_turn())
    shared = lax.all_to_all(maps.reshape(pipe, lay.per, 2, lay.rank, LANES), "pipe", 0, 0)
    by_column, cots = lax.optimization_barrier((by_column, cots))
    pre_part = call(
        functools.partial(pre_kernel, lay),
        jax.ShapeDtypeStruct((lay.y, lay.rows, LANES), BF16),
        (index, maps, by_column),
        flops=PRE_WEIGHT * 2 * lay.y * lay.rows * lay.span * LANES,
    )
    message = lay.ranks + lay.gram + LANES
    parts = call(
        functools.partial(pack_kernel, lay),
        jax.ShapeDtypeStruct((lay.group, lay.piece, message), BF16),
        (index, shared, pre_part, cots),
        flops=4 * lay.y * lay.rows * lay.share * lay.ranks,
    )
    parts = lax.all_to_all(parts, both, 0, 0, axis_index_groups=lay.plane)
    reply = 2 * lay.ranks + lay.gram
    sums = call(
        functools.partial(sum_kernel, lay),
        jax.ShapeDtypeStruct((lay.group, lay.piece, reply), BF16),
        (index, parts),
    )
    sums = lax.all_to_all(sums, both, 0, 0, axis_index_groups=lay.plane)
    tokens = lay.y * lay.rows
    grads = call(
        functools.partial(chain_kernel, lay),
        jax.ShapeDtypeStruct((lay.z, 2 * lay.rank, LANES), BF16),
        (index, sums, shared, cots, by_column),
        scratch=(
            pltpu.VMEM((tokens, lay.ranks), F32),
            pltpu.VMEM((tokens, lay.ranks), F32),
            pltpu.VMEM((tokens, lay.ranks), BF16),
            pltpu.VMEM((lay.tiles, tokens, LANES), BF16),
            pltpu.VMEM((lay.ranks, lay.gram), BF16),
            pltpu.VMEM((2, lay.rank, lay.span), F32),
        ),
        flops=8 * tokens * lay.ranks * lay.share,
    )
    grads = lax.all_to_all(grads, "dp", 0, 0, axis_index_groups=lay.along_z)
    grads = jnp.sum(grads.astype(F32), axis=0)
    squares = jnp.sum((grads * grads).reshape(-1, 8, LANES), axis=0)
    grad_up = lax.ppermute(grads[lay.rank :], both, lay.gradient_home())
    squares = jnp.broadcast_to(squares, (lay.group, 8, LANES))
    squares = lax.all_to_all(squares, both, 0, 0, axis_index_groups=lay.plane)
    squares, grad_up = lax.optimization_barrier((jnp.sum(squares, axis=0), grad_up))
    squares = jnp.broadcast_to(squares, (lay.z, 8, LANES))
    squares = lax.all_to_all(squares, "dp", 0, 0, axis_index_groups=lay.along_z)
    norm_limit = CLIP_RMS * math.sqrt(2.0 * pipe * lay.rank * lay.width)
    state = jax.ShapeDtypeStruct(master.shape, F32)
    return pl.pallas_call(
        functools.partial(update_kernel, norm_limit),
        out_shape=(state, state, state, jax.ShapeDtypeStruct(master.shape, BF16)),
        in_specs=vmem_specs(6),
        out_specs=tuple(vmem_specs(4)),
        compiler_params=pltpu.CompilerParams(vmem_limit_bytes=8 * 1024 * 1024),
        cost_estimate=pl.CostEstimate(
            flops=0, bytes_accessed=30 * math.prod(master.shape), transcendentals=0
        ),
        interpret=INTERPRET,
    )(squares, grads, grad_up, master, moment1, moment2)


def solution(mesh):
    in_specs = (
        P("pipe", "dp", None),
        P("dp", "pipe"),
        P("pipe", None, None, "dp"),
        P("pipe", None, None, "dp"),
        P("pipe", None, None, "dp"),
        P("pipe", None, None, "dp"),
        P("dp"),
    )
    out_specs = (
        P("pipe", None, None, "dp"),
        P("pipe", None, None, "dp"),
        P("pipe", None, None, "dp"),
        P("pipe", None, None, "dp"),
    )
    return jax.shard_map(body, mesh=mesh, in_specs=in_specs, out_specs=out_specs, check_vma=False)
```

```python
import functools
import math

import jax
import jax.numpy as jnp
from jax import lax
from jax.experimental import pallas as pl
from jax.experimental.pallas import tpu as pltpu
from jax.sharding import PartitionSpec as P

BETA_ONE = 0.9
BETA_TWO = 0.95
LEARN_RATE = 0.05
DECAY_RATE = 0.1
ADAM_EPS = 1e-08
CLIP_RMS = 2.0
NORM_EPS = 1e-12

LANES = 128
Y_SIZE = 4
VMEM_LIMIT = 48 * 1024 * 1024
SORT_LIMIT = 63 * 1024 * 1024
PRE_WEIGHT = 12
INTERPRET = False
BF16 = jnp.bfloat16
F32 = jnp.float32


def contract_last(a, b):
    return lax.dot_general(a, b, (((1,), (1,)), ((), ())), preferred_element_type=F32)


def contract_first(a, b):
    return lax.dot_general(a, b, (((0,), (0,)), ((), ())), preferred_element_type=F32)


def vmem_specs(count):
    return [pl.BlockSpec(memory_space=pltpu.VMEM)] * count


def call(kernel, out_shape, operands, scratch=(), flops=0):
    size = sum(math.prod(a.shape) * a.dtype.itemsize for a in (*operands, out_shape))
    return pl.pallas_call(
        kernel,
        out_shape=out_shape,
        in_specs=[pl.BlockSpec(memory_space=pltpu.SMEM)] + vmem_specs(len(operands) - 1),
        out_specs=pl.BlockSpec(memory_space=pltpu.VMEM),
        scratch_shapes=list(scratch),
        compiler_params=pltpu.CompilerParams(vmem_limit_bytes=VMEM_LIMIT),
        cost_estimate=pl.CostEstimate(flops=flops, bytes_accessed=size, transcendentals=0),
        interpret=INTERPRET,
    )(*operands)


class Layout:
    def __init__(self, pipe, dp, rows, width, rank):
        self.pipe, self.dp, self.rows, self.width, self.rank = pipe, dp, rows, width, rank
        self.y = Y_SIZE if dp >= 64 else 2
        self.z = dp // self.y
        self.group = pipe * self.y
        self.span = width // self.y
        self.share = width // self.group
        self.per = self.z // pipe
        self.half = pipe // self.y
        self.piece = rows // pipe
        self.tiles = pipe * rank // LANES
        self.ranks = pipe * rank
        self.gram = 2 * LANES
        self.slots = {(a, b): (a, b) for a in range(1, self.tiles) for b in range(min(a, 2))}
        spare = [(a, 1) for a in range(1, self.tiles) if (a, 1) not in self.slots]
        rest = [(a, b) for a in range(1, self.tiles) for b in range(2, a)]
        self.slots.update(zip(rest, spare))
        y, z = self.y, self.z
        self.along_z = [[a * z + b for b in range(z)] for a in range(y)]
        self.along_y = [[a * z + b for a in range(y)] for b in range(z)]
        self.plane = [
            [p * dp + a * z + b for p in range(pipe) for a in range(y)] for b in range(z)
        ]

    def device(self, p, y, z):
        return p * self.dp + y * self.z + z

    def everywhere(self):
        return [(p, a, b) for p in range(self.pipe) for a in range(self.y) for b in range(self.z)]

    def cotangent_turn(self):
        return [
            (
                self.device(p, a, b),
                self.device(self.y * (p % self.half) + a, p // self.half, b),
            )
            for p, a, b in self.everywhere()
        ]

    def gradient_home(self):
        return [
            (
                self.device(p, a, b),
                self.device(b // self.per, a, p * self.per + b % self.per),
            )
            for p, a, b in self.everywhere()
        ]


def sort_kernel(lay, valid, x_ref, c_ref, out_ref, held, cots, sems):
    loads, stores = [], []
    fetch = pltpu.make_async_copy(c_ref, cots, sems.at[3 * lay.y])
    fetch.start()
    for a in range(lay.y):
        cols = pl.ds(a * lay.span, lay.span)
        loads.append(pltpu.make_async_copy(x_ref.at[:, cols], held.at[a], sems.at[a]))
        stores.append(
            pltpu.make_async_copy(
                held.at[a], out_ref.at[a, :, pl.ds(0, lay.span)], sems.at[lay.y + a]
            )
        )
        loads[a].start()
    fetch.wait()
    cot = cots[...]
    live = lax.broadcasted_iota(jnp.int32, cot.shape, 0) < valid[0]
    cots[...] = jnp.where(live, cot, jnp.zeros_like(cot))
    for a in range(lay.y):
        stores.append(
            pltpu.make_async_copy(
                cots.at[:, pl.ds(a * lay.share, lay.share)],
                out_ref.at[a, :, pl.ds(lay.span, lay.share)],
                sems.at[2 * lay.y + a],
            )
        )
        stores[lay.y + a].start()
    for a in range(lay.y):
        loads[a].wait()
        stores[a].start()
    for store in stores:
        store.wait()


def sort_columns(lay, valid_rows, inputs, cotangent):
    both = lay.span + lay.share
    return pl.pallas_call(
        functools.partial(sort_kernel, lay),
        out_shape=jax.ShapeDtypeStruct((lay.y, lay.rows, both), BF16),
        in_specs=[
            pl.BlockSpec(memory_space=pltpu.SMEM),
            pl.BlockSpec(memory_space=pltpu.HBM),
            pl.BlockSpec(memory_space=pltpu.HBM),
        ],
        out_specs=pl.BlockSpec(memory_space=pltpu.HBM),
        scratch_shapes=[
            pltpu.VMEM((lay.y, lay.rows, lay.span), BF16),
            pltpu.VMEM(cotangent.shape, BF16),
            pltpu.SemaphoreType.DMA((3 * lay.y + 1,)),
        ],
        compiler_params=pltpu.CompilerParams(vmem_limit_bytes=SORT_LIMIT),
        cost_estimate=pl.CostEstimate(
            flops=0, bytes_accessed=4 * lay.y * lay.rows * both, transcendentals=0
        ),
        interpret=INTERPRET,
    )(valid_rows, inputs, cotangent)


def pre_kernel(lay, index, w_ref, x_ref, out_ref):
    lower = index[0] % 2
    maps = jnp.concatenate(
        [jnp.concatenate([w_ref[b, lower], w_ref[b, 1 - lower]], axis=0) for b in range(lay.z)],
        axis=1,
    )
    for a in range(lay.y):
        out_ref[a] = contract_last(x_ref[a, :, 0 : lay.span], maps).astype(BF16)


def section_maps(lay, w_ref, which):
    return jnp.concatenate(
        [
            jnp.concatenate([w_ref[s, j, which] for j in range(lay.per)], axis=1)
            for s in range(lay.pipe)
        ],
        axis=0,
    )


def gram_tile(down, up, row, col):
    rows, cols = slice(row * LANES, (row + 1) * LANES), slice(col * LANES, (col + 1) * LANES)
    return contract_last(down[rows], up[cols]).astype(BF16)


def diagonal_tile(lay, down, up):
    rank = lay.rank
    lower = lax.broadcasted_iota(jnp.int32, (rank, LANES), 1) < rank
    blocks = []
    for t in range(lay.tiles):
        odd = down[t * LANES + rank : (t + 1) * LANES]
        block = contract_last(odd, up[t * LANES : (t + 1) * LANES])
        blocks.append(block if t % 2 == 0 else pltpu.roll(block, rank, 1))
    halves = [jnp.where(lower, blocks[t], blocks[t + 1]) for t in range(0, lay.tiles, 2)]
    if len(halves) == 1:
        halves.append(halves[0])
    return jnp.concatenate(halves[::-1], axis=0).astype(BF16)


def pack_kernel(lay, index, w_ref, pre_ref, c_ref, out_ref):
    down, up = section_maps(lay, w_ref, 0), section_maps(lay, w_ref, 1)
    gram_at, pre_at = lay.ranks, lay.ranks + lay.gram
    for a in range(lay.y):
        part = contract_last(c_ref[a], up).astype(BF16)
        for p in range(lay.pipe):
            rows = slice(p * lay.piece, (p + 1) * lay.piece)
            out_ref[p * lay.y + a, :, 0:gram_at] = part[rows]
            out_ref[p * lay.y + a, :, pre_at:] = pre_ref[a, rows, :]
    grams = {spot: gram_tile(down, up, *tile) for tile, spot in lay.slots.items()}
    grams[0, 0] = diagonal_tile(lay, down, up)
    each = lay.ranks // lay.group
    count = LANES // each
    for t in range(lay.tiles):
        for side in range(2):
            cols = slice(gram_at + side * LANES, gram_at + (side + 1) * LANES)
            tile = grams.get((t, side), jnp.zeros((LANES, LANES), BF16))
            for q in range(count):
                out_ref[t * count + q, :, cols] = tile[q * each : (q + 1) * each]


def sum_kernel(lay, index, r_ref, out_ref):
    gram_end = lay.ranks + lay.gram
    total = r_ref[0, :, 0:gram_end].astype(F32)
    for q in range(1, lay.group):
        total += r_ref[q, :, 0:gram_end].astype(F32)
    lower = lax.broadcasted_iota(jnp.int32, (lay.piece, LANES), 1) < lay.rank
    pres = []
    for s in range(lay.pipe):
        one = r_ref[s * lay.y, :, gram_end:].astype(F32)
        for a in range(1, lay.y):
            one += r_ref[s * lay.y + a, :, gram_end:].astype(F32)
        pres.append(one)
    cols = [total] + [jnp.where(lower, pres[2 * t], pres[2 * t + 1]) for t in range(lay.tiles)]
    message = jnp.concatenate(cols, axis=1).astype(BF16)
    for q in range(lay.group):
        out_ref[q] = message


def chain_kernel(lay, index, q_ref, w_ref, c_ref, x_ref, out_ref, *scratch):
    along, slope, acts, backs, gram, held = scratch
    width_scale, rank_scale = 1.0 / math.sqrt(lay.width), 1.0 / math.sqrt(lay.rank)
    gram_at, pre_at = lay.ranks, lay.ranks + lay.gram
    each = lay.ranks // lay.group
    for q in range(lay.group):
        p, a = q // lay.y, q % lay.y
        rows = slice(a * lay.rows + p * lay.piece, a * lay.rows + (p + 1) * lay.piece)
        along[rows, :] = q_ref[q, :, 0:gram_at].astype(F32)
        gram[q * each : (q + 1) * each, :] = q_ref[q, :, gram_at:pre_at]
        pre = q_ref[q, :, pre_at:].astype(F32) * width_scale
        gate = 1.0 / (1.0 + jnp.exp(-pre))
        acts[rows, :] = (pre * gate).astype(BF16)
        slope[rows, :] = gate * (1.0 + pre * (1.0 - gate)) * rank_scale
    tokens = lay.y * lay.rows
    lower = lax.broadcasted_iota(jnp.int32, (tokens, LANES), 1) < lay.rank
    for s in range(lay.pipe - 1, -1, -1):
        t, odd = s // 2, s % 2 == 1
        tile = slice(t * LANES, (t + 1) * LANES)
        back = along[:, tile] * slope[:, tile]
        back = jnp.where(lower != odd, back, 0.0).astype(BF16)
        if odd:
            backs[t] = back
        else:
            backs[t] = backs[t] + back
        if s == 0:
            continue
        wide = min(t, 2)
        if wide:
            cols = slice(0, wide * LANES)
            along[:, cols] += width_scale * jnp.dot(
                back, gram[tile, cols], preferred_element_type=F32
            )
        for c in range(2, t):
            cols = slice(c * LANES, (c + 1) * LANES)
            row, side = lay.slots[t, c]
            along[:, cols] += width_scale * jnp.dot(
                back,
                gram[row * LANES : (row + 1) * LANES, side * LANES : (side + 1) * LANES],
                preferred_element_type=F32,
            )
        if odd:
            pair = gram[0:LANES, 0:LANES].astype(F32)
            if t % 2 == 1:
                pair = pltpu.roll(pair, lay.rank, 1)
            if t >= 2:
                pair = jnp.concatenate([pair[lay.rank :], pair[: lay.rank]], axis=0)
            along[:, tile] += width_scale * jnp.dot(
                back, pair.astype(BF16), preferred_element_type=F32
            )
    acted = acts[...]
    back_all = jnp.concatenate([backs[t] for t in range(lay.tiles)], axis=1)
    cross = contract_first(acted, back_all)
    before = lax.broadcasted_iota(jnp.int32, cross.shape, 0) // lay.rank
    after = lax.broadcasted_iota(jnp.int32, cross.shape, 1) // lay.rank
    cross = jnp.where(before < after, cross * width_scale, 0.0).astype(BF16)
    cot_all = c_ref[...].reshape(tokens, lay.share)
    grad_up = contract_first(acted, cot_all) + jnp.dot(
        cross, section_maps(lay, w_ref, 0), preferred_element_type=F32
    )
    grad_up = (grad_up * rank_scale).astype(BF16)
    for s in range(lay.pipe):
        for j in range(lay.per):
            out_ref[s * lay.per + j, lay.rank :, :] = grad_up[
                s * lay.rank : (s + 1) * lay.rank, j * LANES : (j + 1) * LANES
            ]
    mine, odd = index[0] // 2, index[0] % 2
    total = None
    for a in range(lay.y):
        rows = slice(a * lay.rows, (a + 1) * lay.rows)
        part = contract_first(backs[mine, rows, :], x_ref[a, :, 0 : lay.span])
        total = part if total is None else total + part
    held[...] = (total * width_scale).reshape(2, lay.rank, lay.span)
    grad_down = held[odd].astype(BF16)
    for b in range(lay.z):
        out_ref[b, 0 : lay.rank, :] = grad_down[:, b * LANES : (b + 1) * LANES]


def update_kernel(norm_limit, squares, grads, grad_up, master, moment1, moment2, *outs):
    new_master, new_moment1, new_moment2, new_weights = outs
    rank = grad_up.shape[0]
    square_sum = jnp.sum(jnp.sum(squares[...], axis=0), keepdims=True)
    clip_factor = jnp.minimum(1.0, norm_limit / jnp.sqrt(square_sum + NORM_EPS))
    for side, grad in enumerate((grads[0:rank, :], grad_up[...])):
        scaled = grad * clip_factor
        first = BETA_ONE * moment1[0, side] + (1.0 - BETA_ONE) * scaled
        second = BETA_TWO * moment2[0, side] + (1.0 - BETA_TWO) * scaled * scaled
        old = master[0, side]
        new = old - LEARN_RATE * (first / (jnp.sqrt(second) + ADAM_EPS) + DECAY_RATE * old)
        new_moment1[0, side] = first
        new_moment2[0, side] = second
        new_master[0, side] = new
        new_weights[0, side] = new.astype(BF16)


def body(saved_inputs, cotangent, weights_bf16, master, moment1, moment2, valid_rows):
    pipe, dp = lax.axis_size("pipe"), lax.axis_size("dp")
    inputs, weights = saved_inputs[0], weights_bf16[0]
    lay = Layout(pipe, dp, inputs.shape[0], inputs.shape[1], weights.shape[1])
    both = ("pipe", "dp")
    index = lax.axis_index("pipe").astype(jnp.int32).reshape(1)

    by_column = sort_columns(lay, valid_rows, inputs, cotangent)
    by_column = lax.all_to_all(by_column, "dp", 0, 0, axis_index_groups=lay.along_y)
    maps = lax.all_gather(weights, "dp", axis_index_groups=lay.along_z)
    cots, maps = lax.optimization_barrier((by_column[:, :, lay.span :], maps))
    cots = lax.ppermute(cots, both, lay.cotangent_turn())
    shared = lax.all_to_all(maps.reshape(pipe, lay.per, 2, lay.rank, LANES), "pipe", 0, 0)
    by_column, cots = lax.optimization_barrier((by_column, cots))
    pre_part = call(
        functools.partial(pre_kernel, lay),
        jax.ShapeDtypeStruct((lay.y, lay.rows, LANES), BF16),
        (index, maps, by_column),
        flops=PRE_WEIGHT * 2 * lay.y * lay.rows * lay.span * LANES,
    )
    message = lay.ranks + lay.gram + LANES
    parts = call(
        functools.partial(pack_kernel, lay),
        jax.ShapeDtypeStruct((lay.group, lay.piece, message), BF16),
        (index, shared, pre_part, cots),
        flops=4 * lay.y * lay.rows * lay.share * lay.ranks,
    )
    parts = lax.all_to_all(parts, both, 0, 0, axis_index_groups=lay.plane)
    reply = 2 * lay.ranks + lay.gram
    sums = call(
        functools.partial(sum_kernel, lay),
        jax.ShapeDtypeStruct((lay.group, lay.piece, reply), BF16),
        (index, parts),
    )
    sums = lax.all_to_all(sums, both, 0, 0, axis_index_groups=lay.plane)
    tokens = lay.y * lay.rows
    grads = call(
        functools.partial(chain_kernel, lay),
        jax.ShapeDtypeStruct((lay.z, 2 * lay.rank, LANES), BF16),
        (index, sums, shared, cots, by_column),
        scratch=(
            pltpu.VMEM((tokens, lay.ranks), F32),
            pltpu.VMEM((tokens, lay.ranks), F32),
            pltpu.VMEM((tokens, lay.ranks), BF16),
            pltpu.VMEM((lay.tiles, tokens, LANES), BF16),
            pltpu.VMEM((lay.ranks, lay.gram), BF16),
            pltpu.VMEM((2, lay.rank, lay.span), F32),
        ),
        flops=8 * tokens * lay.ranks * lay.share,
    )
    grads = lax.all_to_all(grads, "dp", 0, 0, axis_index_groups=lay.along_z)
    grads = jnp.sum(grads.astype(F32), axis=0)
    squares = jnp.sum((grads * grads).reshape(-1, 8, LANES), axis=0)
    grad_up = lax.ppermute(grads[lay.rank :], both, lay.gradient_home())
    squares = jnp.broadcast_to(squares, (lay.z, 8, LANES))
    squares = lax.all_to_all(squares, "dp", 0, 0, axis_index_groups=lay.along_z)
    squares, grad_up = lax.optimization_barrier((jnp.sum(squares, axis=0), grad_up))
    squares = jnp.broadcast_to(squares, (lay.group, 8, LANES))
    squares = lax.all_to_all(squares, both, 0, 0, axis_index_groups=lay.plane)
    norm_limit = CLIP_RMS * math.sqrt(2.0 * pipe * lay.rank * lay.width)
    state = jax.ShapeDtypeStruct(master.shape, F32)
    return pl.pallas_call(
        functools.partial(update_kernel, norm_limit),
        out_shape=(state, state, state, jax.ShapeDtypeStruct(master.shape, BF16)),
        in_specs=vmem_specs(6),
        out_specs=tuple(vmem_specs(4)),
        compiler_params=pltpu.CompilerParams(vmem_limit_bytes=8 * 1024 * 1024),
        cost_estimate=pl.CostEstimate(
            flops=0, bytes_accessed=30 * math.prod(master.shape), transcendentals=0
        ),
        interpret=INTERPRET,
    )(squares, grads, grad_up, master, moment1, moment2)


def solution(mesh):
    in_specs = (
        P("pipe", "dp", None),
        P("dp", "pipe"),
        P("pipe", None, None, "dp"),
        P("pipe", None, None, "dp"),
        P("pipe", None, None, "dp"),
        P("pipe", None, None, "dp"),
        P("dp"),
    )
    out_specs = (
        P("pipe", None, None, "dp"),
        P("pipe", None, None, "dp"),
        P("pipe", None, None, "dp"),
        P("pipe", None, None, "dp"),
    )
    return jax.shard_map(body, mesh=mesh, in_specs=in_specs, out_specs=out_specs, check_vma=False)
```

```python
import functools
import math

import jax
import jax.numpy as jnp
from jax import lax
from jax.experimental import pallas as pl
from jax.experimental.pallas import tpu as pltpu
from jax.sharding import PartitionSpec as P

BETA_ONE = 0.9
BETA_TWO = 0.95
LEARN_RATE = 0.05
DECAY_RATE = 0.1
ADAM_EPS = 1e-08
CLIP_RMS = 2.0
NORM_EPS = 1e-12

LANES = 128
Y_SIZE = 4
VMEM_LIMIT = 48 * 1024 * 1024
SORT_LIMIT = 63 * 1024 * 1024
SMALL_LIMIT = 8 * 1024 * 1024
PRE_WEIGHT = 12
JOIN_WEIGHT = 1 << 34
INTERPRET = False
BF16 = jnp.bfloat16
F32 = jnp.float32


def contract_last(a, b):
    return lax.dot_general(a, b, (((1,), (1,)), ((), ())), preferred_element_type=F32)


def contract_first(a, b):
    return lax.dot_general(a, b, (((0,), (0,)), ((), ())), preferred_element_type=F32)


def vmem_specs(count):
    return [pl.BlockSpec(memory_space=pltpu.VMEM)] * count


def call(kernel, out_shape, operands, scratch=(), flops=0):
    size = sum(math.prod(a.shape) * a.dtype.itemsize for a in (*operands, out_shape))
    return pl.pallas_call(
        kernel,
        out_shape=out_shape,
        in_specs=[pl.BlockSpec(memory_space=pltpu.SMEM)] + vmem_specs(len(operands) - 1),
        out_specs=pl.BlockSpec(memory_space=pltpu.VMEM),
        scratch_shapes=list(scratch),
        compiler_params=pltpu.CompilerParams(vmem_limit_bytes=VMEM_LIMIT),
        cost_estimate=pl.CostEstimate(flops=flops, bytes_accessed=size, transcendentals=0),
        interpret=INTERPRET,
    )(*operands)


class Layout:
    def __init__(self, pipe, dp, rows, width, rank):
        self.pipe, self.dp, self.rows, self.width, self.rank = pipe, dp, rows, width, rank
        self.y = Y_SIZE if dp >= 64 else 2
        self.z = dp // self.y
        self.group = pipe * self.y
        self.span = width // self.y
        self.share = width // self.group
        self.per = self.z // pipe
        self.half = pipe // self.y
        self.piece = rows // pipe
        self.tiles = pipe * rank // LANES
        self.ranks = pipe * rank
        self.gram = 2 * LANES
        self.slots = {(a, b): (a, b) for a in range(1, self.tiles) for b in range(min(a, 2))}
        spare = [(a, 1) for a in range(1, self.tiles) if (a, 1) not in self.slots]
        rest = [(a, b) for a in range(1, self.tiles) for b in range(2, a)]
        self.slots.update(zip(rest, spare))
        y, z = self.y, self.z
        self.along_z = [[a * z + b for b in range(z)] for a in range(y)]
        self.along_y = [[a * z + b for a in range(y)] for b in range(z)]
        self.plane = [
            [p * dp + a * z + b for p in range(pipe) for a in range(y)] for b in range(z)
        ]

    def device(self, p, y, z):
        return p * self.dp + y * self.z + z

    def everywhere(self):
        return [(p, a, b) for p in range(self.pipe) for a in range(self.y) for b in range(self.z)]

    def cotangent_turn(self):
        return [
            (
                self.device(p, a, b),
                self.device(self.y * (p % self.half) + a, p // self.half, b),
            )
            for p, a, b in self.everywhere()
        ]

    def gradient_home(self):
        return [
            (
                self.device(p, a, b),
                self.device(b // self.per, a, p * self.per + b % self.per),
            )
            for p, a, b in self.everywhere()
        ]


def sort_kernel(lay, valid, x_ref, c_ref, out_ref, held, cots, sems):
    loads, stores = [], []
    fetch = pltpu.make_async_copy(c_ref, cots, sems.at[3 * lay.y])
    fetch.start()
    for a in range(lay.y):
        cols = pl.ds(a * lay.span, lay.span)
        loads.append(pltpu.make_async_copy(x_ref.at[:, cols], held.at[a], sems.at[a]))
        stores.append(
            pltpu.make_async_copy(
                held.at[a], out_ref.at[a, :, pl.ds(0, lay.span)], sems.at[lay.y + a]
            )
        )
        loads[a].start()
    fetch.wait()
    cot = cots[...]
    live = lax.broadcasted_iota(jnp.int32, cot.shape, 0) < valid[0]
    cots[...] = jnp.where(live, cot, jnp.zeros_like(cot))
    for a in range(lay.y):
        stores.append(
            pltpu.make_async_copy(
                cots.at[:, pl.ds(a * lay.share, lay.share)],
                out_ref.at[a, :, pl.ds(lay.span, lay.share)],
                sems.at[2 * lay.y + a],
            )
        )
        stores[lay.y + a].start()
    for a in range(lay.y):
        loads[a].wait()
        stores[a].start()
    for store in stores:
        store.wait()


def sort_columns(lay, valid_rows, inputs, cotangent):
    both = lay.span + lay.share
    return pl.pallas_call(
        functools.partial(sort_kernel, lay),
        out_shape=jax.ShapeDtypeStruct((lay.y, lay.rows, both), BF16),
        in_specs=[
            pl.BlockSpec(memory_space=pltpu.SMEM),
            pl.BlockSpec(memory_space=pltpu.HBM),
            pl.BlockSpec(memory_space=pltpu.HBM),
        ],
        out_specs=pl.BlockSpec(memory_space=pltpu.HBM),
        scratch_shapes=[
            pltpu.VMEM((lay.y, lay.rows, lay.span), BF16),
            pltpu.VMEM(cotangent.shape, BF16),
            pltpu.SemaphoreType.DMA((3 * lay.y + 1,)),
        ],
        compiler_params=pltpu.CompilerParams(vmem_limit_bytes=SORT_LIMIT),
        cost_estimate=pl.CostEstimate(
            flops=0, bytes_accessed=4 * lay.y * lay.rows * both, transcendentals=0
        ),
        interpret=INTERPRET,
    )(valid_rows, inputs, cotangent)


def pre_kernel(lay, index, w_ref, x_ref, out_ref):
    lower = index[0] % 2
    maps = jnp.concatenate(
        [jnp.concatenate([w_ref[b, lower], w_ref[b, 1 - lower]], axis=0) for b in range(lay.z)],
        axis=1,
    )
    for a in range(lay.y):
        out_ref[a] = contract_last(x_ref[a, :, 0 : lay.span], maps).astype(BF16)


def section_maps(lay, w_ref, which):
    return jnp.concatenate(
        [
            jnp.concatenate([w_ref[s, j, which] for j in range(lay.per)], axis=1)
            for s in range(lay.pipe)
        ],
        axis=0,
    )


def gram_tile(down, up, row, col):
    rows, cols = slice(row * LANES, (row + 1) * LANES), slice(col * LANES, (col + 1) * LANES)
    return contract_last(down[rows], up[cols]).astype(BF16)


def diagonal_tile(lay, down, up):
    rank = lay.rank
    lower = lax.broadcasted_iota(jnp.int32, (rank, LANES), 1) < rank
    blocks = []
    for t in range(lay.tiles):
        odd = down[t * LANES + rank : (t + 1) * LANES]
        block = contract_last(odd, up[t * LANES : (t + 1) * LANES])
        blocks.append(block if t % 2 == 0 else pltpu.roll(block, rank, 1))
    halves = [jnp.where(lower, blocks[t], blocks[t + 1]) for t in range(0, lay.tiles, 2)]
    if len(halves) == 1:
        halves.append(halves[0])
    return jnp.concatenate(halves[::-1], axis=0).astype(BF16)


def pack_kernel(lay, index, w_ref, pre_ref, c_ref, out_ref):
    down, up = section_maps(lay, w_ref, 0), section_maps(lay, w_ref, 1)
    gram_at, pre_at = lay.ranks, lay.ranks + lay.gram
    for a in range(lay.y):
        part = contract_last(c_ref[a], up).astype(BF16)
        for p in range(lay.pipe):
            rows = slice(p * lay.piece, (p + 1) * lay.piece)
            out_ref[p * lay.y + a, :, 0:gram_at] = part[rows]
            out_ref[p * lay.y + a, :, pre_at:] = pre_ref[a, rows, :]
    grams = {spot: gram_tile(down, up, *tile) for tile, spot in lay.slots.items()}
    grams[0, 0] = diagonal_tile(lay, down, up)
    each = lay.ranks // lay.group
    count = LANES // each
    for t in range(lay.tiles):
        for side in range(2):
            cols = slice(gram_at + side * LANES, gram_at + (side + 1) * LANES)
            tile = grams.get((t, side), jnp.zeros((LANES, LANES), BF16))
            for q in range(count):
                out_ref[t * count + q, :, cols] = tile[q * each : (q + 1) * each]


def sum_kernel(lay, index, r_ref, out_ref):
    gram_end = lay.ranks + lay.gram
    total = r_ref[0, :, 0:gram_end].astype(F32)
    for q in range(1, lay.group):
        total += r_ref[q, :, 0:gram_end].astype(F32)
    lower = lax.broadcasted_iota(jnp.int32, (lay.piece, LANES), 1) < lay.rank
    pres = []
    for s in range(lay.pipe):
        one = r_ref[s * lay.y, :, gram_end:].astype(F32)
        for a in range(1, lay.y):
            one += r_ref[s * lay.y + a, :, gram_end:].astype(F32)
        pres.append(one)
    cols = [total] + [jnp.where(lower, pres[2 * t], pres[2 * t + 1]) for t in range(lay.tiles)]
    message = jnp.concatenate(cols, axis=1).astype(BF16)
    for q in range(lay.group):
        out_ref[q] = message


def chain_kernel(lay, index, q_ref, w_ref, c_ref, x_ref, out_ref, *scratch):
    along, slope, acts, backs, gram, held = scratch
    width_scale, rank_scale = 1.0 / math.sqrt(lay.width), 1.0 / math.sqrt(lay.rank)
    gram_at, pre_at = lay.ranks, lay.ranks + lay.gram
    each = lay.ranks // lay.group
    for q in range(lay.group):
        p, a = q // lay.y, q % lay.y
        rows = slice(a * lay.rows + p * lay.piece, a * lay.rows + (p + 1) * lay.piece)
        along[rows, :] = q_ref[q, :, 0:gram_at].astype(F32)
        gram[q * each : (q + 1) * each, :] = q_ref[q, :, gram_at:pre_at]
        pre = q_ref[q, :, pre_at:].astype(F32) * width_scale
        gate = 1.0 / (1.0 + jnp.exp(-pre))
        acts[rows, :] = (pre * gate).astype(BF16)
        slope[rows, :] = gate * (1.0 + pre * (1.0 - gate)) * rank_scale
    tokens = lay.y * lay.rows
    lower = lax.broadcasted_iota(jnp.int32, (tokens, LANES), 1) < lay.rank
    for s in range(lay.pipe - 1, -1, -1):
        t, odd = s // 2, s % 2 == 1
        tile = slice(t * LANES, (t + 1) * LANES)
        back = along[:, tile] * slope[:, tile]
        back = jnp.where(lower != odd, back, 0.0).astype(BF16)
        if odd:
            backs[t] = back
        else:
            backs[t] = backs[t] + back
        if s == 0:
            continue
        wide = min(t, 2)
        if wide:
            cols = slice(0, wide * LANES)
            along[:, cols] += width_scale * jnp.dot(
                back, gram[tile, cols], preferred_element_type=F32
            )
        for c in range(2, t):
            cols = slice(c * LANES, (c + 1) * LANES)
            row, side = lay.slots[t, c]
            along[:, cols] += width_scale * jnp.dot(
                back,
                gram[row * LANES : (row + 1) * LANES, side * LANES : (side + 1) * LANES],
                preferred_element_type=F32,
            )
        if odd:
            pair = gram[0:LANES, 0:LANES].astype(F32)
            if t % 2 == 1:
                pair = pltpu.roll(pair, lay.rank, 1)
            if t >= 2:
                pair = jnp.concatenate([pair[lay.rank :], pair[: lay.rank]], axis=0)
            along[:, tile] += width_scale * jnp.dot(
                back, pair.astype(BF16), preferred_element_type=F32
            )
    acted = acts[...]
    back_all = jnp.concatenate([backs[t] for t in range(lay.tiles)], axis=1)
    cross = contract_first(acted, back_all)
    before = lax.broadcasted_iota(jnp.int32, cross.shape, 0) // lay.rank
    after = lax.broadcasted_iota(jnp.int32, cross.shape, 1) // lay.rank
    cross = jnp.where(before < after, cross * width_scale, 0.0).astype(BF16)
    cot_all = c_ref[...].reshape(tokens, lay.share)
    grad_up = contract_first(acted, cot_all) + jnp.dot(
        cross, section_maps(lay, w_ref, 0), preferred_element_type=F32
    )
    grad_up = (grad_up * rank_scale).astype(BF16)
    for s in range(lay.pipe):
        for j in range(lay.per):
            out_ref[s * lay.per + j, lay.rank :, :] = grad_up[
                s * lay.rank : (s + 1) * lay.rank, j * LANES : (j + 1) * LANES
            ]
    mine, odd = index[0] // 2, index[0] % 2
    total = None
    for a in range(lay.y):
        rows = slice(a * lay.rows, (a + 1) * lay.rows)
        part = contract_first(backs[mine, rows, :], x_ref[a, :, 0 : lay.span])
        total = part if total is None else total + part
    held[...] = (total * width_scale).reshape(2, lay.rank, lay.span)
    grad_down = held[odd].astype(BF16)
    for b in range(lay.z):
        out_ref[b, 0 : lay.rank, :] = grad_down[:, b * LANES : (b + 1) * LANES]


def join_kernel(grads, grad_up, out_ref):
    out_ref[0] = grads[0 : grad_up.shape[0], :]
    out_ref[1] = grad_up[...]


def update_kernel(norm_limit, squares, grads, master, moment1, moment2, *outs):
    new_master, new_moment1, new_moment2, new_weights = outs
    square_sum = jnp.sum(jnp.sum(squares[...], axis=0), keepdims=True)
    clip_factor = jnp.minimum(1.0, norm_limit / jnp.sqrt(square_sum + NORM_EPS))
    for side in range(2):
        scaled = grads[side] * clip_factor
        first = BETA_ONE * moment1[0, side] + (1.0 - BETA_ONE) * scaled
        second = BETA_TWO * moment2[0, side] + (1.0 - BETA_TWO) * scaled * scaled
        old = master[0, side]
        new = old - LEARN_RATE * (first / (jnp.sqrt(second) + ADAM_EPS) + DECAY_RATE * old)
        new_moment1[0, side] = first
        new_moment2[0, side] = second
        new_master[0, side] = new
        new_weights[0, side] = new.astype(BF16)


def body(saved_inputs, cotangent, weights_bf16, master, moment1, moment2, valid_rows):
    pipe, dp = lax.axis_size("pipe"), lax.axis_size("dp")
    inputs, weights = saved_inputs[0], weights_bf16[0]
    lay = Layout(pipe, dp, inputs.shape[0], inputs.shape[1], weights.shape[1])
    both = ("pipe", "dp")
    index = lax.axis_index("pipe").astype(jnp.int32).reshape(1)

    by_column = sort_columns(lay, valid_rows, inputs, cotangent)
    by_column = lax.all_to_all(by_column, "dp", 0, 0, axis_index_groups=lay.along_y)
    maps = lax.all_gather(weights, "dp", axis_index_groups=lay.along_z)
    cots, maps = lax.optimization_barrier((by_column[:, :, lay.span :], maps))
    cots = lax.ppermute(cots, both, lay.cotangent_turn())
    shared = lax.all_to_all(maps.reshape(pipe, lay.per, 2, lay.rank, LANES), "pipe", 0, 0)
    by_column, cots = lax.optimization_barrier((by_column, cots))
    pre_part = call(
        functools.partial(pre_kernel, lay),
        jax.ShapeDtypeStruct((lay.y, lay.rows, LANES), BF16),
        (index, maps, by_column),
        flops=PRE_WEIGHT * 2 * lay.y * lay.rows * lay.span * LANES,
    )
    message = lay.ranks + lay.gram + LANES
    parts = call(
        functools.partial(pack_kernel, lay),
        jax.ShapeDtypeStruct((lay.group, lay.piece, message), BF16),
        (index, shared, pre_part, cots),
        flops=4 * lay.y * lay.rows * lay.share * lay.ranks,
    )
    parts = lax.all_to_all(parts, both, 0, 0, axis_index_groups=lay.plane)
    reply = 2 * lay.ranks + lay.gram
    sums = call(
        functools.partial(sum_kernel, lay),
        jax.ShapeDtypeStruct((lay.group, lay.piece, reply), BF16),
        (index, parts),
    )
    sums = lax.all_to_all(sums, both, 0, 0, axis_index_groups=lay.plane)
    tokens = lay.y * lay.rows
    grads = call(
        functools.partial(chain_kernel, lay),
        jax.ShapeDtypeStruct((lay.z, 2 * lay.rank, LANES), BF16),
        (index, sums, shared, cots, by_column),
        scratch=(
            pltpu.VMEM((tokens, lay.ranks), F32),
            pltpu.VMEM((tokens, lay.ranks), F32),
            pltpu.VMEM((tokens, lay.ranks), BF16),
            pltpu.VMEM((lay.tiles, tokens, LANES), BF16),
            pltpu.VMEM((lay.ranks, lay.gram), BF16),
            pltpu.VMEM((2, lay.rank, lay.span), F32),
        ),
        flops=8 * tokens * lay.ranks * lay.share,
    )
    grads = lax.all_to_all(grads, "dp", 0, 0, axis_index_groups=lay.along_z)
    grads = jnp.sum(grads.astype(F32), axis=0)
    squares = jnp.sum((grads * grads).reshape(-1, 8, LANES), axis=0)
    grad_up = lax.ppermute(grads[lay.rank :], both, lay.gradient_home())
    joined = pl.pallas_call(
        join_kernel,
        out_shape=jax.ShapeDtypeStruct((2, lay.rank, LANES), F32),
        in_specs=vmem_specs(2),
        out_specs=vmem_specs(1)[0],
        compiler_params=pltpu.CompilerParams(vmem_limit_bytes=SMALL_LIMIT),
        cost_estimate=pl.CostEstimate(flops=JOIN_WEIGHT, bytes_accessed=0, transcendentals=0),
        interpret=INTERPRET,
    )(grads, grad_up)
    squares = jnp.broadcast_to(squares, (lay.group, 8, LANES))
    squares = lax.all_to_all(squares, both, 0, 0, axis_index_groups=lay.plane)
    squares = jnp.broadcast_to(jnp.sum(squares, axis=0), (lay.z, 8, LANES))
    squares = lax.all_to_all(squares, "dp", 0, 0, axis_index_groups=lay.along_z)
    norm_limit = CLIP_RMS * math.sqrt(2.0 * pipe * lay.rank * lay.width)
    state = jax.ShapeDtypeStruct(master.shape, F32)
    return pl.pallas_call(
        functools.partial(update_kernel, norm_limit),
        out_shape=(state, state, state, jax.ShapeDtypeStruct(master.shape, BF16)),
        in_specs=vmem_specs(5),
        out_specs=tuple(vmem_specs(4)),
        compiler_params=pltpu.CompilerParams(vmem_limit_bytes=SMALL_LIMIT),
        cost_estimate=pl.CostEstimate(
            flops=0, bytes_accessed=30 * math.prod(master.shape), transcendentals=0
        ),
        interpret=INTERPRET,
    )(squares, joined, master, moment1, moment2)


def solution(mesh):
    in_specs = (
        P("pipe", "dp", None),
        P("dp", "pipe"),
        P("pipe", None, None, "dp"),
        P("pipe", None, None, "dp"),
        P("pipe", None, None, "dp"),
        P("pipe", None, None, "dp"),
        P("dp"),
    )
    out_specs = (
        P("pipe", None, None, "dp"),
        P("pipe", None, None, "dp"),
        P("pipe", None, None, "dp"),
        P("pipe", None, None, "dp"),
    )
    return jax.shard_map(body, mesh=mesh, in_specs=in_specs, out_specs=out_specs, check_vma=False)
```

```python
import functools
import math

import jax
import jax.numpy as jnp
from jax import lax
from jax.experimental import pallas as pl
from jax.experimental.pallas import tpu as pltpu
from jax.sharding import PartitionSpec as P

BETA_ONE = 0.9
BETA_TWO = 0.95
LEARN_RATE = 0.05
DECAY_RATE = 0.1
ADAM_EPS = 1e-08
CLIP_RMS = 2.0
NORM_EPS = 1e-12

LANES = 128
Y_SIZE = 4
VMEM_LIMIT = 48 * 1024 * 1024
SORT_LIMIT = 63 * 1024 * 1024
SMALL_LIMIT = 8 * 1024 * 1024
PRE_WEIGHT = 12
JOIN_WEIGHT = 1 << 34
INTERPRET = False
BF16 = jnp.bfloat16
F32 = jnp.float32


def contract_last(a, b):
    return lax.dot_general(a, b, (((1,), (1,)), ((), ())), preferred_element_type=F32)


def contract_first(a, b):
    return lax.dot_general(a, b, (((0,), (0,)), ((), ())), preferred_element_type=F32)


def vmem_specs(count):
    return [pl.BlockSpec(memory_space=pltpu.VMEM)] * count


def call(kernel, out_shape, operands, scratch=(), flops=0):
    size = sum(math.prod(a.shape) * a.dtype.itemsize for a in (*operands, out_shape))
    return pl.pallas_call(
        kernel,
        out_shape=out_shape,
        in_specs=[pl.BlockSpec(memory_space=pltpu.SMEM)] + vmem_specs(len(operands) - 1),
        out_specs=pl.BlockSpec(memory_space=pltpu.VMEM),
        scratch_shapes=list(scratch),
        compiler_params=pltpu.CompilerParams(vmem_limit_bytes=VMEM_LIMIT),
        cost_estimate=pl.CostEstimate(flops=flops, bytes_accessed=size, transcendentals=0),
        interpret=INTERPRET,
    )(*operands)


class Layout:
    def __init__(self, pipe, dp, rows, width, rank):
        self.pipe, self.dp, self.rows, self.width, self.rank = pipe, dp, rows, width, rank
        self.y = Y_SIZE if dp >= 64 else 2
        self.z = dp // self.y
        self.group = pipe * self.y
        self.span = width // self.y
        self.share = width // self.group
        self.per = self.z // pipe
        self.half = pipe // self.y
        self.piece = rows // pipe
        self.tiles = pipe * rank // LANES
        self.ranks = pipe * rank
        self.gram = 2 * LANES
        self.slots = {(a, b): (a, b) for a in range(1, self.tiles) for b in range(min(a, 2))}
        spare = [(a, 1) for a in range(1, self.tiles) if (a, 1) not in self.slots]
        rest = [(a, b) for a in range(1, self.tiles) for b in range(2, a)]
        self.slots.update(zip(rest, spare))
        y, z = self.y, self.z
        self.along_z = [[a * z + b for b in range(z)] for a in range(y)]
        self.along_y = [[a * z + b for a in range(y)] for b in range(z)]
        self.plane = [
            [p * dp + a * z + b for p in range(pipe) for a in range(y)] for b in range(z)
        ]

    def device(self, p, y, z):
        return p * self.dp + y * self.z + z

    def everywhere(self):
        return [(p, a, b) for p in range(self.pipe) for a in range(self.y) for b in range(self.z)]

    def cotangent_turn(self):
        return [
            (
                self.device(p, a, b),
                self.device(self.y * (p % self.half) + a, p // self.half, b),
            )
            for p, a, b in self.everywhere()
        ]

    def gradient_home(self):
        return [
            (
                self.device(p, a, b),
                self.device(b // self.per, a, p * self.per + b % self.per),
            )
            for p, a, b in self.everywhere()
        ]


def sort_kernel(lay, valid, x_ref, c_ref, out_ref, held, cots, sems):
    loads, stores = [], []
    fetch = pltpu.make_async_copy(c_ref, cots, sems.at[3 * lay.y])
    fetch.start()
    for a in range(lay.y):
        cols = pl.ds(a * lay.span, lay.span)
        loads.append(pltpu.make_async_copy(x_ref.at[:, cols], held.at[a], sems.at[a]))
        stores.append(
            pltpu.make_async_copy(
                held.at[a], out_ref.at[a, :, pl.ds(0, lay.span)], sems.at[lay.y + a]
            )
        )
        loads[a].start()
    fetch.wait()
    cot = cots[...]
    live = lax.broadcasted_iota(jnp.int32, cot.shape, 0) < valid[0]
    cots[...] = jnp.where(live, cot, jnp.zeros_like(cot))
    for a in range(lay.y):
        stores.append(
            pltpu.make_async_copy(
                cots.at[:, pl.ds(a * lay.share, lay.share)],
                out_ref.at[a, :, pl.ds(lay.span, lay.share)],
                sems.at[2 * lay.y + a],
            )
        )
        stores[lay.y + a].start()
    for a in range(lay.y):
        loads[a].wait()
        stores[a].start()
    for store in stores:
        store.wait()


def sort_columns(lay, valid_rows, inputs, cotangent):
    both = lay.span + lay.share
    return pl.pallas_call(
        functools.partial(sort_kernel, lay),
        out_shape=jax.ShapeDtypeStruct((lay.y, lay.rows, both), BF16),
        in_specs=[
            pl.BlockSpec(memory_space=pltpu.SMEM),
            pl.BlockSpec(memory_space=pltpu.HBM),
            pl.BlockSpec(memory_space=pltpu.HBM),
        ],
        out_specs=pl.BlockSpec(memory_space=pltpu.HBM),
        scratch_shapes=[
            pltpu.VMEM((lay.y, lay.rows, lay.span), BF16),
            pltpu.VMEM(cotangent.shape, BF16),
            pltpu.SemaphoreType.DMA((3 * lay.y + 1,)),
        ],
        compiler_params=pltpu.CompilerParams(vmem_limit_bytes=SORT_LIMIT),
        cost_estimate=pl.CostEstimate(
            flops=0, bytes_accessed=4 * lay.y * lay.rows * both, transcendentals=0
        ),
        interpret=INTERPRET,
    )(valid_rows, inputs, cotangent)


def pre_kernel(lay, index, w_ref, x_ref, out_ref):
    lower = index[0] % 2
    maps = jnp.concatenate(
        [jnp.concatenate([w_ref[b, lower], w_ref[b, 1 - lower]], axis=0) for b in range(lay.z)],
        axis=1,
    )
    for a in range(lay.y):
        out_ref[a] = contract_last(x_ref[a, :, 0 : lay.span], maps).astype(BF16)


def section_maps(lay, w_ref, which):
    return jnp.concatenate(
        [
            jnp.concatenate([w_ref[s, j, which] for j in range(lay.per)], axis=1)
            for s in range(lay.pipe)
        ],
        axis=0,
    )


def gram_tile(down, up, row, col):
    rows, cols = slice(row * LANES, (row + 1) * LANES), slice(col * LANES, (col + 1) * LANES)
    return contract_last(down[rows], up[cols]).astype(BF16)


def diagonal_tile(lay, down, up):
    rank = lay.rank
    lower = lax.broadcasted_iota(jnp.int32, (rank, LANES), 1) < rank
    blocks = []
    for t in range(lay.tiles):
        odd = down[t * LANES + rank : (t + 1) * LANES]
        block = contract_last(odd, up[t * LANES : (t + 1) * LANES])
        blocks.append(block if t % 2 == 0 else pltpu.roll(block, rank, 1))
    halves = [jnp.where(lower, blocks[t], blocks[t + 1]) for t in range(0, lay.tiles, 2)]
    if len(halves) == 1:
        halves.append(halves[0])
    return jnp.concatenate(halves[::-1], axis=0).astype(BF16)


def pack_kernel(lay, index, w_ref, pre_ref, c_ref, out_ref):
    down, up = section_maps(lay, w_ref, 0), section_maps(lay, w_ref, 1)
    gram_at, pre_at = lay.ranks, lay.ranks + lay.gram
    for a in range(lay.y):
        part = contract_last(c_ref[a], up).astype(BF16)
        for p in range(lay.pipe):
            rows = slice(p * lay.piece, (p + 1) * lay.piece)
            out_ref[p * lay.y + a, :, 0:gram_at] = part[rows]
            out_ref[p * lay.y + a, :, pre_at:] = pre_ref[a, rows, :]
    grams = {spot: gram_tile(down, up, *tile) for tile, spot in lay.slots.items()}
    grams[0, 0] = diagonal_tile(lay, down, up)
    each = lay.ranks // lay.group
    count = LANES // each
    for t in range(lay.tiles):
        for side in range(2):
            cols = slice(gram_at + side * LANES, gram_at + (side + 1) * LANES)
            tile = grams.get((t, side), jnp.zeros((LANES, LANES), BF16))
            for q in range(count):
                out_ref[t * count + q, :, cols] = tile[q * each : (q + 1) * each]


def sum_kernel(lay, index, r_ref, out_ref):
    gram_end = lay.ranks + lay.gram
    total = r_ref[0, :, 0:gram_end].astype(F32)
    for q in range(1, lay.group):
        total += r_ref[q, :, 0:gram_end].astype(F32)
    lower = lax.broadcasted_iota(jnp.int32, (lay.piece, LANES), 1) < lay.rank
    pres = []
    for s in range(lay.pipe):
        one = r_ref[s * lay.y, :, gram_end:].astype(F32)
        for a in range(1, lay.y):
            one += r_ref[s * lay.y + a, :, gram_end:].astype(F32)
        pres.append(one)
    cols = [total] + [jnp.where(lower, pres[2 * t], pres[2 * t + 1]) for t in range(lay.tiles)]
    message = jnp.concatenate(cols, axis=1).astype(BF16)
    for q in range(lay.group):
        out_ref[q] = message


def chain_kernel(lay, index, q_ref, w_ref, c_ref, x_ref, out_ref, *scratch):
    along, slope, acts, backs, gram, held = scratch
    width_scale, rank_scale = 1.0 / math.sqrt(lay.width), 1.0 / math.sqrt(lay.rank)
    gram_at, pre_at = lay.ranks, lay.ranks + lay.gram
    each = lay.ranks // lay.group
    for q in range(lay.group):
        p, a = q // lay.y, q % lay.y
        rows = slice(a * lay.rows + p * lay.piece, a * lay.rows + (p + 1) * lay.piece)
        along[rows, :] = q_ref[q, :, 0:gram_at].astype(F32)
        gram[q * each : (q + 1) * each, :] = q_ref[q, :, gram_at:pre_at]
        pre = q_ref[q, :, pre_at:].astype(F32) * width_scale
        gate = 1.0 / (1.0 + jnp.exp(-pre))
        acts[rows, :] = (pre * gate).astype(BF16)
        slope[rows, :] = gate * (1.0 + pre * (1.0 - gate)) * rank_scale
    tokens = lay.y * lay.rows
    lower = lax.broadcasted_iota(jnp.int32, (tokens, LANES), 1) < lay.rank
    for s in range(lay.pipe - 1, -1, -1):
        t, odd = s // 2, s % 2 == 1
        tile = slice(t * LANES, (t + 1) * LANES)
        back = along[:, tile] * slope[:, tile]
        back = jnp.where(lower != odd, back, 0.0).astype(BF16)
        if odd:
            backs[t] = back
        else:
            backs[t] = backs[t] + back
        if s == 0:
            continue
        wide = min(t, 2)
        if wide:
            cols = slice(0, wide * LANES)
            along[:, cols] += width_scale * jnp.dot(
                back, gram[tile, cols], preferred_element_type=F32
            )
        for c in range(2, t):
            cols = slice(c * LANES, (c + 1) * LANES)
            row, side = lay.slots[t, c]
            along[:, cols] += width_scale * jnp.dot(
                back,
                gram[row * LANES : (row + 1) * LANES, side * LANES : (side + 1) * LANES],
                preferred_element_type=F32,
            )
        if odd:
            pair = gram[0:LANES, 0:LANES].astype(F32)
            if t % 2 == 1:
                pair = pltpu.roll(pair, lay.rank, 1)
            if t >= 2:
                pair = jnp.concatenate([pair[lay.rank :], pair[: lay.rank]], axis=0)
            along[:, tile] += width_scale * jnp.dot(
                back, pair.astype(BF16), preferred_element_type=F32
            )
    acted = acts[...]
    back_all = jnp.concatenate([backs[t] for t in range(lay.tiles)], axis=1)
    cross = contract_first(acted, back_all)
    before = lax.broadcasted_iota(jnp.int32, cross.shape, 0) // lay.rank
    after = lax.broadcasted_iota(jnp.int32, cross.shape, 1) // lay.rank
    cross = jnp.where(before < after, cross * width_scale, 0.0).astype(BF16)
    cot_all = c_ref[...].reshape(tokens, lay.share)
    grad_up = contract_first(acted, cot_all) + jnp.dot(
        cross, section_maps(lay, w_ref, 0), preferred_element_type=F32
    )
    grad_up = (grad_up * rank_scale).astype(BF16)
    for s in range(lay.pipe):
        for j in range(lay.per):
            out_ref[s * lay.per + j, lay.rank :, :] = grad_up[
                s * lay.rank : (s + 1) * lay.rank, j * LANES : (j + 1) * LANES
            ]
    mine, odd = index[0] // 2, index[0] % 2
    total = None
    for a in range(lay.y):
        rows = slice(a * lay.rows, (a + 1) * lay.rows)
        part = contract_first(backs[mine, rows, :], x_ref[a, :, 0 : lay.span])
        total = part if total is None else total + part
    held[...] = (total * width_scale).reshape(2, lay.rank, lay.span)
    grad_down = held[odd].astype(BF16)
    for b in range(lay.z):
        out_ref[b, 0 : lay.rank, :] = grad_down[:, b * LANES : (b + 1) * LANES]


def join_kernel(grads, grad_up, out_ref):
    out_ref[0] = grads[0 : grad_up.shape[0], :]
    out_ref[1] = grad_up[...]


def update_kernel(norm_limit, squares, grads, master, moment1, moment2, *outs):
    new_master, new_moment1, new_moment2, new_weights = outs
    square_sum = jnp.sum(jnp.sum(squares[...], axis=0), keepdims=True)
    clip_factor = jnp.minimum(1.0, norm_limit / jnp.sqrt(square_sum + NORM_EPS))
    for side in range(2):
        scaled = grads[side] * clip_factor
        first = BETA_ONE * moment1[0, side] + (1.0 - BETA_ONE) * scaled
        second = BETA_TWO * moment2[0, side] + (1.0 - BETA_TWO) * scaled * scaled
        old = master[0, side]
        new = old - LEARN_RATE * (first / (jnp.sqrt(second) + ADAM_EPS) + DECAY_RATE * old)
        new_moment1[0, side] = first
        new_moment2[0, side] = second
        new_master[0, side] = new
        new_weights[0, side] = new.astype(BF16)


def body(saved_inputs, cotangent, weights_bf16, master, moment1, moment2, valid_rows):
    pipe, dp = lax.axis_size("pipe"), lax.axis_size("dp")
    inputs, weights = saved_inputs[0], weights_bf16[0]
    lay = Layout(pipe, dp, inputs.shape[0], inputs.shape[1], weights.shape[1])
    both = ("pipe", "dp")
    index = lax.axis_index("pipe").astype(jnp.int32).reshape(1)

    by_column = sort_columns(lay, valid_rows, inputs, cotangent)
    by_column = lax.all_to_all(by_column, "dp", 0, 0, axis_index_groups=lay.along_y)
    maps = lax.all_gather(weights, "dp", axis_index_groups=lay.along_z)
    cots, maps = lax.optimization_barrier((by_column[:, :, lay.span :], maps))
    cots = lax.ppermute(cots, both, lay.cotangent_turn())
    shared = lax.all_to_all(maps.reshape(pipe, lay.per, 2, lay.rank, LANES), "pipe", 0, 0)
    by_column, cots = lax.optimization_barrier((by_column, cots))
    pre_part = call(
        functools.partial(pre_kernel, lay),
        jax.ShapeDtypeStruct((lay.y, lay.rows, LANES), BF16),
        (index, maps, by_column),
        flops=PRE_WEIGHT * 2 * lay.y * lay.rows * lay.span * LANES,
    )
    message = lay.ranks + lay.gram + LANES
    parts = call(
        functools.partial(pack_kernel, lay),
        jax.ShapeDtypeStruct((lay.group, lay.piece, message), BF16),
        (index, shared, pre_part, cots),
        flops=4 * lay.y * lay.rows * lay.share * lay.ranks,
    )
    parts = lax.all_to_all(parts, both, 0, 0, axis_index_groups=lay.plane)
    reply = 2 * lay.ranks + lay.gram
    sums = call(
        functools.partial(sum_kernel, lay),
        jax.ShapeDtypeStruct((lay.group, lay.piece, reply), BF16),
        (index, parts),
    )
    sums = lax.all_to_all(sums, both, 0, 0, axis_index_groups=lay.plane)
    tokens = lay.y * lay.rows
    grads = call(
        functools.partial(chain_kernel, lay),
        jax.ShapeDtypeStruct((lay.z, 2 * lay.rank, LANES), BF16),
        (index, sums, shared, cots, by_column),
        scratch=(
            pltpu.VMEM((tokens, lay.ranks), F32),
            pltpu.VMEM((tokens, lay.ranks), F32),
            pltpu.VMEM((tokens, lay.ranks), BF16),
            pltpu.VMEM((lay.tiles, tokens, LANES), BF16),
            pltpu.VMEM((lay.ranks, lay.gram), BF16),
            pltpu.VMEM((2, lay.rank, lay.span), F32),
        ),
        flops=8 * tokens * lay.ranks * lay.share,
    )
    grads = lax.all_to_all(grads, "dp", 0, 0, axis_index_groups=lay.along_z)
    grads = jnp.sum(grads.astype(F32), axis=0)
    squares = jnp.sum(grads * grads, axis=0, keepdims=True)
    grad_up = lax.ppermute(grads[lay.rank :], both, lay.gradient_home())
    joined = pl.pallas_call(
        join_kernel,
        out_shape=jax.ShapeDtypeStruct((2, lay.rank, LANES), F32),
        in_specs=vmem_specs(2),
        out_specs=vmem_specs(1)[0],
        compiler_params=pltpu.CompilerParams(vmem_limit_bytes=SMALL_LIMIT),
        cost_estimate=pl.CostEstimate(flops=JOIN_WEIGHT, bytes_accessed=0, transcendentals=0),
        interpret=INTERPRET,
    )(grads, grad_up)
    squares = jnp.broadcast_to(squares, (lay.group, 1, LANES))
    squares = lax.all_to_all(squares, both, 0, 0, axis_index_groups=lay.plane)
    squares = jnp.broadcast_to(jnp.sum(squares, axis=0), (lay.z, 1, LANES))
    squares = lax.all_to_all(squares, "dp", 0, 0, axis_index_groups=lay.along_z)
    norm_limit = CLIP_RMS * math.sqrt(2.0 * pipe * lay.rank * lay.width)
    state = jax.ShapeDtypeStruct(master.shape, F32)
    return pl.pallas_call(
        functools.partial(update_kernel, norm_limit),
        out_shape=(state, state, state, jax.ShapeDtypeStruct(master.shape, BF16)),
        in_specs=vmem_specs(5),
        out_specs=tuple(vmem_specs(4)),
        compiler_params=pltpu.CompilerParams(vmem_limit_bytes=SMALL_LIMIT),
        cost_estimate=pl.CostEstimate(
            flops=0, bytes_accessed=30 * math.prod(master.shape), transcendentals=0
        ),
        interpret=INTERPRET,
    )(squares, joined, master, moment1, moment2)


def solution(mesh):
    in_specs = (
        P("pipe", "dp", None),
        P("dp", "pipe"),
        P("pipe", None, None, "dp"),
        P("pipe", None, None, "dp"),
        P("pipe", None, None, "dp"),
        P("pipe", None, None, "dp"),
        P("dp"),
    )
    out_specs = (
        P("pipe", None, None, "dp"),
        P("pipe", None, None, "dp"),
        P("pipe", None, None, "dp"),
        P("pipe", None, None, "dp"),
    )
    return jax.shard_map(body, mesh=mesh, in_specs=in_specs, out_specs=out_specs, check_vma=False)
```

```python
import functools
import math

import jax
import jax.numpy as jnp
from jax import lax
from jax.experimental import pallas as pl
from jax.experimental.pallas import tpu as pltpu
from jax.sharding import PartitionSpec as P

BETA_ONE = 0.9
BETA_TWO = 0.95
LEARN_RATE = 0.05
DECAY_RATE = 0.1
ADAM_EPS = 1e-08
CLIP_RMS = 2.0
NORM_EPS = 1e-12

LANES = 128
Y_SIZE = 4
VMEM_LIMIT = 48 * 1024 * 1024
SORT_LIMIT = 63 * 1024 * 1024
SMALL_LIMIT = 8 * 1024 * 1024
PRE_WEIGHT = 12
SPREAD = 2
INTERPRET = False
BF16 = jnp.bfloat16
F32 = jnp.float32


def contract_last(a, b):
    return lax.dot_general(a, b, (((1,), (1,)), ((), ())), preferred_element_type=F32)


def contract_first(a, b):
    return lax.dot_general(a, b, (((0,), (0,)), ((), ())), preferred_element_type=F32)


def vmem_specs(count):
    return [pl.BlockSpec(memory_space=pltpu.VMEM)] * count


def call(kernel, out_shape, operands, scratch=(), flops=0):
    size = sum(math.prod(a.shape) * a.dtype.itemsize for a in (*operands, out_shape))
    return pl.pallas_call(
        kernel,
        out_shape=out_shape,
        in_specs=[pl.BlockSpec(memory_space=pltpu.SMEM)] + vmem_specs(len(operands) - 1),
        out_specs=pl.BlockSpec(memory_space=pltpu.VMEM),
        scratch_shapes=list(scratch),
        compiler_params=pltpu.CompilerParams(vmem_limit_bytes=VMEM_LIMIT),
        cost_estimate=pl.CostEstimate(flops=flops, bytes_accessed=size, transcendentals=0),
        interpret=INTERPRET,
    )(*operands)


class Layout:
    def __init__(self, pipe, dp, rows, width, rank):
        self.pipe, self.dp, self.rows, self.width, self.rank = pipe, dp, rows, width, rank
        self.y = Y_SIZE if dp >= 64 else 2
        self.z = dp // self.y
        self.group = pipe * self.y
        self.span = width // self.y
        self.share = width // self.group
        self.per = self.z // pipe
        self.half = pipe // self.y
        self.piece = rows // pipe
        self.tiles = pipe * rank // LANES
        self.ranks = pipe * rank
        self.gram = 2 * LANES
        self.slots = {(a, b): (a, b) for a in range(1, self.tiles) for b in range(min(a, 2))}
        spare = [(a, 1) for a in range(1, self.tiles) if (a, 1) not in self.slots]
        rest = [(a, b) for a in range(1, self.tiles) for b in range(2, a)]
        self.slots.update(zip(rest, spare))
        y, z = self.y, self.z
        self.along_z = [[a * z + b for b in range(z)] for a in range(y)]
        self.along_y = [[a * z + b for a in range(y)] for b in range(z)]
        self.plane = [
            [p * dp + a * z + b for p in range(pipe) for a in range(y)] for b in range(z)
        ]

    def device(self, p, y, z):
        return p * self.dp + y * self.z + z

    def everywhere(self):
        return [(p, a, b) for p in range(self.pipe) for a in range(self.y) for b in range(self.z)]

    def cotangent_turn(self):
        return [
            (
                self.device(p, a, b),
                self.device(self.y * (p % self.half) + a, p // self.half, b),
            )
            for p, a, b in self.everywhere()
        ]

    def gradient_home(self):
        return [
            (
                self.device(p, a, b),
                self.device(b // self.per, a, p * self.per + b % self.per),
            )
            for p, a, b in self.everywhere()
        ]


def sort_kernel(lay, valid, x_ref, c_ref, out_ref, held, cots, sems):
    loads, stores = [], []
    fetch = pltpu.make_async_copy(c_ref, cots, sems.at[3 * lay.y])
    fetch.start()
    for a in range(lay.y):
        cols = pl.ds(a * lay.span, lay.span)
        loads.append(pltpu.make_async_copy(x_ref.at[:, cols], held.at[a], sems.at[a]))
        stores.append(
            pltpu.make_async_copy(
                held.at[a], out_ref.at[a, :, pl.ds(0, lay.span)], sems.at[lay.y + a]
            )
        )
        loads[a].start()
    fetch.wait()
    cot = cots[...]
    live = lax.broadcasted_iota(jnp.int32, cot.shape, 0) < valid[0]
    cots[...] = jnp.where(live, cot, jnp.zeros_like(cot))
    for a in range(lay.y):
        stores.append(
            pltpu.make_async_copy(
                cots.at[:, pl.ds(a * lay.share, lay.share)],
                out_ref.at[a, :, pl.ds(lay.span, lay.share)],
                sems.at[2 * lay.y + a],
            )
        )
        stores[lay.y + a].start()
    for a in range(lay.y):
        loads[a].wait()
        stores[a].start()
    for store in stores:
        store.wait()


def sort_columns(lay, valid_rows, inputs, cotangent):
    both = lay.span + lay.share
    return pl.pallas_call(
        functools.partial(sort_kernel, lay),
        out_shape=jax.ShapeDtypeStruct((lay.y, lay.rows, both), BF16),
        in_specs=[
            pl.BlockSpec(memory_space=pltpu.SMEM),
            pl.BlockSpec(memory_space=pltpu.HBM),
            pl.BlockSpec(memory_space=pltpu.HBM),
        ],
        out_specs=pl.BlockSpec(memory_space=pltpu.HBM),
        scratch_shapes=[
            pltpu.VMEM((lay.y, lay.rows, lay.span), BF16),
            pltpu.VMEM(cotangent.shape, BF16),
            pltpu.SemaphoreType.DMA((3 * lay.y + 1,)),
        ],
        compiler_params=pltpu.CompilerParams(vmem_limit_bytes=SORT_LIMIT),
        cost_estimate=pl.CostEstimate(
            flops=0, bytes_accessed=4 * lay.y * lay.rows * both, transcendentals=0
        ),
        interpret=INTERPRET,
    )(valid_rows, inputs, cotangent)


def pre_kernel(lay, index, w_ref, x_ref, out_ref):
    lower = index[0] % 2
    maps = jnp.concatenate(
        [jnp.concatenate([w_ref[b, lower], w_ref[b, 1 - lower]], axis=0) for b in range(lay.z)],
        axis=1,
    )
    for a in range(lay.y):
        out_ref[a] = contract_last(x_ref[a, :, 0 : lay.span], maps).astype(BF16)


def section_maps(lay, w_ref, which):
    return jnp.concatenate(
        [
            jnp.concatenate([w_ref[s, j, which] for j in range(lay.per)], axis=1)
            for s in range(lay.pipe)
        ],
        axis=0,
    )


def gram_tile(down, up, row, col):
    rows, cols = slice(row * LANES, (row + 1) * LANES), slice(col * LANES, (col + 1) * LANES)
    return contract_last(down[rows], up[cols]).astype(BF16)


def diagonal_tile(lay, down, up):
    rank = lay.rank
    lower = lax.broadcasted_iota(jnp.int32, (rank, LANES), 1) < rank
    blocks = []
    for t in range(lay.tiles):
        odd = down[t * LANES + rank : (t + 1) * LANES]
        block = contract_last(odd, up[t * LANES : (t + 1) * LANES])
        blocks.append(block if t % 2 == 0 else pltpu.roll(block, rank, 1))
    halves = [jnp.where(lower, blocks[t], blocks[t + 1]) for t in range(0, lay.tiles, 2)]
    if len(halves) == 1:
        halves.append(halves[0])
    return jnp.concatenate(halves[::-1], axis=0).astype(BF16)


def pack_kernel(lay, index, w_ref, pre_ref, c_ref, out_ref):
    down, up = section_maps(lay, w_ref, 0), section_maps(lay, w_ref, 1)
    gram_at, pre_at = lay.ranks, lay.ranks + lay.gram
    for a in range(lay.y):
        part = contract_last(c_ref[a], up).astype(BF16)
        for p in range(lay.pipe):
            rows = slice(p * lay.piece, (p + 1) * lay.piece)
            out_ref[p * lay.y + a, :, 0:gram_at] = part[rows]
            out_ref[p * lay.y + a, :, pre_at:] = pre_ref[a, rows, :]
    grams = {spot: gram_tile(down, up, *tile) for tile, spot in lay.slots.items()}
    grams[0, 0] = diagonal_tile(lay, down, up)
    each = lay.ranks // lay.group
    count = LANES // each
    for t in range(lay.tiles):
        for side in range(2):
            cols = slice(gram_at + side * LANES, gram_at + (side + 1) * LANES)
            tile = grams.get((t, side), jnp.zeros((LANES, LANES), BF16))
            for q in range(count):
                out_ref[t * count + q, :, cols] = tile[q * each : (q + 1) * each]


def sum_kernel(lay, index, r_ref, out_ref):
    gram_end = lay.ranks + lay.gram
    total = r_ref[0, :, 0:gram_end].astype(F32)
    for q in range(1, lay.group):
        total += r_ref[q, :, 0:gram_end].astype(F32)
    lower = lax.broadcasted_iota(jnp.int32, (lay.piece, LANES), 1) < lay.rank
    pres = []
    for s in range(lay.pipe):
        one = r_ref[s * lay.y, :, gram_end:].astype(F32)
        for a in range(1, lay.y):
            one += r_ref[s * lay.y + a, :, gram_end:].astype(F32)
        pres.append(one)
    cols = [total] + [jnp.where(lower, pres[2 * t], pres[2 * t + 1]) for t in range(lay.tiles)]
    message = jnp.concatenate(cols, axis=1).astype(BF16)
    for q in range(lay.group):
        out_ref[q] = message


def chain_kernel(lay, index, q_ref, w_ref, c_ref, x_ref, out_ref, *scratch):
    along, slope, acts, backs, gram, held = scratch
    width_scale, rank_scale = 1.0 / math.sqrt(lay.width), 1.0 / math.sqrt(lay.rank)
    gram_at, pre_at = lay.ranks, lay.ranks + lay.gram
    each = lay.ranks // lay.group
    for q in range(lay.group):
        p, a = q // lay.y, q % lay.y
        rows = slice(a * lay.rows + p * lay.piece, a * lay.rows + (p + 1) * lay.piece)
        along[rows, :] = q_ref[q, :, 0:gram_at].astype(F32)
        gram[q * each : (q + 1) * each, :] = q_ref[q, :, gram_at:pre_at]
        pre = q_ref[q, :, pre_at:].astype(F32) * width_scale
        gate = 1.0 / (1.0 + jnp.exp(-pre))
        acts[rows, :] = (pre * gate).astype(BF16)
        slope[rows, :] = gate * (1.0 + pre * (1.0 - gate)) * rank_scale
    tokens = lay.y * lay.rows
    lower = lax.broadcasted_iota(jnp.int32, (tokens, LANES), 1) < lay.rank
    for s in range(lay.pipe - 1, -1, -1):
        t, odd = s // 2, s % 2 == 1
        tile = slice(t * LANES, (t + 1) * LANES)
        back = along[:, tile] * slope[:, tile]
        back = jnp.where(lower != odd, back, 0.0).astype(BF16)
        if odd:
            backs[t] = back
        else:
            backs[t] = backs[t] + back
        if s == 0:
            continue
        wide = min(t, 2)
        if wide:
            cols = slice(0, wide * LANES)
            along[:, cols] += width_scale * jnp.dot(
                back, gram[tile, cols], preferred_element_type=F32
            )
        for c in range(2, t):
            cols = slice(c * LANES, (c + 1) * LANES)
            row, side = lay.slots[t, c]
            along[:, cols] += width_scale * jnp.dot(
                back,
                gram[row * LANES : (row + 1) * LANES, side * LANES : (side + 1) * LANES],
                preferred_element_type=F32,
            )
        if odd:
            pair = gram[0:LANES, 0:LANES].astype(F32)
            if t % 2 == 1:
                pair = pltpu.roll(pair, lay.rank, 1)
            if t >= 2:
                pair = jnp.concatenate([pair[lay.rank :], pair[: lay.rank]], axis=0)
            along[:, tile] += width_scale * jnp.dot(
                back, pair.astype(BF16), preferred_element_type=F32
            )
    acted = acts[...]
    back_all = jnp.concatenate([backs[t] for t in range(lay.tiles)], axis=1)
    cross = contract_first(acted, back_all)
    before = lax.broadcasted_iota(jnp.int32, cross.shape, 0) // lay.rank
    after = lax.broadcasted_iota(jnp.int32, cross.shape, 1) // lay.rank
    cross = jnp.where(before < after, cross * width_scale, 0.0).astype(BF16)
    cot_all = c_ref[...].reshape(tokens, lay.share)
    grad_up = contract_first(acted, cot_all) + jnp.dot(
        cross, section_maps(lay, w_ref, 0), preferred_element_type=F32
    )
    grad_up = (grad_up * rank_scale).astype(BF16)
    for s in range(lay.pipe):
        for j in range(lay.per):
            out_ref[s * lay.per + j, lay.rank :, :] = grad_up[
                s * lay.rank : (s + 1) * lay.rank, j * LANES : (j + 1) * LANES
            ]
    mine, odd = index[0] // 2, index[0] % 2
    total = None
    for a in range(lay.y):
        rows = slice(a * lay.rows, (a + 1) * lay.rows)
        part = contract_first(backs[mine, rows, :], x_ref[a, :, 0 : lay.span])
        total = part if total is None else total + part
    held[...] = (total * width_scale).reshape(2, lay.rank, lay.span)
    grad_down = held[odd].astype(BF16)
    for b in range(lay.z):
        out_ref[b, 0 : lay.rank, :] = grad_down[:, b * LANES : (b + 1) * LANES]


def update_kernel(norm_limit, squares, grads, grad_up, master, moment1, moment2, *outs):
    new_master, new_moment1, new_moment2, new_weights = outs
    square_sum = jnp.sum(jnp.sum(squares[:, 0:1, :], axis=0), keepdims=True)
    clip_factor = jnp.minimum(1.0, norm_limit / jnp.sqrt(square_sum + NORM_EPS))
    rank = grad_up.shape[0]
    for side, grad in enumerate((grads[0:rank, :], grad_up[...])):
        scaled = grad * clip_factor
        first = BETA_ONE * moment1[0, side] + (1.0 - BETA_ONE) * scaled
        second = BETA_TWO * moment2[0, side] + (1.0 - BETA_TWO) * scaled * scaled
        old = master[0, side]
        new = old - LEARN_RATE * (first / (jnp.sqrt(second) + ADAM_EPS) + DECAY_RATE * old)
        new_moment1[0, side] = first
        new_moment2[0, side] = second
        new_master[0, side] = new
        new_weights[0, side] = new.astype(BF16)


def body(saved_inputs, cotangent, weights_bf16, master, moment1, moment2, valid_rows):
    pipe, dp = lax.axis_size("pipe"), lax.axis_size("dp")
    inputs, weights = saved_inputs[0], weights_bf16[0]
    lay = Layout(pipe, dp, inputs.shape[0], inputs.shape[1], weights.shape[1])
    both = ("pipe", "dp")
    index = lax.axis_index("pipe").astype(jnp.int32).reshape(1)

    by_column = sort_columns(lay, valid_rows, inputs, cotangent)
    by_column = lax.all_to_all(by_column, "dp", 0, 0, axis_index_groups=lay.along_y)
    maps = lax.all_gather(weights, "dp", axis_index_groups=lay.along_z)
    cots, maps = lax.optimization_barrier((by_column[:, :, lay.span :], maps))
    cots = lax.ppermute(cots, both, lay.cotangent_turn())
    shared = lax.all_to_all(maps.reshape(pipe, lay.per, 2, lay.rank, LANES), "pipe", 0, 0)
    by_column, cots = lax.optimization_barrier((by_column, cots))
    pre_part = call(
        functools.partial(pre_kernel, lay),
        jax.ShapeDtypeStruct((lay.y, lay.rows, LANES), BF16),
        (index, maps, by_column),
        flops=PRE_WEIGHT * 2 * lay.y * lay.rows * lay.span * LANES,
    )
    message = lay.ranks + lay.gram + LANES
    parts = call(
        functools.partial(pack_kernel, lay),
        jax.ShapeDtypeStruct((lay.group, lay.piece, message), BF16),
        (index, shared, pre_part, cots),
        flops=4 * lay.y * lay.rows * lay.share * lay.ranks,
    )
    parts = lax.all_to_all(parts, both, 0, 0, axis_index_groups=lay.plane)
    reply = 2 * lay.ranks + lay.gram
    sums = call(
        functools.partial(sum_kernel, lay),
        jax.ShapeDtypeStruct((lay.group, lay.piece, reply), BF16),
        (index, parts),
    )
    sums = lax.all_to_all(sums, both, 0, 0, axis_index_groups=lay.plane)
    tokens = lay.y * lay.rows
    grads = call(
        functools.partial(chain_kernel, lay),
        jax.ShapeDtypeStruct((lay.z, 2 * lay.rank, LANES), BF16),
        (index, sums, shared, cots, by_column),
        scratch=(
            pltpu.VMEM((tokens, lay.ranks), F32),
            pltpu.VMEM((tokens, lay.ranks), F32),
            pltpu.VMEM((tokens, lay.ranks), BF16),
            pltpu.VMEM((lay.tiles, tokens, LANES), BF16),
            pltpu.VMEM((lay.ranks, lay.gram), BF16),
            pltpu.VMEM((2, lay.rank, lay.span), F32),
        ),
        flops=8 * tokens * lay.ranks * lay.share,
    )
    grads = lax.all_to_all(grads, "dp", 0, 0, axis_index_groups=lay.along_z)
    grads = jnp.sum(grads.astype(F32), axis=0)
    squares = jnp.sum(grads * grads, axis=0, keepdims=True)
    squares = jnp.broadcast_to(squares, (lay.group, 1, LANES))
    squares = lax.all_to_all(squares, both, 0, 0, axis_index_groups=lay.plane)
    grad_up = lax.ppermute(grads[lay.rank :], both, lay.gradient_home())
    squares = jnp.broadcast_to(jnp.sum(squares, axis=0), (lay.z, SPREAD, LANES))
    squares = lax.all_to_all(squares, "dp", 0, 0, axis_index_groups=lay.along_z)
    norm_limit = CLIP_RMS * math.sqrt(2.0 * pipe * lay.rank * lay.width)
    state = jax.ShapeDtypeStruct(master.shape, F32)
    return pl.pallas_call(
        functools.partial(update_kernel, norm_limit),
        out_shape=(state, state, state, jax.ShapeDtypeStruct(master.shape, BF16)),
        in_specs=vmem_specs(6),
        out_specs=tuple(vmem_specs(4)),
        compiler_params=pltpu.CompilerParams(vmem_limit_bytes=SMALL_LIMIT),
        cost_estimate=pl.CostEstimate(
            flops=0, bytes_accessed=30 * math.prod(master.shape), transcendentals=0
        ),
        interpret=INTERPRET,
    )(squares, grads, grad_up, master, moment1, moment2)


def solution(mesh):
    in_specs = (
        P("pipe", "dp", None),
        P("dp", "pipe"),
        P("pipe", None, None, "dp"),
        P("pipe", None, None, "dp"),
        P("pipe", None, None, "dp"),
        P("pipe", None, None, "dp"),
        P("dp"),
    )
    out_specs = (
        P("pipe", None, None, "dp"),
        P("pipe", None, None, "dp"),
        P("pipe", None, None, "dp"),
        P("pipe", None, None, "dp"),
    )
    return jax.shard_map(body, mesh=mesh, in_specs=in_specs, out_specs=out_specs, check_vma=False)
```

```python
import functools
import math

import jax
import jax.numpy as jnp
from jax import lax
from jax.experimental import pallas as pl
from jax.experimental.pallas import tpu as pltpu
from jax.sharding import PartitionSpec as P

BETA_ONE = 0.9
BETA_TWO = 0.95
LEARN_RATE = 0.05
DECAY_RATE = 0.1
ADAM_EPS = 1e-08
CLIP_RMS = 2.0
NORM_EPS = 1e-12

LANES = 128
Y_SIZE = 4
VMEM_LIMIT = 48 * 1024 * 1024
SORT_LIMIT = 63 * 1024 * 1024
SMALL_LIMIT = 8 * 1024 * 1024
PRE_WEIGHT = 12
SPREAD = 1
INTERPRET = False
BF16 = jnp.bfloat16
F32 = jnp.float32


def contract_last(a, b):
    return lax.dot_general(a, b, (((1,), (1,)), ((), ())), preferred_element_type=F32)


def contract_first(a, b):
    return lax.dot_general(a, b, (((0,), (0,)), ((), ())), preferred_element_type=F32)


def vmem_specs(count):
    return [pl.BlockSpec(memory_space=pltpu.VMEM)] * count


def call(kernel, out_shape, operands, scratch=(), flops=0):
    size = sum(math.prod(a.shape) * a.dtype.itemsize for a in (*operands, out_shape))
    return pl.pallas_call(
        kernel,
        out_shape=out_shape,
        in_specs=[pl.BlockSpec(memory_space=pltpu.SMEM)] + vmem_specs(len(operands) - 1),
        out_specs=pl.BlockSpec(memory_space=pltpu.VMEM),
        scratch_shapes=list(scratch),
        compiler_params=pltpu.CompilerParams(vmem_limit_bytes=VMEM_LIMIT),
        cost_estimate=pl.CostEstimate(flops=flops, bytes_accessed=size, transcendentals=0),
        interpret=INTERPRET,
    )(*operands)


class Layout:
    def __init__(self, pipe, dp, rows, width, rank):
        self.pipe, self.dp, self.rows, self.width, self.rank = pipe, dp, rows, width, rank
        self.y = Y_SIZE if dp >= 64 else 2
        self.z = dp // self.y
        self.group = pipe * self.y
        self.span = width // self.y
        self.share = width // self.group
        self.per = self.z // pipe
        self.half = pipe // self.y
        self.piece = rows // pipe
        self.tiles = pipe * rank // LANES
        self.ranks = pipe * rank
        self.gram = 2 * LANES
        self.slots = {(a, b): (a, b) for a in range(1, self.tiles) for b in range(min(a, 2))}
        spare = [(a, 1) for a in range(1, self.tiles) if (a, 1) not in self.slots]
        rest = [(a, b) for a in range(1, self.tiles) for b in range(2, a)]
        self.slots.update(zip(rest, spare))
        y, z = self.y, self.z
        self.along_z = [[a * z + b for b in range(z)] for a in range(y)]
        self.along_y = [[a * z + b for a in range(y)] for b in range(z)]
        self.plane = [
            [p * dp + a * z + b for p in range(pipe) for a in range(y)] for b in range(z)
        ]

    def device(self, p, y, z):
        return p * self.dp + y * self.z + z

    def everywhere(self):
        return [(p, a, b) for p in range(self.pipe) for a in range(self.y) for b in range(self.z)]

    def cotangent_turn(self):
        return [
            (
                self.device(p, a, b),
                self.device(self.y * (p % self.half) + a, p // self.half, b),
            )
            for p, a, b in self.everywhere()
        ]

    def gradient_home(self):
        return [
            (
                self.device(p, a, b),
                self.device(b // self.per, a, p * self.per + b % self.per),
            )
            for p, a, b in self.everywhere()
        ]


def sort_kernel(lay, valid, x_ref, c_ref, out_ref, held, cots, sems):
    loads, stores = [], []
    fetch = pltpu.make_async_copy(c_ref, cots, sems.at[3 * lay.y])
    fetch.start()
    for a in range(lay.y):
        cols = pl.ds(a * lay.span, lay.span)
        loads.append(pltpu.make_async_copy(x_ref.at[:, cols], held.at[a], sems.at[a]))
        stores.append(
            pltpu.make_async_copy(
                held.at[a], out_ref.at[a, :, pl.ds(0, lay.span)], sems.at[lay.y + a]
            )
        )
        loads[a].start()
    fetch.wait()
    cot = cots[...]
    live = lax.broadcasted_iota(jnp.int32, cot.shape, 0) < valid[0]
    cots[...] = jnp.where(live, cot, jnp.zeros_like(cot))
    for a in range(lay.y):
        stores.append(
            pltpu.make_async_copy(
                cots.at[:, pl.ds(a * lay.share, lay.share)],
                out_ref.at[a, :, pl.ds(lay.span, lay.share)],
                sems.at[2 * lay.y + a],
            )
        )
        stores[lay.y + a].start()
    for a in range(lay.y):
        loads[a].wait()
        stores[a].start()
    for store in stores:
        store.wait()


def sort_columns(lay, valid_rows, inputs, cotangent):
    both = lay.span + lay.share
    return pl.pallas_call(
        functools.partial(sort_kernel, lay),
        out_shape=jax.ShapeDtypeStruct((lay.y, lay.rows, both), BF16),
        in_specs=[
            pl.BlockSpec(memory_space=pltpu.SMEM),
            pl.BlockSpec(memory_space=pltpu.HBM),
            pl.BlockSpec(memory_space=pltpu.HBM),
        ],
        out_specs=pl.BlockSpec(memory_space=pltpu.HBM),
        scratch_shapes=[
            pltpu.VMEM((lay.y, lay.rows, lay.span), BF16),
            pltpu.VMEM(cotangent.shape, BF16),
            pltpu.SemaphoreType.DMA((3 * lay.y + 1,)),
        ],
        compiler_params=pltpu.CompilerParams(vmem_limit_bytes=SORT_LIMIT),
        cost_estimate=pl.CostEstimate(
            flops=0, bytes_accessed=4 * lay.y * lay.rows * both, transcendentals=0
        ),
        interpret=INTERPRET,
    )(valid_rows, inputs, cotangent)


def pre_kernel(lay, index, w_ref, x_ref, out_ref):
    lower = index[0] % 2
    maps = jnp.concatenate(
        [jnp.concatenate([w_ref[b, lower], w_ref[b, 1 - lower]], axis=0) for b in range(lay.z)],
        axis=1,
    )
    for a in range(lay.y):
        out_ref[a] = contract_last(x_ref[a, :, 0 : lay.span], maps).astype(BF16)


def section_maps(lay, w_ref, which):
    return jnp.concatenate(
        [
            jnp.concatenate([w_ref[s, j, which] for j in range(lay.per)], axis=1)
            for s in range(lay.pipe)
        ],
        axis=0,
    )


def gram_tile(down, up, row, col):
    rows, cols = slice(row * LANES, (row + 1) * LANES), slice(col * LANES, (col + 1) * LANES)
    return contract_last(down[rows], up[cols]).astype(BF16)


def diagonal_tile(lay, down, up):
    rank = lay.rank
    lower = lax.broadcasted_iota(jnp.int32, (rank, LANES), 1) < rank
    blocks = []
    for t in range(lay.tiles):
        odd = down[t * LANES + rank : (t + 1) * LANES]
        block = contract_last(odd, up[t * LANES : (t + 1) * LANES])
        blocks.append(block if t % 2 == 0 else pltpu.roll(block, rank, 1))
    halves = [jnp.where(lower, blocks[t], blocks[t + 1]) for t in range(0, lay.tiles, 2)]
    if len(halves) == 1:
        halves.append(halves[0])
    return jnp.concatenate(halves[::-1], axis=0).astype(BF16)


def pack_kernel(lay, index, w_ref, pre_ref, c_ref, out_ref):
    down, up = section_maps(lay, w_ref, 0), section_maps(lay, w_ref, 1)
    gram_at, pre_at = lay.ranks, lay.ranks + lay.gram
    for a in range(lay.y):
        part = contract_last(c_ref[a], up).astype(BF16)
        for p in range(lay.pipe):
            rows = slice(p * lay.piece, (p + 1) * lay.piece)
            out_ref[p * lay.y + a, :, 0:gram_at] = part[rows]
            out_ref[p * lay.y + a, :, pre_at:] = pre_ref[a, rows, :]
    grams = {spot: gram_tile(down, up, *tile) for tile, spot in lay.slots.items()}
    grams[0, 0] = diagonal_tile(lay, down, up)
    each = lay.ranks // lay.group
    count = LANES // each
    for t in range(lay.tiles):
        for side in range(2):
            cols = slice(gram_at + side * LANES, gram_at + (side + 1) * LANES)
            tile = grams.get((t, side), jnp.zeros((LANES, LANES), BF16))
            for q in range(count):
                out_ref[t * count + q, :, cols] = tile[q * each : (q + 1) * each]


def sum_kernel(lay, index, r_ref, out_ref):
    gram_end = lay.ranks + lay.gram
    total = r_ref[0, :, 0:gram_end].astype(F32)
    for q in range(1, lay.group):
        total += r_ref[q, :, 0:gram_end].astype(F32)
    lower = lax.broadcasted_iota(jnp.int32, (lay.piece, LANES), 1) < lay.rank
    pres = []
    for s in range(lay.pipe):
        one = r_ref[s * lay.y, :, gram_end:].astype(F32)
        for a in range(1, lay.y):
            one += r_ref[s * lay.y + a, :, gram_end:].astype(F32)
        pres.append(one)
    cols = [total] + [jnp.where(lower, pres[2 * t], pres[2 * t + 1]) for t in range(lay.tiles)]
    message = jnp.concatenate(cols, axis=1).astype(BF16)
    for q in range(lay.group):
        out_ref[q] = message


def chain_kernel(lay, index, q_ref, w_ref, c_ref, x_ref, out_ref, *scratch):
    along, slope, acts, backs, gram, held = scratch
    width_scale, rank_scale = 1.0 / math.sqrt(lay.width), 1.0 / math.sqrt(lay.rank)
    gram_at, pre_at = lay.ranks, lay.ranks + lay.gram
    each = lay.ranks // lay.group
    for q in range(lay.group):
        p, a = q // lay.y, q % lay.y
        rows = slice(a * lay.rows + p * lay.piece, a * lay.rows + (p + 1) * lay.piece)
        along[rows, :] = q_ref[q, :, 0:gram_at].astype(F32)
        gram[q * each : (q + 1) * each, :] = q_ref[q, :, gram_at:pre_at]
        pre = q_ref[q, :, pre_at:].astype(F32) * width_scale
        gate = 1.0 / (1.0 + jnp.exp(-pre))
        acts[rows, :] = (pre * gate).astype(BF16)
        slope[rows, :] = gate * (1.0 + pre * (1.0 - gate)) * rank_scale
    tokens = lay.y * lay.rows
    lower = lax.broadcasted_iota(jnp.int32, (tokens, LANES), 1) < lay.rank
    for s in range(lay.pipe - 1, -1, -1):
        t, odd = s // 2, s % 2 == 1
        tile = slice(t * LANES, (t + 1) * LANES)
        back = along[:, tile] * slope[:, tile]
        back = jnp.where(lower != odd, back, 0.0).astype(BF16)
        if odd:
            backs[t] = back
        else:
            backs[t] = backs[t] + back
        if s == 0:
            continue
        wide = min(t, 2)
        if wide:
            cols = slice(0, wide * LANES)
            along[:, cols] += width_scale * jnp.dot(
                back, gram[tile, cols], preferred_element_type=F32
            )
        for c in range(2, t):
            cols = slice(c * LANES, (c + 1) * LANES)
            row, side = lay.slots[t, c]
            along[:, cols] += width_scale * jnp.dot(
                back,
                gram[row * LANES : (row + 1) * LANES, side * LANES : (side + 1) * LANES],
                preferred_element_type=F32,
            )
        if odd:
            pair = gram[0:LANES, 0:LANES].astype(F32)
            if t % 2 == 1:
                pair = pltpu.roll(pair, lay.rank, 1)
            if t >= 2:
                pair = jnp.concatenate([pair[lay.rank :], pair[: lay.rank]], axis=0)
            along[:, tile] += width_scale * jnp.dot(
                back, pair.astype(BF16), preferred_element_type=F32
            )
    acted = acts[...]
    back_all = jnp.concatenate([backs[t] for t in range(lay.tiles)], axis=1)
    cross = contract_first(acted, back_all)
    before = lax.broadcasted_iota(jnp.int32, cross.shape, 0) // lay.rank
    after = lax.broadcasted_iota(jnp.int32, cross.shape, 1) // lay.rank
    cross = jnp.where(before < after, cross * width_scale, 0.0).astype(BF16)
    cot_all = c_ref[...].reshape(tokens, lay.share)
    grad_up = contract_first(acted, cot_all) + jnp.dot(
        cross, section_maps(lay, w_ref, 0), preferred_element_type=F32
    )
    grad_up = (grad_up * rank_scale).astype(BF16)
    for s in range(lay.pipe):
        for j in range(lay.per):
            out_ref[s * lay.per + j, lay.rank :, :] = grad_up[
                s * lay.rank : (s + 1) * lay.rank, j * LANES : (j + 1) * LANES
            ]
    mine, odd = index[0] // 2, index[0] % 2
    total = None
    for a in range(lay.y):
        rows = slice(a * lay.rows, (a + 1) * lay.rows)
        part = contract_first(backs[mine, rows, :], x_ref[a, :, 0 : lay.span])
        total = part if total is None else total + part
    held[...] = (total * width_scale).reshape(2, lay.rank, lay.span)
    grad_down = held[odd].astype(BF16)
    for b in range(lay.z):
        out_ref[b, 0 : lay.rank, :] = grad_down[:, b * LANES : (b + 1) * LANES]


def update_kernel(norm_limit, squares, grads, grad_up, master, moment1, moment2, *outs):
    new_master, new_moment1, new_moment2, new_weights = outs
    square_sum = jnp.sum(jnp.sum(squares[:, 0:1, :], axis=0), keepdims=True)
    clip_factor = jnp.minimum(1.0, norm_limit / jnp.sqrt(square_sum + NORM_EPS))
    rank = grad_up.shape[0]
    for side, grad in enumerate((grads[0:rank, :], grad_up[...])):
        scaled = grad * clip_factor
        first = BETA_ONE * moment1[0, side] + (1.0 - BETA_ONE) * scaled
        second = BETA_TWO * moment2[0, side] + (1.0 - BETA_TWO) * scaled * scaled
        old = master[0, side]
        new = old - LEARN_RATE * (first / (jnp.sqrt(second) + ADAM_EPS) + DECAY_RATE * old)
        new_moment1[0, side] = first
        new_moment2[0, side] = second
        new_master[0, side] = new
        new_weights[0, side] = new.astype(BF16)


def body(saved_inputs, cotangent, weights_bf16, master, moment1, moment2, valid_rows):
    pipe, dp = lax.axis_size("pipe"), lax.axis_size("dp")
    inputs, weights = saved_inputs[0], weights_bf16[0]
    lay = Layout(pipe, dp, inputs.shape[0], inputs.shape[1], weights.shape[1])
    both = ("pipe", "dp")
    index = lax.axis_index("pipe").astype(jnp.int32).reshape(1)

    by_column = sort_columns(lay, valid_rows, inputs, cotangent)
    by_column = lax.all_to_all(by_column, "dp", 0, 0, axis_index_groups=lay.along_y)
    maps = lax.all_gather(weights, "dp", axis_index_groups=lay.along_z)
    cots, maps = lax.optimization_barrier((by_column[:, :, lay.span :], maps))
    cots = lax.ppermute(cots, both, lay.cotangent_turn())
    shared = lax.all_to_all(maps.reshape(pipe, lay.per, 2, lay.rank, LANES), "pipe", 0, 0)
    by_column, cots = lax.optimization_barrier((by_column, cots))
    pre_part = call(
        functools.partial(pre_kernel, lay),
        jax.ShapeDtypeStruct((lay.y, lay.rows, LANES), BF16),
        (index, maps, by_column),
        flops=PRE_WEIGHT * 2 * lay.y * lay.rows * lay.span * LANES,
    )
    message = lay.ranks + lay.gram + LANES
    parts = call(
        functools.partial(pack_kernel, lay),
        jax.ShapeDtypeStruct((lay.group, lay.piece, message), BF16),
        (index, shared, pre_part, cots),
        flops=4 * lay.y * lay.rows * lay.share * lay.ranks,
    )
    parts = lax.all_to_all(parts, both, 0, 0, axis_index_groups=lay.plane)
    reply = 2 * lay.ranks + lay.gram
    sums = call(
        functools.partial(sum_kernel, lay),
        jax.ShapeDtypeStruct((lay.group, lay.piece, reply), BF16),
        (index, parts),
    )
    sums = lax.all_to_all(sums, both, 0, 0, axis_index_groups=lay.plane)
    tokens = lay.y * lay.rows
    grads = call(
        functools.partial(chain_kernel, lay),
        jax.ShapeDtypeStruct((lay.z, 2 * lay.rank, LANES), BF16),
        (index, sums, shared, cots, by_column),
        scratch=(
            pltpu.VMEM((tokens, lay.ranks), F32),
            pltpu.VMEM((tokens, lay.ranks), F32),
            pltpu.VMEM((tokens, lay.ranks), BF16),
            pltpu.VMEM((lay.tiles, tokens, LANES), BF16),
            pltpu.VMEM((lay.ranks, lay.gram), BF16),
            pltpu.VMEM((2, lay.rank, lay.span), F32),
        ),
        flops=8 * tokens * lay.ranks * lay.share,
    )
    grads = lax.all_to_all(grads, "dp", 0, 0, axis_index_groups=lay.along_z)
    grads = jnp.sum(grads.astype(F32), axis=0)
    squares = jnp.sum(grads * grads, axis=0, keepdims=True)
    squares = jnp.broadcast_to(squares, (lay.group, 1, LANES))
    squares = lax.all_to_all(squares, both, 0, 0, axis_index_groups=lay.plane)
    grad_up = lax.ppermute(grads[lay.rank :], both, lay.gradient_home())
    squares = jnp.broadcast_to(jnp.sum(squares, axis=0), (lay.z, SPREAD, LANES))
    squares = lax.all_to_all(squares, "dp", 0, 0, axis_index_groups=lay.along_z)
    norm_limit = CLIP_RMS * math.sqrt(2.0 * pipe * lay.rank * lay.width)
    state = jax.ShapeDtypeStruct(master.shape, F32)
    return pl.pallas_call(
        functools.partial(update_kernel, norm_limit),
        out_shape=(state, state, state, jax.ShapeDtypeStruct(master.shape, BF16)),
        in_specs=vmem_specs(6),
        out_specs=tuple(vmem_specs(4)),
        compiler_params=pltpu.CompilerParams(vmem_limit_bytes=SMALL_LIMIT),
        cost_estimate=pl.CostEstimate(
            flops=0, bytes_accessed=30 * math.prod(master.shape), transcendentals=0
        ),
        interpret=INTERPRET,
    )(squares, grads, grad_up, master, moment1, moment2)


def solution(mesh):
    in_specs = (
        P("pipe", "dp", None),
        P("dp", "pipe"),
        P("pipe", None, None, "dp"),
        P("pipe", None, None, "dp"),
        P("pipe", None, None, "dp"),
        P("pipe", None, None, "dp"),
        P("dp"),
    )
    out_specs = (
        P("pipe", None, None, "dp"),
        P("pipe", None, None, "dp"),
        P("pipe", None, None, "dp"),
        P("pipe", None, None, "dp"),
    )
    return jax.shard_map(body, mesh=mesh, in_specs=in_specs, out_specs=out_specs, check_vma=False)
```
